512 devices in a mesh: dp: 4 (over y), outer: 32 (over z, core), inner: 4 (over x).
Axes of the slice: x: 4, y: 4, z: 16, core: 2. Of those that a mesh axis runs over, the one named last changes fastest.
Arguments:
- query_rows: bfloat16 [65536, 256], P(('dp', 'outer', 'inner')), parts along dimension 0, may hold values from -8 to 8
- key_rows: bfloat16 [65536, 256], P(('dp', 'outer', 'inner')), parts along dimension 0, may hold values from -8 to 8
- value_rows: bfloat16 [65536, 1024], P(('dp', 'outer', 'inner')), parts along dimension 0, may hold values from -6 to 6
- conv_weight: float32 [3, 1024], replicated, may hold values from -1 to 1
- norm_gain: float32 [1024], replicated, may hold values from 0.1 to 1.9
Outputs:
- layer_out: bfloat16 [65536, 1024], P(('dp', 'outer', 'inner')), parts along dimension 0
The draws below stay inside these ranges and needn't reach their ends.
There are 4 independent parts, one for each index of `dp`. The reference program is written for one: setup_inputs(seed, part) draws one part's arguments, and reference() takes and returns one part's arrays. A program takes and returns all parts, laid end to end along the dimension named above; an argument that names none is the same for every part. Nothing has to cross between parts.
All inputs are finite; a program needn't handle non-finite values.
Results may differ from the reference program's by a relative error of at most 0.013.
Values may be sent and summed in bfloat16 or wider, within the bound.
No kernel may reach another device: no remote copies, remote signals or barrier semaphores. Data moves between devices by JAX's collectives and lax.ppermute only.
A program may use at most 128 MiB of HBM per device.

```python
import math
import jax
import jax.numpy as jnp
from jax import lax

HEADS = 16
FEAT = 16
VDIM = 64
PHI = 273
TAPS = 3
WIN = 64
BLK = 128
TOKENS = 16384


def draw_query_rows(key, part):
    noise_key = jax.random.fold_in(key, 1)
    entries = jnp.clip(jax.random.normal(noise_key, (TOKENS, HEADS * FEAT)), -6.0, 6.0)
    return entries.astype(jnp.bfloat16)


def draw_key_rows(key, part):
    noise_key = jax.random.fold_in(key, 2)
    entries = jnp.clip(jax.random.normal(noise_key, (TOKENS, HEADS * FEAT)), -6.0, 6.0)
    return entries.astype(jnp.bfloat16)


def level_of(rng, extent, cuts, smallest, high):
    gain = 1.0
    for dim, parts in cuts:
        draws = jax.random.uniform(jax.random.fold_in(jax.random.fold_in(rng, 6), dim), (parts,), jnp.float32, smallest / len(cuts), high / len(cuts))
        gain = gain * jnp.repeat(jnp.exp(draws), extent[dim] // parts).reshape((-1,) + (1,) * (len(extent) - 1 - dim))
    return gain


def bell_draw(stream_key, extent, width, bound, pieces=(), held_as=jnp.bfloat16):
    values = jax.random.normal(stream_key, extent, jnp.float32) * width
    if len(pieces) > 0:
        values = level_of(stream_key, extent, pieces, -0.22, 0.18) * values
    return jnp.clip(values, min=-bound, max=bound).astype(held_as)


def setup_inputs(seed: int = 0, part: int = 0) -> dict:
    arg_keys = jax.random.split(jax.random.key(seed), 6)
    part_splits = jax.random.split(jax.random.fold_in(arg_keys[5], part), 6)
    return {
        "query_rows": draw_query_rows(jax.random.fold_in(jax.random.fold_in(arg_keys[5], part), 71), part),
        "key_rows": draw_key_rows(jax.random.fold_in(jax.random.fold_in(arg_keys[5], part), 71), part),
        "value_rows": bell_draw(part_splits[2], (TOKENS, HEADS * VDIM), 1.0, 6.0, ((0, 128),)),
        "conv_weight": jnp.clip(jax.random.uniform(arg_keys[3], (TAPS, HEADS * VDIM), jnp.float32, -1.0, 1.0), -1.0, 1.0),
        "norm_gain": jnp.clip(1.0 + 0.18 * jax.random.normal(arg_keys[4], (HEADS * VDIM,), jnp.float32), 0.1, 1.9),
    }


def features(rows_in):
    entries = rows_in.astype(jnp.float32)
    leading = entries.shape[:-1]
    pair_terms = (entries[..., :, None] * entries[..., None, :]).reshape(leading + (FEAT * FEAT,))
    const_term = jnp.ones(leading + (1,), jnp.float32)
    joined = jnp.concatenate([const_term, entries * (1.0 / FEAT ** 0.25), pair_terms * (1.0 / math.sqrt(2.0 * FEAT))], axis=-1)
    return joined.astype(jnp.bfloat16)

def convolve(padded, conv_weight, out_rows):
    conv_sum = jnp.zeros((out_rows, padded.shape[1]), jnp.float32)
    for tap_index in range(TAPS):
        offset = TAPS - 1 - tap_index
        conv_sum = conv_sum + conv_weight[tap_index][None, :] * padded[offset:offset + out_rows].astype(jnp.float32)
    return conv_sum.astype(jnp.bfloat16)

def reference(query_rows, key_rows, value_rows, conv_weight, norm_gain):
    lag_rows = TAPS - 1
    block_count = TOKENS // BLK
    score_scale = 1.0 / math.sqrt(FEAT)
    gain_heads = norm_gain.reshape(HEADS, VDIM)
    causal = jnp.arange(BLK)[:, None] >= jnp.arange(BLK)[None, :]
    offset_rows = jnp.arange(WIN + BLK)[None, :] - jnp.arange(BLK)[:, None]
    inside = (offset_rows >= 0) & (offset_rows <= WIN)

    def advance(fold_carry, inputs):
        key_state, prev_keys, prev_conv, prev_raw = fold_carry
        query_blk, key_blk, value_blk, block_index = inputs
        conv_blk = convolve(jnp.concatenate([prev_raw, value_blk], 0), conv_weight, BLK)
        query_heads = query_blk.reshape(BLK, HEADS, FEAT).astype(jnp.float32)
        key_heads = key_blk.reshape(BLK, HEADS, FEAT).astype(jnp.float32)
        conv_heads = conv_blk.reshape(BLK, HEADS, VDIM).astype(jnp.float32)
        scores = jnp.einsum('iaf,jaf->aij', query_heads, key_heads) * score_scale
        intra_weights = jnp.where(causal[None], 1.0 + scores + 0.5 * scores * scores, 0.0).astype(jnp.bfloat16)
        own_part = jnp.einsum('aij,jac->iac', intra_weights.astype(jnp.float32), conv_heads)
        phi_query = features(query_blk.reshape(BLK, HEADS, FEAT))
        phi_key = features(key_blk.reshape(BLK, HEADS, FEAT))
        state_rounded = key_state.astype(jnp.bfloat16)
        earlier_part = jnp.einsum('iaf,fac->iac', phi_query.astype(jnp.float32), state_rounded.astype(jnp.float32))
        numerator = own_part + earlier_part
        mean_square = lax.optimization_barrier(jnp.mean(numerator * numerator, axis=-1, keepdims=True))
        linear_out = numerator * lax.rsqrt(mean_square + 1e-06) * gain_heads
        ext_keys = jnp.concatenate([prev_keys, key_blk], 0).reshape(WIN + BLK, HEADS, FEAT).astype(jnp.float32)
        ext_conv = jnp.concatenate([prev_conv, conv_blk], 0).reshape(WIN + BLK, HEADS, VDIM).astype(jnp.float32)
        window_scores = jnp.einsum('iaf,jaf->aij', query_heads, ext_keys) * score_scale
        position = block_index * BLK + jnp.arange(WIN + BLK, dtype=jnp.int32) - WIN
        allowed = inside[None] & (position >= 0)[None, None, :]
        masked = jnp.where(allowed, window_scores, -1e+30)
        row_max = lax.optimization_barrier(jnp.max(masked, axis=-1, keepdims=True))
        exp_scores = jnp.where(allowed, jnp.exp(masked - row_max), 0.0)
        window_probs = (exp_scores / lax.optimization_barrier(jnp.sum(exp_scores, axis=-1, keepdims=True))).astype(jnp.bfloat16)
        window_out = jnp.einsum('aij,jac->iac', window_probs.astype(jnp.float32), ext_conv)
        layer_blk = (linear_out + window_out).astype(jnp.bfloat16).reshape(BLK, HEADS * VDIM)
        key_state = key_state + jnp.einsum('jaf,jac->fac', phi_key.astype(jnp.float32), conv_heads)
        next_carry = (key_state, key_blk[BLK - WIN:], conv_blk[BLK - WIN:], value_blk[BLK - lag_rows:])
        return (next_carry, layer_blk)
    start_carry = (jnp.zeros((PHI, HEADS, VDIM), jnp.float32), jnp.zeros((WIN, HEADS * FEAT), jnp.bfloat16), jnp.zeros((WIN, HEADS * VDIM), jnp.bfloat16), jnp.zeros((lag_rows, HEADS * VDIM), jnp.bfloat16))
    inputs = (query_rows.reshape(block_count, BLK, HEADS * FEAT), key_rows.reshape(block_count, BLK, HEADS * FEAT), value_rows.reshape(block_count, BLK, HEADS * VDIM), jnp.arange(block_count, dtype=jnp.int32))
    final_carry, layer_blocks = lax.scan(advance, start_carry, inputs)
    return layer_blocks.reshape(TOKENS, HEADS * VDIM)
```

```python
import jax
import jax.numpy as jnp
import numpy as np
from jax import lax
from jax.experimental import pallas as pl
from jax.experimental.pallas import tpu as pltpu
from jax.sharding import Mesh, PartitionSpec as P

HEADS = 16
FEAT = 16
VDIM = 64
TAPS = 3
WIN = 64
BLK = 128
NPHI = 160
SPLIT = 128
STATE_ROWS = VDIM + (NPHI - SPLIT)
PART = FEAT + FEAT + VDIM
F32 = jnp.float32
BF16 = jnp.bfloat16


def nt(lhs, rhs):
    return lax.dot_general(lhs, rhs, (((1,), (1,)), ((), ())), preferred_element_type=F32)


def tn(lhs, rhs):
    return lax.dot_general(lhs, rhs, (((0,), (0,)), ((), ())), preferred_element_type=F32)


def nn(lhs, rhs):
    return lax.dot_general(lhs, rhs, (((1,), (0,)), ((), ())), preferred_element_type=F32)


def features(entries, weighted):
    lin, diag, off = (0.25, 1.0 / 32.0, 1.0 / 16.0) if weighted else (1.0, 1.0, 1.0)
    rows = [entries * lin if weighted else entries]
    base = entries * off if weighted else entries
    rows.append(entries * entries * diag if weighted else entries * entries)
    for step in range(1, FEAT // 2):
        rolled = jnp.concatenate([entries[step:], entries[:step]], axis=0)
        rows.append(base * rolled)
    rows.append(base[: FEAT // 2] * entries[FEAT // 2 :])
    tail = lax.broadcasted_iota(jnp.int32, (8, entries.shape[1]), 0)
    rows.append(jnp.where(tail == 0, 1.0, 0.0).astype(F32))
    return jnp.concatenate(rows, axis=0).astype(BF16)


def pack_kernel(q_ref, k_ref, v_ref, halo_ref, w_ref, out_ref):
    value = v_ref[...].astype(F32)
    halo = halo_ref[...].astype(F32)
    row = lax.broadcasted_iota(jnp.int32, value.shape, 0)
    last = halo[1:2, :]
    before = halo[0:1, :]
    one = jnp.where(row == 0, last, pltpu.roll(value, 1, 0))
    two = jnp.where(row == 0, before, jnp.where(row == 1, last, pltpu.roll(value, 2, 0)))
    conv = w_ref[0:1, :] * value + w_ref[1:2, :] * one + w_ref[2:3, :] * two
    out_ref[:, 0:FEAT, :] = q_ref[...].T.reshape(HEADS, FEAT, BLK)
    out_ref[:, FEAT : 2 * FEAT, :] = k_ref[...].T.reshape(HEADS, FEAT, BLK)
    out_ref[:, 2 * FEAT :, :] = conv.astype(BF16).T.reshape(HEADS, VDIM, BLK)


def state_kernel(x_ref, sent_ref, own_ref):
    count = x_ref.shape[0]
    total = jnp.zeros((VDIM, NPHI), F32)
    for blk in range(count):
        phi = features(x_ref[blk, FEAT : 2 * FEAT, :].astype(F32), True)
        total = total + nt(x_ref[blk, 2 * FEAT :, :], phi)
    rest = total[:, SPLIT:].T
    state = jnp.concatenate([total[:, :SPLIT], jnp.concatenate([rest, rest], axis=1)], axis=0)
    own_ref[...] = state
    sent_ref[0:STATE_ROWS, :] = state.astype(BF16)
    sent_ref[STATE_ROWS:, :] = x_ref[count - 1, FEAT:, :]


def local_kernel(first_ref, x_ref, recv_ref, num_ref, win_ref, phi_ref):
    count = x_ref.shape[0]
    key_row = lax.broadcasted_iota(jnp.int32, (BLK, BLK), 0)
    query_lane = lax.broadcasted_iota(jnp.int32, (BLK, BLK), 1)
    causal = key_row <= query_lane
    span = WIN + BLK
    near_row = lax.broadcasted_iota(jnp.int32, (span, BLK), 0)
    near_lane = lax.broadcasted_iota(jnp.int32, (span, BLK), 1)
    inside = (near_row >= near_lane) & (near_row <= near_lane + WIN)
    inside_first = inside & ((near_row >= WIN) | (first_ref[0] == 0))
    before_key = recv_ref[STATE_ROWS : STATE_ROWS + FEAT, :]
    before_val = recv_ref[STATE_ROWS + FEAT :, :]
    state = jnp.zeros((VDIM, NPHI), F32)
    blank = jnp.zeros((BLK - WIN, BLK), BF16)
    for blk in range(count):
        query = x_ref[blk, 0:FEAT, :]
        key = x_ref[blk, FEAT : 2 * FEAT, :]
        value = x_ref[blk, 2 * FEAT :, :]
        phi_query = features(query.astype(F32), False)
        phi_ref[:, blk * BLK : (blk + 1) * BLK] = phi_query
        scores = tn(jnp.concatenate([before_key, key], axis=1), query) * 0.25
        own = scores[BLK:]
        weights = jnp.where(causal, 1.0 + own + 0.5 * own * own, 0.0).astype(BF16)
        num = nn(value, weights)
        if blk > 0:
            num = num + nn(state.astype(BF16), phi_query)
        num_ref[blk] = num
        masked = jnp.where(inside_first if blk == 0 else inside, scores[BLK - WIN :], -1e30)
        row_max = jnp.max(masked, axis=0, keepdims=True)
        exp_scores = jnp.exp(masked - row_max)
        row_sum = jnp.sum(exp_scores, axis=0, keepdims=True)
        probs = jnp.concatenate([blank, exp_scores.astype(BF16)], axis=0)
        win = nn(jnp.concatenate([before_val, value], axis=1), probs)
        win_ref[blk] = win / row_sum
        if blk + 1 < count:
            state = state + nt(value, features(key.astype(F32), True))
        before_key, before_val = key, value


def final_kernel(quad_ref, recv_ref, others_ref, num_ref, win_ref, phi_ref, gain_ref, out_ref):
    carried = recv_ref[0:STATE_ROWS, :].astype(F32)
    for quad in range(others_ref.shape[0]):
        reached = quad < quad_ref[0]
        carried = carried + jnp.where(reached, others_ref[quad].astype(F32), 0.0)
    state = jnp.concatenate([carried[:VDIM], carried[VDIM:, :VDIM].T], axis=1).astype(BF16)
    gain = gain_ref[...]
    for blk in range(num_ref.shape[0]):
        num = num_ref[blk] + nn(state, phi_ref[:, blk * BLK : (blk + 1) * BLK])
        mean_square = jnp.sum(num * num, axis=0, keepdims=True) * (1.0 / VDIM)
        linear = num * lax.rsqrt(mean_square + 1e-06) * gain
        out_ref[blk] = (linear + win_ref[blk]).astype(BF16)


def unpack_kernel(x_ref, out_ref):
    out_ref[...] = x_ref[...].reshape(HEADS * VDIM, BLK).T


SMEM = pl.BlockSpec(memory_space=pltpu.SMEM)
VMEM = pl.BlockSpec(memory_space=pltpu.VMEM)


def call(kernel, shapes, scalars, arrays):
    outs = tuple(jax.ShapeDtypeStruct(shape, dtype) for shape, dtype in shapes)
    single = len(outs) == 1
    return pl.pallas_call(
        kernel,
        out_shape=outs[0] if single else outs,
        in_specs=[SMEM] * len(scalars) + [VMEM] * len(arrays),
        out_specs=VMEM if single else tuple(VMEM for _ in outs),
    )(*scalars, *arrays)


def on_device(query_rows, key_rows, value_rows, conv_weight, norm_gain):
    seq = ("quad", "half", "pair", "core", "inner")
    group = ("pair", "core", "inner")
    members = lax.axis_size(group)
    blocks = lax.axis_size(seq)
    halo = lax.ppermute(value_rows[BLK - (TAPS - 1) :], seq, [(i, i + 1) for i in range(blocks - 1)])
    packed = call(
        pack_kernel,
        [((HEADS, PART, BLK), BF16)],
        [],
        [query_rows, key_rows, value_rows, halo, conv_weight],
    )
    mine = lax.all_to_all(packed, group, 0, 0)
    sent, own_state = call(
        state_kernel,
        [((STATE_ROWS + FEAT + VDIM, BLK), BF16), ((STATE_ROWS, BLK), F32)],
        [],
        [mine],
    )
    groups = lax.axis_size(("quad", "half"))
    recv = lax.ppermute(sent, ("quad", "half"), [(i, i + 1) for i in range(groups - 1)])
    two = (own_state + recv[:STATE_ROWS].astype(F32)).astype(BF16)
    quads = lax.axis_size("quad")
    others = lax.all_to_all(jnp.broadcast_to(two[None], (quads, STATE_ROWS, BLK)), "quad", 0, 0)
    first = (lax.axis_index(("quad", "half")) == 0).astype(jnp.int32).reshape(1)
    tokens = members * BLK
    num, win, phi = call(
        local_kernel,
        [((members, VDIM, BLK), F32), ((members, VDIM, BLK), F32), ((NPHI, tokens), BF16)],
        [first],
        [mine, recv],
    )
    head = lax.axis_index(group)
    gain = lax.dynamic_slice(norm_gain, (head * VDIM,), (VDIM,))
    gain = jnp.broadcast_to(gain[:, None], (VDIM, BLK))
    done = call(
        final_kernel,
        [((members, VDIM, BLK), BF16)],
        [lax.axis_index("quad").astype(jnp.int32).reshape(1)],
        [recv, others, num, win, phi, gain],
    )
    heads = lax.all_to_all(done, group, 0, 0)
    return call(unpack_kernel, [((BLK, HEADS * VDIM), BF16)], [], [heads])


def solution(mesh):
    outer, inner = mesh.shape["outer"], mesh.shape["inner"]
    pair = 16 // inner // 2
    shape = (mesh.shape["dp"], outer // (2 * 2 * pair), 2, pair, 2, inner)
    split = Mesh(
        np.asarray(mesh.devices).reshape(shape), ("dp", "quad", "half", "pair", "core", "inner")
    )
    rows = P(("dp", "quad", "half", "pair", "core", "inner"), None)
    return jax.shard_map(
        on_device,
        mesh=split,
        in_specs=(rows, rows, rows, P(), P()),
        out_specs=rows,
        check_vma=False,
    )
```

```python
import jax
import jax.numpy as jnp
import numpy as np
from jax import lax
from jax.experimental import pallas as pl
from jax.experimental.pallas import tpu as pltpu
from jax.sharding import Mesh, PartitionSpec as P

HEADS = 16
FEAT = 16
VDIM = 64
TAPS = 3
WIN = 64
BLK = 128
NPHI = 160
LANES = 128
EDGE = NPHI - LANES
HALF = VDIM // 2
STATE_ROWS = VDIM + HALF
PART = FEAT + FEAT + VDIM
F32 = jnp.float32
BF16 = jnp.bfloat16


def nt(lhs, rhs):
    return lax.dot_general(lhs, rhs, (((1,), (1,)), ((), ())), preferred_element_type=F32)


def tn(lhs, rhs):
    return lax.dot_general(lhs, rhs, (((0,), (0,)), ((), ())), preferred_element_type=F32)


def nn(lhs, rhs):
    return lax.dot_general(lhs, rhs, (((1,), (0,)), ((), ())), preferred_element_type=F32)


def lanes(rows):
    return lax.broadcasted_iota(jnp.int32, (rows, LANES), 1)


def features(entries, weighted):
    lin, diag, off = (0.25, 1.0 / 32.0, 1.0 / 16.0) if weighted else (1.0, 1.0, 1.0)
    rows = [entries * lin if weighted else entries]
    base = entries * off if weighted else entries
    rows.append(entries * entries * diag if weighted else entries * entries)
    for step in range(1, FEAT // 2):
        rolled = jnp.concatenate([entries[step:], entries[:step]], axis=0)
        rows.append(base * rolled)
    rows.append(base[: FEAT // 2] * entries[FEAT // 2 :])
    tail = lax.broadcasted_iota(jnp.int32, (8, entries.shape[1]), 0)
    rows.append(jnp.where(tail == 0, 1.0, 0.0).astype(F32))
    return jnp.concatenate(rows, axis=0).astype(BF16)


def convolve(taps, raw, before):
    lane = lanes(VDIM)
    one = jnp.where(lane < 1, pltpu.roll(before, 1, 1), pltpu.roll(raw, 1, 1))
    two = jnp.where(lane < 2, pltpu.roll(before, 2, 1), pltpu.roll(raw, 2, 1))
    return (taps[0] * raw + taps[1] * one + taps[2] * two).astype(BF16)


def fold(main, rest):
    both = rest[:HALF] + pltpu.roll(rest[HALF:], LANES // 2, 1)
    return jnp.concatenate([main, both], axis=0).astype(BF16)


def unfold(packed):
    wide = packed.astype(F32)
    both = wide[VDIM:STATE_ROWS]
    low = lanes(HALF) < LANES // 2
    upper = jnp.where(low, both, 0.0)
    lower = jnp.where(low, pltpu.roll(both, LANES // 2, 1), 0.0)
    return wide[:VDIM], jnp.concatenate([upper, lower], axis=0)


def edge_state(taps, key_rest, tail_rest):
    lane = lanes(VDIM)
    same = pltpu.roll(tail_rest, LANES - EDGE, 1)
    last = pltpu.roll(tail_rest, LANES - EDGE - 1, 1)
    first = jnp.where(lane == 0, taps[1] * last + taps[2] * same, 0.0)
    missing = jnp.where(lane == 1, taps[2] * same, first).astype(BF16)
    keys = pltpu.roll(key_rest[:FEAT], LANES - EDGE - 2, 1)
    keys = jnp.where(lanes(FEAT) < 2, keys, 0.0)
    state = nt(missing, features(keys, True))
    blank = jnp.zeros((VDIM, LANES - EDGE), F32)
    return state[:, :LANES], jnp.concatenate([state[:, LANES:], blank], axis=1)


def joined(rest, tail_rest, key_rest):
    lane = lanes(VDIM)
    return jnp.where(lane < EDGE, rest, jnp.where(lane < EDGE + 2, tail_rest, key_rest))


def pack_kernel(head_ref, q_ref, k_ref, v_ref, w_ref, gain_ref, out_ref, taps_ref):
    out_ref[:, 0:FEAT, :] = q_ref[...].T.reshape(HEADS, FEAT, BLK)
    out_ref[:, FEAT : 2 * FEAT, :] = k_ref[...].T.reshape(HEADS, FEAT, BLK)
    out_ref[:, 2 * FEAT :, :] = v_ref[...].T.reshape(HEADS, VDIM, BLK)
    rows = jnp.concatenate([w_ref[...], gain_ref[...], jnp.zeros((4, HEADS * VDIM), F32)], axis=0)
    mine = jnp.zeros((8, VDIM), F32)
    for head in range(HEADS):
        mine = jnp.where(head_ref[0] == head, rows[:, head * VDIM : (head + 1) * VDIM], mine)
    columns = mine.T
    for index in range(TAPS + 1):
        taps_ref[index] = jnp.broadcast_to(columns[:, index : index + 1], (VDIM, LANES))


def state_kernel(x_ref, taps_ref, sent_ref, own_ref, conv_ref):
    count = x_ref.shape[0]
    taps = [taps_ref[index] for index in range(TAPS)]
    total = jnp.zeros((VDIM, NPHI), F32)
    before = jnp.zeros((VDIM, BLK), F32)
    for blk in range(count):
        raw = x_ref[blk, 2 * FEAT :, :].astype(F32)
        conv = convolve(taps, raw, before)
        conv_ref[blk] = conv
        phi = features(x_ref[blk, FEAT : 2 * FEAT, :].astype(F32), True)
        total = total + nt(conv, phi)
        before = raw
    lane = lanes(VDIM)
    blank = jnp.zeros((VDIM, LANES - EDGE), F32)
    rest = jnp.concatenate([total[:, LANES:], blank], axis=1)
    tail = pltpu.roll(before, EDGE + 2, 1)
    first = x_ref[0, FEAT : 2 * FEAT, :].astype(F32)
    first = jnp.concatenate([first, jnp.zeros((VDIM - FEAT, BLK), F32)], axis=0)
    first = jnp.where(lane < EDGE + 4, pltpu.roll(first, EDGE + 2, 1), 0.0)
    rest = joined(rest, tail, first)
    main = total[:, :LANES]
    own_ref[0] = main
    own_ref[1] = rest
    sent_ref[0:STATE_ROWS, :] = fold(main, rest)
    sent_ref[STATE_ROWS:, :] = x_ref[count - 1, FEAT:, :]


def merge_one_kernel(own_ref, recv_ref, taps_ref, sent_ref, pair_ref):
    main, rest = own_ref[0], own_ref[1]
    recv_main, recv_rest = unfold(recv_ref[0:STATE_ROWS, :])
    edge_main, edge_rest = edge_state(taps_ref, rest, recv_rest)
    main = main + recv_main + edge_main
    rest = joined(rest + recv_rest + edge_rest, rest, recv_rest)
    pair_ref[0] = main
    pair_ref[1] = rest
    sent_ref[...] = fold(main, rest)


def merge_two_kernel(pair_ref, near_ref, recv_ref, taps_ref, sent_ref, carried_ref):
    main, rest = pair_ref[0], pair_ref[1]
    recv_main, recv_rest = unfold(recv_ref[...])
    edge_main, edge_rest = edge_state(taps_ref, rest, recv_rest)
    far_main, far_rest = recv_main + edge_main, recv_rest + edge_rest
    near_main, near_rest = unfold(near_ref[0:STATE_ROWS, :])
    carried_ref[0] = near_main + far_main
    carried_ref[1] = joined(near_rest + far_rest, recv_rest, recv_rest)
    sent_ref[...] = fold(main + far_main, joined(rest + far_rest, rest, recv_rest))


def local_kernel(
    first_ref, x_ref, conv_ref, halo_ref, taps_ref, carried_ref, num_ref, win_ref, phi_ref
):
    count = x_ref.shape[0]
    taps = [taps_ref[index] for index in range(TAPS)]
    key_row = lax.broadcasted_iota(jnp.int32, (BLK, BLK), 0)
    query_lane = lax.broadcasted_iota(jnp.int32, (BLK, BLK), 1)
    causal = key_row <= query_lane
    span = WIN + BLK
    near_row = lax.broadcasted_iota(jnp.int32, (span, BLK), 0)
    near_lane = lax.broadcasted_iota(jnp.int32, (span, BLK), 1)
    inside = (near_row >= near_lane) & (near_row <= near_lane + WIN)
    inside_first = inside & ((near_row >= WIN) | (first_ref[0] == 0))
    before_key = halo_ref[STATE_ROWS : STATE_ROWS + FEAT, :]
    before_raw = halo_ref[STATE_ROWS + FEAT :, :].astype(F32)
    before_val = convolve(taps, before_raw, jnp.zeros((VDIM, BLK), F32))
    first_val = convolve(taps, x_ref[0, 2 * FEAT :, :].astype(F32), before_raw)
    state = jnp.concatenate([carried_ref[0], carried_ref[1][:, :EDGE]], axis=1)
    blank = jnp.zeros((BLK - WIN, BLK), BF16)
    for blk in range(count):
        query = x_ref[blk, 0:FEAT, :]
        key = x_ref[blk, FEAT : 2 * FEAT, :]
        value = first_val if blk == 0 else conv_ref[blk]
        phi_query = features(query.astype(F32), False)
        phi_ref[:, blk * BLK : (blk + 1) * BLK] = phi_query
        scores = tn(jnp.concatenate([before_key, key], axis=1), query) * 0.25
        own = scores[BLK:]
        weights = jnp.where(causal, 1.0 + own + 0.5 * own * own, 0.0).astype(BF16)
        num_ref[blk] = nn(value, weights) + nn(state.astype(BF16), phi_query)
        masked = jnp.where(inside_first if blk == 0 else inside, scores[BLK - WIN :], -1e30)
        row_max = jnp.max(masked, axis=0, keepdims=True)
        exp_scores = jnp.exp(masked - row_max)
        row_sum = jnp.sum(exp_scores, axis=0, keepdims=True)
        probs = jnp.concatenate([blank, exp_scores.astype(BF16)], axis=0)
        win = nn(jnp.concatenate([before_val, value], axis=1), probs)
        win_ref[blk] = win / row_sum
        if blk + 1 < count:
            state = state + nt(value, features(key.astype(F32), True))
        before_key, before_val = key, value


def final_kernel(carried_ref, recv_ref, taps_ref, num_ref, win_ref, phi_ref, out_ref):
    recv_main, recv_rest = unfold(recv_ref[...])
    edge_main, edge_rest = edge_state(taps_ref, carried_ref[1], recv_rest)
    rest = (recv_rest + edge_rest)[:, :EDGE]
    state = jnp.concatenate([recv_main + edge_main, rest], axis=1).astype(BF16)
    gain = taps_ref[TAPS]
    for blk in range(num_ref.shape[0]):
        num = num_ref[blk] + nn(state, phi_ref[:, blk * BLK : (blk + 1) * BLK])
        mean_square = jnp.sum(num * num, axis=0, keepdims=True) * (1.0 / VDIM)
        linear = num * lax.rsqrt(mean_square + 1e-06) * gain
        out_ref[blk] = (linear + win_ref[blk]).astype(BF16)


def unpack_kernel(x_ref, out_ref):
    out_ref[...] = x_ref[...].reshape(HEADS * VDIM, BLK).T


SMEM = pl.BlockSpec(memory_space=pltpu.SMEM)
VMEM = pl.BlockSpec(memory_space=pltpu.VMEM)


def call(kernel, outs, scalars, outer_arrays, arrays):
    arrays = [pltpu.with_memory_space_constraint(array, pltpu.VMEM) for array in arrays]
    count = len(outer_arrays) + len(arrays)
    single = len(outs) == 1
    return pl.pallas_call(
        kernel,
        out_shape=outs[0] if single else tuple(outs),
        in_specs=[SMEM] * len(scalars) + [VMEM] * count,
        out_specs=VMEM if single else tuple(VMEM for _ in outs),
    )(*scalars, *outer_arrays, *arrays)


def scalar(value):
    return jnp.asarray(value).astype(jnp.int32).reshape(1)


def on_device(query_rows, key_rows, value_rows, conv_weight, norm_gain):
    group = ("pair", "core", "inner")
    stack = ("quad", "half")
    members = lax.axis_size(group)
    groups = lax.axis_size(stack)
    tokens = members * BLK

    def upward(value, step):
        return lax.ppermute(value, stack, [(i, i + step) for i in range(groups - step)])

    packed, taps = call(
        pack_kernel,
        [pltpu.VMEM((HEADS, PART, BLK), BF16), pltpu.VMEM((TAPS + 1, VDIM, LANES), F32)],
        [scalar(lax.axis_index(group))],
        [query_rows, key_rows, value_rows, conv_weight, norm_gain.reshape(1, HEADS * VDIM)],
        [],
    )
    mine = lax.all_to_all(packed, group, 0, 0)
    sent, own, conv = call(
        state_kernel,
        [
            pltpu.VMEM((STATE_ROWS + FEAT + VDIM, BLK), BF16),
            pltpu.VMEM((2, VDIM, LANES), F32),
            pltpu.VMEM((members, VDIM, BLK), BF16),
        ],
        [],
        [],
        [mine, taps],
    )
    near = upward(sent, 1)
    state_shapes = [pltpu.VMEM((STATE_ROWS, LANES), BF16), pltpu.VMEM((2, VDIM, LANES), F32)]
    sent, pair = call(merge_one_kernel, state_shapes, [], [], [own, near, taps])
    far = upward(sent, 2)
    sent, carried = call(merge_two_kernel, state_shapes, [], [], [pair, near, far, taps])
    farthest = upward(sent, 4)
    num, win, phi = call(
        local_kernel,
        [
            pltpu.VMEM((members, VDIM, BLK), F32),
            pltpu.VMEM((members, VDIM, BLK), F32),
            pltpu.VMEM((NPHI, tokens), BF16),
        ],
        [scalar(lax.axis_index(stack) == 0)],
        [],
        [mine, conv, near, taps, carried],
    )
    done = call(
        final_kernel,
        [pltpu.VMEM((members, VDIM, BLK), BF16)],
        [],
        [],
        [carried, farthest, taps, num, win, phi],
    )
    heads = lax.all_to_all(done, group, 0, 0)
    out = jax.ShapeDtypeStruct((BLK, HEADS * VDIM), BF16)
    return call(unpack_kernel, [out], [], [], [heads])


def solution(mesh):
    outer, inner = mesh.shape["outer"], mesh.shape["inner"]
    pair = HEADS // inner // 2
    shape = (mesh.shape["dp"], outer // (2 * 2 * pair), 2, pair, 2, inner)
    split = Mesh(
        np.asarray(mesh.devices).reshape(shape), ("dp", "quad", "half", "pair", "core", "inner")
    )
    rows = P(("dp", "quad", "half", "pair", "core", "inner"), None)
    return jax.shard_map(
        on_device,
        mesh=split,
        in_specs=(rows, rows, rows, P(), P()),
        out_specs=rows,
        check_vma=False,
    )
```

```python
import jax
import jax.numpy as jnp
import numpy as np
from jax import lax
from jax.experimental import pallas as pl
from jax.experimental.pallas import tpu as pltpu
from jax.sharding import Mesh, PartitionSpec as P

HEADS = 16
FEAT = 16
VDIM = 64
TAPS = 3
WIN = 64
BLK = 128
NPHI = 160
LANES = 128
EDGE = NPHI - LANES
HALF = VDIM // 2
STATE_ROWS = VDIM + HALF
PART = FEAT + FEAT + VDIM
F32 = jnp.float32
BF16 = jnp.bfloat16


def nt(lhs, rhs):
    return lax.dot_general(lhs, rhs, (((1,), (1,)), ((), ())), preferred_element_type=F32)


def tn(lhs, rhs):
    return lax.dot_general(lhs, rhs, (((0,), (0,)), ((), ())), preferred_element_type=F32)


def nn(lhs, rhs):
    return lax.dot_general(lhs, rhs, (((1,), (0,)), ((), ())), preferred_element_type=F32)


def lanes(rows):
    return lax.broadcasted_iota(jnp.int32, (rows, LANES), 1)


def features(entries, weighted):
    lin, diag, off = (0.25, 1.0 / 32.0, 1.0 / 16.0) if weighted else (1.0, 1.0, 1.0)
    rows = [entries * lin if weighted else entries]
    base = entries * off if weighted else entries
    rows.append(entries * entries * diag if weighted else entries * entries)
    for step in range(1, FEAT // 2):
        rolled = jnp.concatenate([entries[step:], entries[:step]], axis=0)
        rows.append(base * rolled)
    rows.append(base[: FEAT // 2] * entries[FEAT // 2 :])
    tail = lax.broadcasted_iota(jnp.int32, (8, entries.shape[1]), 0)
    rows.append(jnp.where(tail == 0, 1.0, 0.0).astype(F32))
    return jnp.concatenate(rows, axis=0).astype(BF16)


def convolve(taps, raw, before):
    lane = lanes(VDIM)
    one = jnp.where(lane < 1, pltpu.roll(before, 1, 1), pltpu.roll(raw, 1, 1))
    two = jnp.where(lane < 2, pltpu.roll(before, 2, 1), pltpu.roll(raw, 2, 1))
    return (taps[0] * raw + taps[1] * one + taps[2] * two).astype(BF16)


def fold(main, rest):
    both = rest[:HALF] + pltpu.roll(rest[HALF:], LANES // 2, 1)
    return jnp.concatenate([main, both], axis=0).astype(BF16)


def unfold(packed):
    wide = packed.astype(F32)
    both = wide[VDIM:STATE_ROWS]
    low = lanes(HALF) < LANES // 2
    upper = jnp.where(low, both, 0.0)
    lower = jnp.where(low, pltpu.roll(both, LANES // 2, 1), 0.0)
    return wide[:VDIM], jnp.concatenate([upper, lower], axis=0)


def edge_state(taps, key_rest, tail_rest):
    lane = lanes(VDIM)
    same = pltpu.roll(tail_rest, LANES - EDGE, 1)
    last = pltpu.roll(tail_rest, LANES - EDGE - 1, 1)
    first = jnp.where(lane == 0, taps[1] * last + taps[2] * same, 0.0)
    missing = jnp.where(lane == 1, taps[2] * same, first).astype(BF16)
    keys = pltpu.roll(key_rest[:FEAT], LANES - EDGE - 2, 1)
    keys = jnp.where(lanes(FEAT) < 2, keys, 0.0)
    state = nt(missing, features(keys, True))
    blank = jnp.zeros((VDIM, LANES - EDGE), F32)
    return state[:, :LANES], jnp.concatenate([state[:, LANES:], blank], axis=1)


def joined(rest, tail_rest, key_rest):
    lane = lanes(VDIM)
    return jnp.where(lane < EDGE, rest, jnp.where(lane < EDGE + 2, tail_rest, key_rest))


def pack_kernel(head_ref, q_ref, k_ref, v_ref, w_ref, gain_ref, out_ref, taps_ref):
    out_ref[:, 0:FEAT, :] = q_ref[...].T.reshape(HEADS, FEAT, BLK)
    out_ref[:, FEAT : 2 * FEAT, :] = k_ref[...].T.reshape(HEADS, FEAT, BLK)
    out_ref[:, 2 * FEAT :, :] = v_ref[...].T.reshape(HEADS, VDIM, BLK)
    rows = jnp.concatenate([w_ref[...], gain_ref[...], jnp.zeros((4, HEADS * VDIM), F32)], axis=0)
    mine = jnp.zeros((8, VDIM), F32)
    for head in range(HEADS):
        mine = jnp.where(head_ref[0] == head, rows[:, head * VDIM : (head + 1) * VDIM], mine)
    columns = mine.T
    for index in range(TAPS + 1):
        taps_ref[index] = jnp.broadcast_to(columns[:, index : index + 1], (VDIM, LANES))


def state_kernel(x_ref, taps_ref, sent_ref, own_ref, conv_ref):
    count = x_ref.shape[0]
    taps = [taps_ref[index] for index in range(TAPS)]
    total = jnp.zeros((VDIM, NPHI), F32)
    before = jnp.zeros((VDIM, BLK), F32)
    for blk in range(count):
        raw = x_ref[blk, 2 * FEAT :, :].astype(F32)
        conv = convolve(taps, raw, before)
        conv_ref[blk] = conv
        phi = features(x_ref[blk, FEAT : 2 * FEAT, :].astype(F32), True)
        total = total + nt(conv, phi)
        before = raw
    lane = lanes(VDIM)
    blank = jnp.zeros((VDIM, LANES - EDGE), F32)
    rest = jnp.concatenate([total[:, LANES:], blank], axis=1)
    tail = pltpu.roll(before, EDGE + 2, 1)
    first = x_ref[0, FEAT : 2 * FEAT, :].astype(F32)
    first = jnp.concatenate([first, jnp.zeros((VDIM - FEAT, BLK), F32)], axis=0)
    first = jnp.where(lane < EDGE + 4, pltpu.roll(first, EDGE + 2, 1), 0.0)
    rest = joined(rest, tail, first)
    main = total[:, :LANES]
    own_ref[0] = main
    own_ref[1] = rest
    sent_ref[0:STATE_ROWS, :] = fold(main, rest)
    sent_ref[STATE_ROWS:, :] = x_ref[count - 1, FEAT:, :]


def merge_one_kernel(own_ref, recv_ref, taps_ref, sent_ref, pair_ref):
    main, rest = own_ref[0], own_ref[1]
    recv_main, recv_rest = unfold(recv_ref[0:STATE_ROWS, :])
    edge_main, edge_rest = edge_state(taps_ref, rest, recv_rest)
    main = main + recv_main + edge_main
    rest = joined(rest + recv_rest + edge_rest, rest, recv_rest)
    pair_ref[0] = main
    pair_ref[1] = rest
    sent_ref[...] = fold(main, rest)


def merge_two_kernel(pair_ref, near_ref, recv_ref, taps_ref, sent_ref, carried_ref):
    main, rest = pair_ref[0], pair_ref[1]
    recv_main, recv_rest = unfold(recv_ref[...])
    edge_main, edge_rest = edge_state(taps_ref, rest, recv_rest)
    far_main, far_rest = recv_main + edge_main, recv_rest + edge_rest
    near_main, near_rest = unfold(near_ref[0:STATE_ROWS, :])
    carried_ref[0] = near_main + far_main
    carried_ref[1] = joined(near_rest + far_rest, recv_rest, recv_rest)
    sent_ref[...] = fold(main + far_main, joined(rest + far_rest, rest, recv_rest))


def local_kernel(
    first_ref, x_ref, conv_ref, halo_ref, taps_ref, carried_ref, num_ref, win_ref, phi_ref
):
    count = x_ref.shape[0]
    taps = [taps_ref[index] for index in range(TAPS)]
    key_row = lax.broadcasted_iota(jnp.int32, (BLK, BLK), 0)
    query_lane = lax.broadcasted_iota(jnp.int32, (BLK, BLK), 1)
    causal = key_row <= query_lane
    span = WIN + BLK
    near_row = lax.broadcasted_iota(jnp.int32, (span, BLK), 0)
    near_lane = lax.broadcasted_iota(jnp.int32, (span, BLK), 1)
    inside = (near_row >= near_lane) & (near_row <= near_lane + WIN)
    inside_first = inside & ((near_row >= WIN) | (first_ref[0] == 0))
    before_key = halo_ref[STATE_ROWS : STATE_ROWS + FEAT, :]
    before_raw = halo_ref[STATE_ROWS + FEAT :, :].astype(F32)
    before_val = convolve(taps, before_raw, jnp.zeros((VDIM, BLK), F32))
    first_val = convolve(taps, x_ref[0, 2 * FEAT :, :].astype(F32), before_raw)
    state = jnp.concatenate([carried_ref[0], carried_ref[1][:, :EDGE]], axis=1)
    blank = jnp.zeros((BLK - WIN, BLK), BF16)
    for blk in range(count):
        query = x_ref[blk, 0:FEAT, :]
        key = x_ref[blk, FEAT : 2 * FEAT, :]
        value = first_val if blk == 0 else conv_ref[blk]
        phi_query = features(query.astype(F32), False)
        phi_ref[:, blk * BLK : (blk + 1) * BLK] = phi_query
        scores = tn(jnp.concatenate([before_key, key], axis=1), query) * 0.25
        own = scores[BLK:]
        weights = jnp.where(causal, 1.0 + own + 0.5 * own * own, 0.0).astype(BF16)
        num_ref[blk] = nn(value, weights) + nn(state.astype(BF16), phi_query)
        masked = jnp.where(inside_first if blk == 0 else inside, scores[BLK - WIN :], -1e30)
        row_max = jnp.max(masked, axis=0, keepdims=True)
        exp_scores = jnp.exp(masked - row_max)
        row_sum = jnp.sum(exp_scores, axis=0, keepdims=True)
        probs = jnp.concatenate([blank, exp_scores.astype(BF16)], axis=0)
        win = nn(jnp.concatenate([before_val, value], axis=1), probs)
        win_ref[blk] = win / row_sum
        if blk + 1 < count:
            state = state + nt(value, features(key.astype(F32), True))
        before_key, before_val = key, value


def final_kernel(carried_ref, recv_ref, taps_ref, num_ref, win_ref, phi_ref, out_ref):
    recv_main, recv_rest = unfold(recv_ref[...])
    edge_main, edge_rest = edge_state(taps_ref, carried_ref[1], recv_rest)
    rest = (recv_rest + edge_rest)[:, :EDGE]
    state = jnp.concatenate([recv_main + edge_main, rest], axis=1).astype(BF16)
    gain = taps_ref[TAPS]
    for blk in range(num_ref.shape[0]):
        num = num_ref[blk] + nn(state, phi_ref[:, blk * BLK : (blk + 1) * BLK])
        mean_square = jnp.sum(num * num, axis=0, keepdims=True) * (1.0 / VDIM)
        linear = num * lax.rsqrt(mean_square + 1e-06) * gain
        out_ref[blk] = (linear + win_ref[blk]).astype(BF16)


def unpack_kernel(x_ref, out_ref):
    out_ref[...] = x_ref[...].reshape(HEADS * VDIM, BLK).T


SMEM = pl.BlockSpec(memory_space=pltpu.SMEM)
VMEM = pl.BlockSpec(memory_space=pltpu.VMEM)


def call(kernel, outs, scalars, outer_arrays, arrays):
    arrays = [pltpu.with_memory_space_constraint(array, pltpu.VMEM) for array in arrays]
    count = len(outer_arrays) + len(arrays)
    single = len(outs) == 1
    return pl.pallas_call(
        kernel,
        out_shape=outs[0] if single else tuple(outs),
        in_specs=[SMEM] * len(scalars) + [VMEM] * count,
        out_specs=VMEM if single else tuple(VMEM for _ in outs),
        compiler_params=pltpu.CompilerParams(vmem_limit_bytes=8 * 1024 * 1024),
    )(*scalars, *outer_arrays, *arrays)


def scalar(value):
    return jnp.asarray(value).astype(jnp.int32).reshape(1)


def on_device(query_rows, key_rows, value_rows, conv_weight, norm_gain):
    group = ("pair", "core", "inner")
    stack = ("quad", "half")
    members = lax.axis_size(group)
    groups = lax.axis_size(stack)
    tokens = members * BLK

    def upward(value, step):
        return lax.ppermute(value, stack, [(i, i + step) for i in range(groups - step)])

    packed, taps = call(
        pack_kernel,
        [pltpu.VMEM((HEADS, PART, BLK), BF16), pltpu.VMEM((TAPS + 1, VDIM, LANES), F32)],
        [scalar(lax.axis_index(group))],
        [query_rows, key_rows, value_rows, conv_weight, norm_gain.reshape(1, HEADS * VDIM)],
        [],
    )
    mine = lax.all_to_all(packed, group, 0, 0)
    sent, own, conv = call(
        state_kernel,
        [
            pltpu.VMEM((STATE_ROWS + FEAT + VDIM, BLK), BF16),
            pltpu.VMEM((2, VDIM, LANES), F32),
            pltpu.VMEM((members, VDIM, BLK), BF16),
        ],
        [],
        [],
        [mine, taps],
    )
    near = upward(sent, 1)
    state_shapes = [pltpu.VMEM((STATE_ROWS, LANES), BF16), pltpu.VMEM((2, VDIM, LANES), F32)]
    sent, pair = call(merge_one_kernel, state_shapes, [], [], [own, near, taps])
    far = upward(sent, 2)
    sent, carried = call(merge_two_kernel, state_shapes, [], [], [pair, near, far, taps])
    farthest = upward(sent, 4)
    num, win, phi = call(
        local_kernel,
        [
            pltpu.VMEM((members, VDIM, BLK), F32),
            pltpu.VMEM((members, VDIM, BLK), F32),
            pltpu.VMEM((NPHI, tokens), BF16),
        ],
        [scalar(lax.axis_index(stack) == 0)],
        [],
        [mine, conv, near, taps, carried],
    )
    done = call(
        final_kernel,
        [pltpu.VMEM((members, VDIM, BLK), BF16)],
        [],
        [],
        [carried, farthest, taps, num, win, phi],
    )
    heads = lax.all_to_all(done, group, 0, 0)
    out = jax.ShapeDtypeStruct((BLK, HEADS * VDIM), BF16)
    return call(unpack_kernel, [out], [], [], [heads])


def solution(mesh):
    outer, inner = mesh.shape["outer"], mesh.shape["inner"]
    pair = HEADS // inner // 2
    shape = (mesh.shape["dp"], outer // (2 * 2 * pair), 2, pair, 2, inner)
    split = Mesh(
        np.asarray(mesh.devices).reshape(shape), ("dp", "quad", "half", "pair", "core", "inner")
    )
    rows = P(("dp", "quad", "half", "pair", "core", "inner"), None)
    return jax.shard_map(
        on_device,
        mesh=split,
        in_specs=(rows, rows, rows, P(), P()),
        out_specs=rows,
        check_vma=False,
    )
```

```python
import jax
import jax.numpy as jnp
import numpy as np
from jax import lax
from jax.experimental import pallas as pl
from jax.experimental.pallas import tpu as pltpu
from jax.sharding import Mesh, PartitionSpec as P

HEADS = 16
FEAT = 16
VDIM = 64
TAPS = 3
WIN = 64
BLK = 128
NPHI = 160
LANES = 128
EDGE = NPHI - LANES
HALF = VDIM // 2
STATE_ROWS = VDIM + HALF
PART = FEAT + FEAT + VDIM
F32 = jnp.float32
BF16 = jnp.bfloat16


def nt(lhs, rhs):
    return lax.dot_general(lhs, rhs, (((1,), (1,)), ((), ())), preferred_element_type=F32)


def tn(lhs, rhs):
    return lax.dot_general(lhs, rhs, (((0,), (0,)), ((), ())), preferred_element_type=F32)


def nn(lhs, rhs):
    return lax.dot_general(lhs, rhs, (((1,), (0,)), ((), ())), preferred_element_type=F32)


def lanes(rows):
    return lax.broadcasted_iota(jnp.int32, (rows, LANES), 1)


def features(entries, weighted):
    lin, diag, off = (0.25, 1.0 / 32.0, 1.0 / 16.0) if weighted else (1.0, 1.0, 1.0)
    rows = [entries * lin if weighted else entries]
    base = entries * off if weighted else entries
    rows.append(entries * entries * diag if weighted else entries * entries)
    for step in range(1, FEAT // 2):
        rolled = jnp.concatenate([entries[step:], entries[:step]], axis=0)
        rows.append(base * rolled)
    rows.append(base[: FEAT // 2] * entries[FEAT // 2 :])
    tail = lax.broadcasted_iota(jnp.int32, (8, entries.shape[1]), 0)
    rows.append(jnp.where(tail == 0, 1.0, 0.0).astype(F32))
    return jnp.concatenate(rows, axis=0).astype(BF16)


def convolve(taps, raw, before):
    lane = lanes(VDIM)
    one = jnp.where(lane < 1, pltpu.roll(before, 1, 1), pltpu.roll(raw, 1, 1))
    two = jnp.where(lane < 2, pltpu.roll(before, 2, 1), pltpu.roll(raw, 2, 1))
    return (taps[0] * raw + taps[1] * one + taps[2] * two).astype(BF16)


def fold(main, rest):
    both = rest[:HALF] + pltpu.roll(rest[HALF:], LANES // 2, 1)
    return jnp.concatenate([main, both], axis=0).astype(BF16)


def unfold(packed):
    wide = packed.astype(F32)
    both = wide[VDIM:STATE_ROWS]
    low = lanes(HALF) < LANES // 2
    upper = jnp.where(low, both, 0.0)
    lower = jnp.where(low, pltpu.roll(both, LANES // 2, 1), 0.0)
    return wide[:VDIM], jnp.concatenate([upper, lower], axis=0)


def edge_state(taps_ref, edges):
    lane = lanes(VDIM)
    values = jnp.zeros((VDIM, LANES), F32)
    keys = jnp.zeros((FEAT, LANES), F32)
    for index, (key_rest, tail_rest, counts) in enumerate(edges):
        at = 2 * index
        same = pltpu.roll(tail_rest, (LANES - EDGE + at) % LANES, 1)
        last = pltpu.roll(tail_rest, (LANES - EDGE - 1 + at) % LANES, 1)
        missing = jnp.where(lane == at, taps_ref[1] * last + taps_ref[2] * same, 0.0)
        missing = jnp.where(lane == at + 1, taps_ref[2] * same, missing)
        if counts is not None:
            missing = jnp.where(counts, missing, 0.0)
        values = values + missing
        moved = pltpu.roll(key_rest[:FEAT], (LANES - EDGE - 2 + at) % LANES, 1)
        place = lanes(FEAT)
        keys = keys + jnp.where((place >= at) & (place < at + 2), moved, 0.0)
    state = nt(values.astype(BF16), features(keys, True))
    blank = jnp.zeros((VDIM, LANES - EDGE), F32)
    return state[:, :LANES], jnp.concatenate([state[:, LANES:], blank], axis=1)


def joined(rest, tail_rest, key_rest):
    lane = lanes(VDIM)
    return jnp.where(lane < EDGE, rest, jnp.where(lane < EDGE + 2, tail_rest, key_rest))


def pack_kernel(head_ref, q_ref, k_ref, v_ref, w_ref, gain_ref, out_ref, taps_ref):
    out_ref[:, 0:FEAT, :] = q_ref[...].T.reshape(HEADS, FEAT, BLK)
    out_ref[:, FEAT : 2 * FEAT, :] = k_ref[...].T.reshape(HEADS, FEAT, BLK)
    out_ref[:, 2 * FEAT :, :] = v_ref[...].T.reshape(HEADS, VDIM, BLK)
    rows = jnp.concatenate([w_ref[...], gain_ref[...], jnp.zeros((4, HEADS * VDIM), F32)], axis=0)
    mine = jnp.zeros((8, VDIM), F32)
    for head in range(HEADS):
        mine = jnp.where(head_ref[0] == head, rows[:, head * VDIM : (head + 1) * VDIM], mine)
    columns = mine.T
    for index in range(TAPS + 1):
        taps_ref[index] = jnp.broadcast_to(columns[:, index : index + 1], (VDIM, LANES))


def state_kernel(x_ref, taps_ref, sent_ref, own_ref, conv_ref):
    count = x_ref.shape[0]
    taps = [taps_ref[index] for index in range(TAPS)]
    total = jnp.zeros((VDIM, NPHI), F32)
    before = jnp.zeros((VDIM, BLK), F32)
    for blk in range(count):
        raw = x_ref[blk, 2 * FEAT :, :].astype(F32)
        conv = convolve(taps, raw, before)
        conv_ref[blk] = conv
        phi = features(x_ref[blk, FEAT : 2 * FEAT, :].astype(F32), True)
        total = total + nt(conv, phi)
        before = raw
    lane = lanes(VDIM)
    blank = jnp.zeros((VDIM, LANES - EDGE), F32)
    rest = jnp.concatenate([total[:, LANES:], blank], axis=1)
    tail = pltpu.roll(before, EDGE + 2, 1)
    first = x_ref[0, FEAT : 2 * FEAT, :].astype(F32)
    first = jnp.concatenate([first, jnp.zeros((VDIM - FEAT, BLK), F32)], axis=0)
    first = jnp.where(lane < EDGE + 4, pltpu.roll(first, EDGE + 2, 1), 0.0)
    rest = joined(rest, tail, first)
    main = total[:, :LANES]
    own_ref[0] = main
    own_ref[1] = rest
    sent_ref[0:STATE_ROWS, :] = fold(main, rest)
    sent_ref[STATE_ROWS:, :] = x_ref[count - 1, FEAT:, :]


def inside_window(first):
    row = lax.broadcasted_iota(jnp.int32, (WIN + BLK, BLK), 0)
    lane = lax.broadcasted_iota(jnp.int32, (WIN + BLK, BLK), 1)
    inside = (row >= lane) & (row <= lane + WIN)
    return inside if first is None else inside & ((row >= WIN) | (first == 0))


def block_parts(query, key, value, before_key, before_value, inside):
    scores = tn(jnp.concatenate([before_key, key], axis=1), query) * 0.25
    own = scores[BLK:]
    key_row = lax.broadcasted_iota(jnp.int32, (BLK, BLK), 0)
    query_lane = lax.broadcasted_iota(jnp.int32, (BLK, BLK), 1)
    weights = 1.0 + own + 0.5 * own * own
    weights = jnp.where(key_row <= query_lane, weights, 0.0).astype(BF16)
    masked = jnp.where(inside, scores[BLK - WIN :], -1e30)
    row_max = jnp.max(masked, axis=0, keepdims=True)
    exp_scores = jnp.exp(masked - row_max)
    row_sum = jnp.sum(exp_scores, axis=0, keepdims=True)
    blank = jnp.zeros((BLK - WIN, BLK), BF16)
    probs = jnp.concatenate([blank, exp_scores.astype(BF16)], axis=0)
    window = nn(jnp.concatenate([before_value, value], axis=1), probs)
    return nn(value, weights), window / row_sum


def local_kernel(x_ref, conv_ref, num_ref, win_ref, phi_ref):
    count = x_ref.shape[0]
    inside = inside_window(None)
    state = jnp.zeros((VDIM, NPHI), F32)
    for blk in range(count):
        query = x_ref[blk, 0:FEAT, :]
        key = x_ref[blk, FEAT : 2 * FEAT, :]
        value = conv_ref[blk]
        phi_query = features(query.astype(F32), False)
        phi_ref[:, blk * BLK : (blk + 1) * BLK] = phi_query
        if blk > 0:
            own, win = block_parts(query, key, value, before_key, before_value, inside)
            num_ref[blk] = own + nn(state.astype(BF16), phi_query)
            win_ref[blk] = win
        if blk + 1 < count:
            state = state + nt(value, features(key.astype(F32), True))
        before_key, before_value = key, value


def merge_kernel(
    first_ref,
    own_ref,
    near_ref,
    taps_ref,
    x_ref,
    num_in_ref,
    win_in_ref,
    sent_ref,
    edge_ref,
    num_ref,
    win_ref,
):
    main, rest = own_ref[0], own_ref[1]
    near_main, near_rest = unfold(near_ref[0:STATE_ROWS, :])
    edge_main, edge_rest = edge_state(taps_ref, [(rest, near_rest, None)])
    edge_ref[0] = edge_main
    edge_ref[1] = edge_rest
    both = fold(main + near_main + edge_main, joined(rest + near_rest + edge_rest, rest, near_rest))
    for quad in range(sent_ref.shape[0]):
        sent_ref[quad] = both
    taps = [taps_ref[index] for index in range(TAPS)]
    raw = near_ref[STATE_ROWS + FEAT :, :].astype(F32)
    before_value = convolve(taps, raw, jnp.zeros((VDIM, BLK), F32))
    value = convolve(taps, x_ref[0, 2 * FEAT :, :].astype(F32), raw)
    num_ref[0], win_ref[0] = block_parts(
        x_ref[0, 0:FEAT, :],
        x_ref[0, FEAT : 2 * FEAT, :],
        value,
        near_ref[STATE_ROWS : STATE_ROWS + FEAT, :],
        before_value,
        inside_window(first_ref[0]),
    )


def final_kernel(
    quad_ref,
    near_ref,
    others_ref,
    taps_ref,
    edge_ref,
    num_ref,
    win_ref,
    phi_ref,
    out_ref,
):
    quads = others_ref.shape[0]
    parts = [unfold(others_ref[quad]) for quad in range(quads)]
    main, rest = unfold(near_ref[0:STATE_ROWS, :])
    edges = []
    for quad in range(quads - 1):
        reached = quad < quad_ref[0]
        main = main + jnp.where(reached, parts[quad][0], 0.0)
        rest = rest + jnp.where(reached, parts[quad][1], 0.0)
        edges.append((parts[quad + 1][1], parts[quad][1], reached))
    edge_main, edge_rest = edge_state(taps_ref, edges)
    state = jnp.concatenate([main + edge_main, (rest + edge_rest)[:, :EDGE]], axis=1)
    group_edge = jnp.concatenate([edge_ref[0], edge_ref[1][:, :EDGE]], axis=1)
    later = (state + group_edge).astype(BF16)
    state = state.astype(BF16)
    gain = taps_ref[TAPS]
    for blk in range(num_ref.shape[0]):
        phi = phi_ref[:, blk * BLK : (blk + 1) * BLK]
        num = num_ref[blk] + nn(state if blk == 0 else later, phi)
        mean_square = jnp.sum(num * num, axis=0, keepdims=True) * (1.0 / VDIM)
        linear = num * lax.rsqrt(mean_square + 1e-06) * gain
        out_ref[blk] = (linear + win_ref[blk]).astype(BF16)


def unpack_kernel(x_ref, out_ref):
    out_ref[...] = x_ref[...].reshape(HEADS * VDIM, BLK).T


SMEM = pl.BlockSpec(memory_space=pltpu.SMEM)
VMEM = pl.BlockSpec(memory_space=pltpu.VMEM)


def call(kernel, outs, scalars, outer_arrays, arrays, aliases=None):
    limit = None if outer_arrays else 8 * 1024 * 1024
    arrays = [pltpu.with_memory_space_constraint(array, pltpu.VMEM) for array in arrays]
    count = len(outer_arrays) + len(arrays)
    single = len(outs) == 1
    return pl.pallas_call(
        kernel,
        out_shape=outs[0] if single else tuple(outs),
        in_specs=[SMEM] * len(scalars) + [VMEM] * count,
        out_specs=VMEM if single else tuple(VMEM for _ in outs),
        input_output_aliases=aliases or {},
        compiler_params=pltpu.CompilerParams(vmem_limit_bytes=limit),
    )(*scalars, *outer_arrays, *arrays)


def scalar(value):
    return jnp.asarray(value).astype(jnp.int32).reshape(1)


def on_device(query_rows, key_rows, value_rows, conv_weight, norm_gain):
    group = ("pair", "core", "inner")
    stack = ("quad", "half")
    members = lax.axis_size(group)
    groups = lax.axis_size(stack)
    quads = lax.axis_size("quad")

    def upward(value):
        return lax.ppermute(value, stack, [(i, i + 1) for i in range(groups - 1)])

    packed, taps = call(
        pack_kernel,
        [pltpu.VMEM((HEADS, PART, BLK), BF16), pltpu.VMEM((TAPS + 1, VDIM, LANES), F32)],
        [scalar(lax.axis_index(group))],
        [query_rows, key_rows, value_rows, conv_weight, norm_gain.reshape(1, HEADS * VDIM)],
        [],
    )
    mine = lax.all_to_all(packed, group, 0, 0)
    sent, own, conv = call(
        state_kernel,
        [
            pltpu.VMEM((STATE_ROWS + FEAT + VDIM, BLK), BF16),
            pltpu.VMEM((2, VDIM, LANES), F32),
            pltpu.VMEM((members, VDIM, BLK), BF16),
        ],
        [],
        [],
        [mine, taps],
    )
    near = upward(sent)
    block = (VDIM, BLK)
    num, win, phi = call(
        local_kernel,
        [
            pltpu.VMEM((members, *block), F32),
            pltpu.VMEM((members, *block), F32),
            pltpu.VMEM((NPHI, members * BLK), BF16),
        ],
        [],
        [],
        [mine, conv],
    )
    sent, edge, num, win = call(
        merge_kernel,
        [
            pltpu.VMEM((quads, STATE_ROWS, LANES), BF16),
            pltpu.VMEM((2, VDIM, LANES), F32),
            pltpu.VMEM((members, *block), F32),
            pltpu.VMEM((members, *block), F32),
        ],
        [scalar(lax.axis_index(stack) == 0)],
        [],
        [own, near, taps, mine, num, win],
        {5: 2, 6: 3},
    )
    others = lax.all_to_all(sent, "quad", 0, 0)
    done = call(
        final_kernel,
        [pltpu.VMEM((members, *block), BF16)],
        [scalar(lax.axis_index("quad"))],
        [],
        [near, others, taps, edge, num, win, phi],
    )
    heads = lax.all_to_all(done, group, 0, 0)
    out = jax.ShapeDtypeStruct((BLK, HEADS * VDIM), BF16)
    return call(unpack_kernel, [out], [], [], [heads])


def solution(mesh):
    outer, inner = mesh.shape["outer"], mesh.shape["inner"]
    pair = HEADS // inner // 2
    shape = (mesh.shape["dp"], outer // (2 * 2 * pair), 2, pair, 2, inner)
    split = Mesh(
        np.asarray(mesh.devices).reshape(shape), ("dp", "quad", "half", "pair", "core", "inner")
    )
    rows = P(("dp", "quad", "half", "pair", "core", "inner"), None)
    return jax.shard_map(
        on_device,
        mesh=split,
        in_specs=(rows, rows, rows, P(), P()),
        out_specs=rows,
        check_vma=False,
    )
```

```python
import jax
import jax.numpy as jnp
import numpy as np
from jax import lax
from jax.experimental import pallas as pl
from jax.experimental.pallas import tpu as pltpu
from jax.sharding import Mesh, PartitionSpec as P

HEADS = 16
FEAT = 16
VDIM = 64
TAPS = 3
WIN = 64
BLK = 128
NPHI = 160
LANES = 128
EDGE = NPHI - LANES
HALF = VDIM // 2
STATE_ROWS = VDIM + HALF
PART = FEAT + FEAT + VDIM
F32 = jnp.float32
BF16 = jnp.bfloat16


def nt(lhs, rhs):
    return lax.dot_general(lhs, rhs, (((1,), (1,)), ((), ())), preferred_element_type=F32)


def tn(lhs, rhs):
    return lax.dot_general(lhs, rhs, (((0,), (0,)), ((), ())), preferred_element_type=F32)


def nn(lhs, rhs):
    return lax.dot_general(lhs, rhs, (((1,), (0,)), ((), ())), preferred_element_type=F32)


def lanes(rows):
    return lax.broadcasted_iota(jnp.int32, (rows, LANES), 1)


def features(entries, weighted):
    lin, diag, off = (0.25, 1.0 / 32.0, 1.0 / 16.0) if weighted else (1.0, 1.0, 1.0)
    rows = [entries * lin if weighted else entries]
    base = entries * off if weighted else entries
    rows.append(entries * entries * diag if weighted else entries * entries)
    for step in range(1, FEAT // 2):
        rolled = jnp.concatenate([entries[step:], entries[:step]], axis=0)
        rows.append(base * rolled)
    rows.append(base[: FEAT // 2] * entries[FEAT // 2 :])
    tail = lax.broadcasted_iota(jnp.int32, (8, entries.shape[1]), 0)
    rows.append(jnp.where(tail == 0, 1.0, 0.0).astype(F32))
    return jnp.concatenate(rows, axis=0).astype(BF16)


def convolve(taps, raw, before):
    lane = lanes(VDIM)
    one = jnp.where(lane < 1, pltpu.roll(before, 1, 1), pltpu.roll(raw, 1, 1))
    two = jnp.where(lane < 2, pltpu.roll(before, 2, 1), pltpu.roll(raw, 2, 1))
    return (taps[0] * raw + taps[1] * one + taps[2] * two).astype(BF16)


def fold(main, rest):
    both = rest[:HALF] + pltpu.roll(rest[HALF:], LANES // 2, 1)
    return jnp.concatenate([main, both], axis=0).astype(BF16)


def unfold(packed):
    wide = packed.astype(F32)
    both = wide[VDIM:STATE_ROWS]
    low = lanes(HALF) < LANES // 2
    upper = jnp.where(low, both, 0.0)
    lower = jnp.where(low, pltpu.roll(both, LANES // 2, 1), 0.0)
    return wide[:VDIM], jnp.concatenate([upper, lower], axis=0)


def edge_state(taps_ref, edges):
    lane = lanes(VDIM)
    values = jnp.zeros((VDIM, LANES), F32)
    keys = jnp.zeros((FEAT, LANES), F32)
    for index, (key_rest, tail_rest, counts) in enumerate(edges):
        at = 2 * index
        same = pltpu.roll(tail_rest, (LANES - EDGE + at) % LANES, 1)
        last = pltpu.roll(tail_rest, (LANES - EDGE - 1 + at) % LANES, 1)
        missing = jnp.where(lane == at, taps_ref[1] * last + taps_ref[2] * same, 0.0)
        missing = jnp.where(lane == at + 1, taps_ref[2] * same, missing)
        if counts is not None:
            missing = jnp.where(counts, missing, 0.0)
        values = values + missing
        moved = pltpu.roll(key_rest[:FEAT], (LANES - EDGE - 2 + at) % LANES, 1)
        place = lanes(FEAT)
        keys = keys + jnp.where((place >= at) & (place < at + 2), moved, 0.0)
    state = nt(values.astype(BF16), features(keys, True))
    blank = jnp.zeros((VDIM, LANES - EDGE), F32)
    return state[:, :LANES], jnp.concatenate([state[:, LANES:], blank], axis=1)


def joined(rest, tail_rest, key_rest):
    lane = lanes(VDIM)
    return jnp.where(lane < EDGE, rest, jnp.where(lane < EDGE + 2, tail_rest, key_rest))


def pack_kernel(head_ref, q_ref, k_ref, v_ref, w_ref, gain_ref, out_ref, taps_ref):
    out_ref[:, 0:FEAT, :] = q_ref[...].T.reshape(HEADS, FEAT, BLK)
    out_ref[:, FEAT : 2 * FEAT, :] = k_ref[...].T.reshape(HEADS, FEAT, BLK)
    out_ref[:, 2 * FEAT :, :] = v_ref[...].T.reshape(HEADS, VDIM, BLK)
    rows = jnp.concatenate([w_ref[...], gain_ref[...], jnp.zeros((4, HEADS * VDIM), F32)], axis=0)
    mine = jnp.zeros((8, VDIM), F32)
    for head in range(HEADS):
        mine = jnp.where(head_ref[0] == head, rows[:, head * VDIM : (head + 1) * VDIM], mine)
    columns = mine.T
    for index in range(TAPS + 1):
        taps_ref[index] = jnp.broadcast_to(columns[:, index : index + 1], (VDIM, LANES))


def state_kernel(x_ref, taps_ref, sent_ref, own_ref, conv_ref):
    count = x_ref.shape[0]
    taps = [taps_ref[index] for index in range(TAPS)]
    total = jnp.zeros((VDIM, NPHI), F32)
    before = jnp.zeros((VDIM, BLK), F32)
    for blk in range(count):
        raw = x_ref[blk, 2 * FEAT :, :].astype(F32)
        conv = convolve(taps, raw, before)
        conv_ref[blk] = conv
        phi = features(x_ref[blk, FEAT : 2 * FEAT, :].astype(F32), True)
        total = total + nt(conv, phi)
        before = raw
    lane = lanes(VDIM)
    blank = jnp.zeros((VDIM, LANES - EDGE), F32)
    rest = jnp.concatenate([total[:, LANES:], blank], axis=1)
    tail = pltpu.roll(before, EDGE + 2, 1)
    first = x_ref[0, FEAT : 2 * FEAT, :].astype(F32)
    first = jnp.concatenate([first, jnp.zeros((VDIM - FEAT, BLK), F32)], axis=0)
    first = jnp.where(lane < EDGE + 4, pltpu.roll(first, EDGE + 2, 1), 0.0)
    rest = joined(rest, tail, first)
    main = total[:, :LANES]
    own_ref[0] = main
    own_ref[1] = rest
    sent_ref[0:STATE_ROWS, :] = fold(main, rest)
    sent_ref[STATE_ROWS:, :] = x_ref[count - 1, FEAT:, :]


def inside_window(first):
    row = lax.broadcasted_iota(jnp.int32, (WIN + BLK, BLK), 0)
    lane = lax.broadcasted_iota(jnp.int32, (WIN + BLK, BLK), 1)
    inside = (row >= lane) & (row <= lane + WIN)
    return inside if first is None else inside & ((row >= WIN) | (first == 0))


def block_parts(query, key, value, before_key, before_value, inside):
    scores = tn(jnp.concatenate([before_key, key], axis=1), query) * 0.25
    own = scores[BLK:]
    key_row = lax.broadcasted_iota(jnp.int32, (BLK, BLK), 0)
    query_lane = lax.broadcasted_iota(jnp.int32, (BLK, BLK), 1)
    weights = 1.0 + own + 0.5 * own * own
    weights = jnp.where(key_row <= query_lane, weights, 0.0).astype(BF16)
    masked = jnp.where(inside, scores[BLK - WIN :], -1e30)
    row_max = jnp.max(masked, axis=0, keepdims=True)
    exp_scores = jnp.exp(masked - row_max)
    row_sum = jnp.sum(exp_scores, axis=0, keepdims=True)
    blank = jnp.zeros((BLK - WIN, BLK), BF16)
    probs = jnp.concatenate([blank, exp_scores.astype(BF16)], axis=0)
    window = nn(jnp.concatenate([before_value, value], axis=1), probs)
    return nn(value, weights), window / row_sum


def local_kernel(x_ref, conv_ref, num_ref, win_ref, phi_ref):
    count = x_ref.shape[0]
    inside = inside_window(None)
    state = jnp.zeros((VDIM, NPHI), F32)
    for blk in range(count):
        query = x_ref[blk, 0:FEAT, :]
        key = x_ref[blk, FEAT : 2 * FEAT, :]
        value = conv_ref[blk]
        phi_query = features(query.astype(F32), False)
        phi_ref[:, blk * BLK : (blk + 1) * BLK] = phi_query
        if blk > 0:
            own, win = block_parts(query, key, value, before_key, before_value, inside)
            num_ref[blk] = own + nn(state.astype(BF16), phi_query)
            win_ref[blk] = win
        if blk + 1 < count:
            state = state + nt(value, features(key.astype(F32), True))
        before_key, before_value = key, value


def merge_kernel(
    first_ref,
    own_ref,
    near_ref,
    taps_ref,
    x_ref,
    num_in_ref,
    win_in_ref,
    sent_ref,
    edge_ref,
    num_ref,
    win_ref,
):
    main, rest = own_ref[0], own_ref[1]
    near_main, near_rest = unfold(near_ref[0:STATE_ROWS, :])
    edge_main, edge_rest = edge_state(taps_ref, [(rest, near_rest, None)])
    edge_ref[0] = edge_main
    edge_ref[1] = edge_rest
    both = fold(main + near_main + edge_main, joined(rest + near_rest + edge_rest, rest, near_rest))
    for quad in range(sent_ref.shape[0]):
        sent_ref[quad] = both
    taps = [taps_ref[index] for index in range(TAPS)]
    raw = near_ref[STATE_ROWS + FEAT :, :].astype(F32)
    before_value = convolve(taps, raw, jnp.zeros((VDIM, BLK), F32))
    value = convolve(taps, x_ref[0, 2 * FEAT :, :].astype(F32), raw)
    num_ref[0], win_ref[0] = block_parts(
        x_ref[0, 0:FEAT, :],
        x_ref[0, FEAT : 2 * FEAT, :],
        value,
        near_ref[STATE_ROWS : STATE_ROWS + FEAT, :],
        before_value,
        inside_window(first_ref[0]),
    )


def late_kernel(quad_ref, others_ref, near_ref, taps_ref, *refs):
    quads = others_ref.shape[0]
    parts = [unfold(others_ref[quad]) for quad in range(quads)]
    main, rest = unfold(near_ref[0:STATE_ROWS, :])
    edges = []
    for quad in range(quads - 1):
        reached = quad < quad_ref[0]
        main = main + jnp.where(reached, parts[quad][0], 0.0)
        rest = rest + jnp.where(reached, parts[quad][1], 0.0)
        edges.append((parts[quad + 1][1], parts[quad][1], reached))
    edge_main, edge_rest = edge_state(taps_ref, edges)
    finish(main + edge_main, rest + edge_rest, taps_ref, *refs)


def early_kernel(near_ref, taps_ref, *refs):
    main, rest = unfold(near_ref[0:STATE_ROWS, :])
    finish(main, rest, taps_ref, *refs)


def finish(main, rest, taps_ref, edge_ref, num_ref, win_ref, phi_ref, out_ref):
    state = jnp.concatenate([main, rest[:, :EDGE]], axis=1)
    group_edge = jnp.concatenate([edge_ref[0], edge_ref[1][:, :EDGE]], axis=1)
    later = (state + group_edge).astype(BF16)
    state = state.astype(BF16)
    gain = taps_ref[TAPS]
    for blk in range(num_ref.shape[0]):
        phi = phi_ref[:, blk * BLK : (blk + 1) * BLK]
        num = num_ref[blk] + nn(state if blk == 0 else later, phi)
        mean_square = jnp.sum(num * num, axis=0, keepdims=True) * (1.0 / VDIM)
        linear = num * lax.rsqrt(mean_square + 1e-06) * gain
        out_ref[blk] = (linear + win_ref[blk]).astype(BF16)


def unpack_kernel(x_ref, out_ref):
    out_ref[...] = x_ref[...].reshape(HEADS * VDIM, BLK).T


SMEM = pl.BlockSpec(memory_space=pltpu.SMEM)
VMEM = pl.BlockSpec(memory_space=pltpu.VMEM)


def call(kernel, outs, scalars, outer_arrays, arrays, aliases=None):
    limit = None if outer_arrays else 8 * 1024 * 1024
    arrays = [pltpu.with_memory_space_constraint(array, pltpu.VMEM) for array in arrays]
    count = len(outer_arrays) + len(arrays)
    single = len(outs) == 1
    return pl.pallas_call(
        kernel,
        out_shape=outs[0] if single else tuple(outs),
        in_specs=[SMEM] * len(scalars) + [VMEM] * count,
        out_specs=VMEM if single else tuple(VMEM for _ in outs),
        input_output_aliases=aliases or {},
        compiler_params=pltpu.CompilerParams(vmem_limit_bytes=limit),
    )(*scalars, *outer_arrays, *arrays)


def scalar(value):
    return jnp.asarray(value).astype(jnp.int32).reshape(1)


def on_device(query_rows, key_rows, value_rows, conv_weight, norm_gain):
    group = ("pair", "core", "inner")
    stack = ("quad", "half")
    members = lax.axis_size(group)
    groups = lax.axis_size(stack)
    quads = lax.axis_size("quad")

    def upward(value):
        return lax.ppermute(value, stack, [(i, i + 1) for i in range(groups - 1)])

    packed, taps = call(
        pack_kernel,
        [pltpu.VMEM((HEADS, PART, BLK), BF16), pltpu.VMEM((TAPS + 1, VDIM, LANES), F32)],
        [scalar(lax.axis_index(group))],
        [query_rows, key_rows, value_rows, conv_weight, norm_gain.reshape(1, HEADS * VDIM)],
        [],
    )
    mine = lax.all_to_all(packed, group, 0, 0)
    sent, own, conv = call(
        state_kernel,
        [
            pltpu.VMEM((STATE_ROWS + FEAT + VDIM, BLK), BF16),
            pltpu.VMEM((2, VDIM, LANES), F32),
            pltpu.VMEM((members, VDIM, BLK), BF16),
        ],
        [],
        [],
        [mine, taps],
    )
    near = upward(sent)
    block = (VDIM, BLK)
    num, win, phi = call(
        local_kernel,
        [
            pltpu.VMEM((members, *block), F32),
            pltpu.VMEM((members, *block), F32),
            pltpu.VMEM((NPHI, members * BLK), BF16),
        ],
        [],
        [],
        [mine, conv],
    )
    sent, edge, num, win = call(
        merge_kernel,
        [
            pltpu.VMEM((quads, STATE_ROWS, LANES), BF16),
            pltpu.VMEM((2, VDIM, LANES), F32),
            pltpu.VMEM((members, *block), F32),
            pltpu.VMEM((members, *block), F32),
        ],
        [scalar(lax.axis_index(stack) == 0)],
        [],
        [own, near, taps, mine, num, win],
        {5: 2, 6: 3},
    )
    quad = lax.axis_index("quad")
    parts = [near, taps, edge, num, win, phi]

    def returned(kernel, scalars, arrays):
        done = call(kernel, [pltpu.VMEM((members, *block), BF16)], scalars, [], arrays)
        heads = lax.all_to_all(done, group, 0, 0)
        return call(unpack_kernel, [jax.ShapeDtypeStruct((BLK, HEADS * VDIM), BF16)], [], [], [heads])

    def early(sent):
        return sent, returned(early_kernel, [], parts)

    def nothing(sent):
        return sent, jnp.zeros((BLK, HEADS * VDIM), BF16)

    sent, out = lax.cond(quad == 0, early, nothing, sent)
    others = lax.all_to_all(sent, "quad", 0, 0)

    def late(out):
        return returned(late_kernel, [scalar(quad)], [others, *parts])

    return lax.cond(quad == 0, lambda out: out, late, out)


def solution(mesh):
    outer, inner = mesh.shape["outer"], mesh.shape["inner"]
    pair = HEADS // inner // 2
    shape = (mesh.shape["dp"], outer // (2 * 2 * pair), 2, pair, 2, inner)
    split = Mesh(
        np.asarray(mesh.devices).reshape(shape), ("dp", "quad", "half", "pair", "core", "inner")
    )
    rows = P(("dp", "quad", "half", "pair", "core", "inner"), None)
    return jax.shard_map(
        on_device,
        mesh=split,
        in_specs=(rows, rows, rows, P(), P()),
        out_specs=rows,
        check_vma=False,
    )
```

```python
import jax
import jax.numpy as jnp
import numpy as np
from jax import lax
from jax.experimental import pallas as pl
from jax.experimental.pallas import tpu as pltpu
from jax.sharding import Mesh, PartitionSpec as P

HEADS = 16
FEAT = 16
VDIM = 64
TAPS = 3
WIN = 64
BLK = 128
NPHI = 160
LANES = 128
EDGE = NPHI - LANES
HALF = VDIM // 2
STATE_ROWS = VDIM + HALF
PART = FEAT + FEAT + VDIM
F32 = jnp.float32
BF16 = jnp.bfloat16


def nt(lhs, rhs):
    return lax.dot_general(lhs, rhs, (((1,), (1,)), ((), ())), preferred_element_type=F32)


def tn(lhs, rhs):
    return lax.dot_general(lhs, rhs, (((0,), (0,)), ((), ())), preferred_element_type=F32)


def nn(lhs, rhs):
    return lax.dot_general(lhs, rhs, (((1,), (0,)), ((), ())), preferred_element_type=F32)


def lanes(rows):
    return lax.broadcasted_iota(jnp.int32, (rows, LANES), 1)


def features(entries, weighted):
    lin, diag, off = (0.25, 1.0 / 32.0, 1.0 / 16.0) if weighted else (1.0, 1.0, 1.0)
    rows = [entries * lin if weighted else entries]
    base = entries * off if weighted else entries
    rows.append(entries * entries * diag if weighted else entries * entries)
    for step in range(1, FEAT // 2):
        rolled = jnp.concatenate([entries[step:], entries[:step]], axis=0)
        rows.append(base * rolled)
    rows.append(base[: FEAT // 2] * entries[FEAT // 2 :])
    tail = lax.broadcasted_iota(jnp.int32, (8, entries.shape[1]), 0)
    rows.append(jnp.where(tail == 0, 1.0, 0.0).astype(F32))
    return jnp.concatenate(rows, axis=0).astype(BF16)


def convolve(taps, raw, before):
    lane = lanes(VDIM)
    one = jnp.where(lane < 1, pltpu.roll(before, 1, 1), pltpu.roll(raw, 1, 1))
    two = jnp.where(lane < 2, pltpu.roll(before, 2, 1), pltpu.roll(raw, 2, 1))
    return (taps[0] * raw + taps[1] * one + taps[2] * two).astype(BF16)


def fold(main, rest):
    both = rest[:HALF] + pltpu.roll(rest[HALF:], LANES // 2, 1)
    return jnp.concatenate([main, both], axis=0).astype(BF16)


def unfold(packed):
    wide = packed.astype(F32)
    both = wide[VDIM:STATE_ROWS]
    low = lanes(HALF) < LANES // 2
    upper = jnp.where(low, both, 0.0)
    lower = jnp.where(low, pltpu.roll(both, LANES // 2, 1), 0.0)
    return wide[:VDIM], jnp.concatenate([upper, lower], axis=0)


def edge_state(taps_ref, edges):
    lane = lanes(VDIM)
    values = jnp.zeros((VDIM, LANES), F32)
    keys = jnp.zeros((FEAT, LANES), F32)
    for index, (key_rest, tail_rest) in enumerate(edges):
        at = 2 * index
        same = pltpu.roll(tail_rest, (LANES - EDGE + at) % LANES, 1)
        last = pltpu.roll(tail_rest, (LANES - EDGE - 1 + at) % LANES, 1)
        missing = jnp.where(lane == at, taps_ref[1] * last + taps_ref[2] * same, 0.0)
        missing = jnp.where(lane == at + 1, taps_ref[2] * same, missing)
        values = values + missing
        moved = pltpu.roll(key_rest[:FEAT], (LANES - EDGE - 2 + at) % LANES, 1)
        place = lanes(FEAT)
        keys = keys + jnp.where((place >= at) & (place < at + 2), moved, 0.0)
    state = nt(values.astype(BF16), features(keys, True))
    blank = jnp.zeros((VDIM, LANES - EDGE), F32)
    return state[:, :LANES], jnp.concatenate([state[:, LANES:], blank], axis=1)


def joined(rest, tail_rest, key_rest):
    lane = lanes(VDIM)
    return jnp.where(lane < EDGE, rest, jnp.where(lane < EDGE + 2, tail_rest, key_rest))


def pack_kernel(head_ref, q_ref, k_ref, v_ref, w_ref, gain_ref, out_ref, taps_ref):
    out_ref[:, 0:FEAT, :] = q_ref[...].T.reshape(HEADS, FEAT, BLK)
    out_ref[:, FEAT : 2 * FEAT, :] = k_ref[...].T.reshape(HEADS, FEAT, BLK)
    out_ref[:, 2 * FEAT :, :] = v_ref[...].T.reshape(HEADS, VDIM, BLK)
    rows = jnp.concatenate([w_ref[...], gain_ref[...], jnp.zeros((4, HEADS * VDIM), F32)], axis=0)
    mine = jnp.zeros((8, VDIM), F32)
    for head in range(HEADS):
        mine = jnp.where(head_ref[0] == head, rows[:, head * VDIM : (head + 1) * VDIM], mine)
    columns = mine.T
    for index in range(TAPS + 1):
        taps_ref[index] = jnp.broadcast_to(columns[:, index : index + 1], (VDIM, LANES))


def state_kernel(x_ref, taps_ref, sent_ref, own_ref, conv_ref):
    count = x_ref.shape[0]
    taps = [taps_ref[index] for index in range(TAPS)]
    total = jnp.zeros((VDIM, NPHI), F32)
    before = jnp.zeros((VDIM, BLK), F32)
    for blk in range(count):
        raw = x_ref[blk, 2 * FEAT :, :].astype(F32)
        conv = convolve(taps, raw, before)
        conv_ref[blk] = conv
        phi = features(x_ref[blk, FEAT : 2 * FEAT, :].astype(F32), True)
        total = total + nt(conv, phi)
        before = raw
    lane = lanes(VDIM)
    blank = jnp.zeros((VDIM, LANES - EDGE), F32)
    rest = jnp.concatenate([total[:, LANES:], blank], axis=1)
    tail = pltpu.roll(before, EDGE + 2, 1)
    first = x_ref[0, FEAT : 2 * FEAT, :].astype(F32)
    first = jnp.concatenate([first, jnp.zeros((VDIM - FEAT, BLK), F32)], axis=0)
    first = jnp.where(lane < EDGE + 4, pltpu.roll(first, EDGE + 2, 1), 0.0)
    rest = joined(rest, tail, first)
    main = total[:, :LANES]
    own_ref[0] = main
    own_ref[1] = rest
    sent_ref[0:STATE_ROWS, :] = fold(main, rest)
    sent_ref[STATE_ROWS:, :] = x_ref[count - 1, FEAT:, :]


def inside_window(first):
    row = lax.broadcasted_iota(jnp.int32, (WIN + BLK, BLK), 0)
    lane = lax.broadcasted_iota(jnp.int32, (WIN + BLK, BLK), 1)
    inside = (row >= lane) & (row <= lane + WIN)
    return inside if first is None else inside & ((row >= WIN) | (first == 0))


def block_parts(query, key, value, before_key, before_value, inside):
    scores = tn(jnp.concatenate([before_key, key], axis=1), query) * 0.25
    own = scores[BLK:]
    key_row = lax.broadcasted_iota(jnp.int32, (BLK, BLK), 0)
    query_lane = lax.broadcasted_iota(jnp.int32, (BLK, BLK), 1)
    weights = 1.0 + own + 0.5 * own * own
    weights = jnp.where(key_row <= query_lane, weights, 0.0).astype(BF16)
    masked = jnp.where(inside, scores[BLK - WIN :], -1e30)
    row_max = jnp.max(masked, axis=0, keepdims=True)
    exp_scores = jnp.exp(masked - row_max)
    row_sum = jnp.sum(exp_scores, axis=0, keepdims=True)
    blank = jnp.zeros((BLK - WIN, BLK), BF16)
    probs = jnp.concatenate([blank, exp_scores.astype(BF16)], axis=0)
    window = nn(jnp.concatenate([before_value, value], axis=1), probs)
    return nn(value, weights), window / row_sum


def local_kernel(x_ref, conv_ref, num_ref, win_ref, phi_ref):
    count = x_ref.shape[0]
    inside = inside_window(None)
    state = jnp.zeros((VDIM, NPHI), F32)
    for blk in range(count):
        query = x_ref[blk, 0:FEAT, :]
        key = x_ref[blk, FEAT : 2 * FEAT, :]
        value = conv_ref[blk]
        phi_query = features(query.astype(F32), False)
        phi_ref[:, blk * BLK : (blk + 1) * BLK] = phi_query
        if blk > 0:
            own, win = block_parts(query, key, value, before_key, before_value, inside)
            num_ref[blk] = own + nn(state.astype(BF16), phi_query)
            win_ref[blk] = win
        if blk + 1 < count:
            state = state + nt(value, features(key.astype(F32), True))
        before_key, before_value = key, value


def merge_kernel(
    first_ref,
    own_ref,
    near_ref,
    taps_ref,
    x_ref,
    num_in_ref,
    win_in_ref,
    sent_ref,
    pair_ref,
    edge_ref,
    num_ref,
    win_ref,
):
    main, rest = own_ref[0], own_ref[1]
    near_main, near_rest = unfold(near_ref[0:STATE_ROWS, :])
    edge_main, edge_rest = edge_state(taps_ref, [(rest, near_rest)])
    edge_ref[0] = edge_main
    edge_ref[1] = edge_rest
    main = main + near_main + edge_main
    rest = joined(rest + near_rest + edge_rest, rest, near_rest)
    pair_ref[0] = main
    pair_ref[1] = rest
    sent_ref[...] = fold(main, rest)
    taps = [taps_ref[index] for index in range(TAPS)]
    raw = near_ref[STATE_ROWS + FEAT :, :].astype(F32)
    before_value = convolve(taps, raw, jnp.zeros((VDIM, BLK), F32))
    value = convolve(taps, x_ref[0, 2 * FEAT :, :].astype(F32), raw)
    num_ref[0], win_ref[0] = block_parts(
        x_ref[0, 0:FEAT, :],
        x_ref[0, FEAT : 2 * FEAT, :],
        value,
        near_ref[STATE_ROWS : STATE_ROWS + FEAT, :],
        before_value,
        inside_window(first_ref[0]),
    )


def join_kernel(quad_ref, pair_ref, recv_ref, taps_ref, sent_ref):
    lowest = quad_ref[0] == 0
    main, rest = pair_ref[0], pair_ref[1]
    recv_main, recv_rest = unfold(recv_ref[...])
    lower = jnp.where(lowest, rest, recv_rest)
    upper = jnp.where(lowest, recv_rest, rest)
    edge_main, edge_rest = edge_state(taps_ref, [(upper, lower)])
    sent_ref[...] = fold(
        main + recv_main + edge_main, joined(rest + recv_rest + edge_rest, upper, lower)
    )


def late_kernel(quad_ref, pair_recv_ref, below_ref, low_ref, near_ref, taps_ref, *refs):
    second = quad_ref[0] == 1
    near_main, near_rest = unfold(near_ref[0:STATE_ROWS, :])
    one_main, one_rest = unfold(pair_recv_ref[...])
    two_main, two_rest = unfold(below_ref[...])
    below_main = jnp.where(second, one_main, two_main)
    below_rest = jnp.where(second, one_rest, two_rest)
    low_main, low_rest = unfold(low_ref[...])
    above_low = jnp.where(quad_ref[0] == 2, near_rest, below_rest)
    edge_main, edge_rest = edge_state(taps_ref, [(near_rest, below_rest), (above_low, low_rest)])
    main = near_main + below_main + low_main + edge_main
    finish(main, near_rest + below_rest + low_rest + edge_rest, taps_ref, *refs)


def early_kernel(near_ref, taps_ref, *refs):
    main, rest = unfold(near_ref[0:STATE_ROWS, :])
    finish(main, rest, taps_ref, *refs)


def finish(main, rest, taps_ref, edge_ref, num_ref, win_ref, phi_ref, out_ref):
    state = jnp.concatenate([main, rest[:, :EDGE]], axis=1)
    group_edge = jnp.concatenate([edge_ref[0], edge_ref[1][:, :EDGE]], axis=1)
    later = (state + group_edge).astype(BF16)
    state = state.astype(BF16)
    gain = taps_ref[TAPS]
    for blk in range(num_ref.shape[0]):
        phi = phi_ref[:, blk * BLK : (blk + 1) * BLK]
        num = num_ref[blk] + nn(state if blk == 0 else later, phi)
        mean_square = jnp.sum(num * num, axis=0, keepdims=True) * (1.0 / VDIM)
        linear = num * lax.rsqrt(mean_square + 1e-06) * gain
        out_ref[blk] = (linear + win_ref[blk]).astype(BF16)


def unpack_kernel(x_ref, out_ref):
    out_ref[...] = x_ref[...].reshape(HEADS * VDIM, BLK).T


SMEM = pl.BlockSpec(memory_space=pltpu.SMEM)
VMEM = pl.BlockSpec(memory_space=pltpu.VMEM)


def call(kernel, outs, scalars, outer_arrays, arrays, aliases=None):
    limit = None if outer_arrays else 8 * 1024 * 1024
    arrays = [pltpu.with_memory_space_constraint(array, pltpu.VMEM) for array in arrays]
    count = len(outer_arrays) + len(arrays)
    single = len(outs) == 1
    return pl.pallas_call(
        kernel,
        out_shape=outs[0] if single else tuple(outs),
        in_specs=[SMEM] * len(scalars) + [VMEM] * count,
        out_specs=VMEM if single else tuple(VMEM for _ in outs),
        input_output_aliases=aliases or {},
        compiler_params=pltpu.CompilerParams(vmem_limit_bytes=limit),
    )(*scalars, *outer_arrays, *arrays)


def scalar(value):
    return jnp.asarray(value).astype(jnp.int32).reshape(1)


def on_device(query_rows, key_rows, value_rows, conv_weight, norm_gain):
    group = ("pair", "core", "inner")
    stack = ("quad", "half")
    members = lax.axis_size(group)
    groups = lax.axis_size(stack)

    def upward(value):
        return lax.ppermute(value, stack, [(i, i + 1) for i in range(groups - 1)])

    packed, taps = call(
        pack_kernel,
        [pltpu.VMEM((HEADS, PART, BLK), BF16), pltpu.VMEM((TAPS + 1, VDIM, LANES), F32)],
        [scalar(lax.axis_index(group))],
        [query_rows, key_rows, value_rows, conv_weight, norm_gain.reshape(1, HEADS * VDIM)],
        [],
    )
    mine = lax.all_to_all(packed, group, 0, 0)
    sent, own, conv = call(
        state_kernel,
        [
            pltpu.VMEM((STATE_ROWS + FEAT + VDIM, BLK), BF16),
            pltpu.VMEM((2, VDIM, LANES), F32),
            pltpu.VMEM((members, VDIM, BLK), BF16),
        ],
        [],
        [],
        [mine, taps],
    )
    near = upward(sent)
    block = (VDIM, BLK)
    num, win, phi = call(
        local_kernel,
        [
            pltpu.VMEM((members, *block), F32),
            pltpu.VMEM((members, *block), F32),
            pltpu.VMEM((NPHI, members * BLK), BF16),
        ],
        [],
        [],
        [mine, conv],
    )
    sent, pair, edge, num, win = call(
        merge_kernel,
        [
            pltpu.VMEM((STATE_ROWS, LANES), BF16),
            pltpu.VMEM((2, VDIM, LANES), F32),
            pltpu.VMEM((2, VDIM, LANES), F32),
            pltpu.VMEM((members, *block), F32),
            pltpu.VMEM((members, *block), F32),
        ],
        [scalar(lax.axis_index(stack) == 0)],
        [],
        [own, near, taps, mine, num, win],
        {5: 3, 6: 4},
    )
    quad = lax.axis_index("quad")
    parts = [near, taps, edge, num, win, phi]

    def returned(kernel, scalars, arrays):
        done = call(kernel, [pltpu.VMEM((members, *block), BF16)], scalars, [], arrays)
        return lax.all_to_all(done, group, 0, 0)

    heads = lax.cond(
        quad == 0,
        lambda: returned(early_kernel, [], parts),
        lambda: jnp.zeros((HEADS, *block), BF16),
    )
    below = lax.ppermute(sent, "quad", [(2, 3)])

    def lower_pair(sent):
        recv = lax.ppermute(sent, "quad", [(0, 1), (1, 0)])
        both = call(
            join_kernel,
            [pltpu.VMEM((STATE_ROWS, LANES), BF16)],
            [scalar(quad)],
            [],
            [pair, recv, taps],
        )
        return both, recv

    ready, heads = lax.optimization_barrier((sent, heads))
    both, pair_recv = lax.cond(quad < 2, lower_pair, lambda sent: (sent, sent), ready)
    low = lax.ppermute(both, "quad", [(0, 2), (1, 3)])
    heads = lax.cond(
        quad == 0,
        lambda heads: heads,
        lambda heads: returned(late_kernel, [scalar(quad)], [pair_recv, below, low, *parts]),
        heads,
    )
    out = jax.ShapeDtypeStruct((BLK, HEADS * VDIM), BF16)
    return call(unpack_kernel, [out], [], [], [heads])


def solution(mesh):
    outer, inner = mesh.shape["outer"], mesh.shape["inner"]
    pair = HEADS // inner // 2
    shape = (mesh.shape["dp"], outer // (2 * 2 * pair), 2, pair, 2, inner)
    split = Mesh(
        np.asarray(mesh.devices).reshape(shape), ("dp", "quad", "half", "pair", "core", "inner")
    )
    rows = P(("dp", "quad", "half", "pair", "core", "inner"), None)
    return jax.shard_map(
        on_device,
        mesh=split,
        in_specs=(rows, rows, rows, P(), P()),
        out_specs=rows,
        check_vma=False,
    )
```

```python
import jax
import jax.numpy as jnp
import numpy as np
from jax import lax
from jax.experimental import pallas as pl
from jax.experimental.pallas import tpu as pltpu
from jax.sharding import Mesh, PartitionSpec as P

HEADS = 16
FEAT = 16
VDIM = 64
TAPS = 3
WIN = 64
BLK = 128
NPHI = 160
LANES = 128
EDGE = NPHI - LANES
HALF = VDIM // 2
STATE_ROWS = VDIM + HALF
PART = FEAT + FEAT + VDIM
F32 = jnp.float32
BF16 = jnp.bfloat16


def nt(lhs, rhs):
    return lax.dot_general(lhs, rhs, (((1,), (1,)), ((), ())), preferred_element_type=F32)


def tn(lhs, rhs):
    return lax.dot_general(lhs, rhs, (((0,), (0,)), ((), ())), preferred_element_type=F32)


def nn(lhs, rhs):
    return lax.dot_general(lhs, rhs, (((1,), (0,)), ((), ())), preferred_element_type=F32)


def lanes(rows):
    return lax.broadcasted_iota(jnp.int32, (rows, LANES), 1)


def features(entries, weighted):
    lin, diag, off = (0.25, 1.0 / 32.0, 1.0 / 16.0) if weighted else (1.0, 1.0, 1.0)
    rows = [entries * lin if weighted else entries]
    base = entries * off if weighted else entries
    rows.append(entries * entries * diag if weighted else entries * entries)
    for step in range(1, FEAT // 2):
        rolled = jnp.concatenate([entries[step:], entries[:step]], axis=0)
        rows.append(base * rolled)
    rows.append(base[: FEAT // 2] * entries[FEAT // 2 :])
    tail = lax.broadcasted_iota(jnp.int32, (8, entries.shape[1]), 0)
    rows.append(jnp.where(tail == 0, 1.0, 0.0).astype(F32))
    return jnp.concatenate(rows, axis=0).astype(BF16)


def convolve(taps, raw, before):
    lane = lanes(VDIM)
    one = jnp.where(lane < 1, pltpu.roll(before, 1, 1), pltpu.roll(raw, 1, 1))
    two = jnp.where(lane < 2, pltpu.roll(before, 2, 1), pltpu.roll(raw, 2, 1))
    return (taps[0] * raw + taps[1] * one + taps[2] * two).astype(BF16)


def fold(main, rest):
    both = rest[:HALF] + pltpu.roll(rest[HALF:], LANES // 2, 1)
    return jnp.concatenate([main, both], axis=0).astype(BF16)


def unfold(packed):
    wide = packed.astype(F32)
    both = wide[VDIM:STATE_ROWS]
    low = lanes(HALF) < LANES // 2
    upper = jnp.where(low, both, 0.0)
    lower = jnp.where(low, pltpu.roll(both, LANES // 2, 1), 0.0)
    return wide[:VDIM], jnp.concatenate([upper, lower], axis=0)


def edge_state(taps_ref, edges):
    lane = lanes(VDIM)
    values = jnp.zeros((VDIM, LANES), F32)
    keys = jnp.zeros((FEAT, LANES), F32)
    for index, (key_rest, tail_rest) in enumerate(edges):
        at = 2 * index
        same = pltpu.roll(tail_rest, (LANES - EDGE + at) % LANES, 1)
        last = pltpu.roll(tail_rest, (LANES - EDGE - 1 + at) % LANES, 1)
        missing = jnp.where(lane == at, taps_ref[1] * last + taps_ref[2] * same, 0.0)
        missing = jnp.where(lane == at + 1, taps_ref[2] * same, missing)
        values = values + missing
        moved = pltpu.roll(key_rest[:FEAT], (LANES - EDGE - 2 + at) % LANES, 1)
        place = lanes(FEAT)
        keys = keys + jnp.where((place >= at) & (place < at + 2), moved, 0.0)
    state = nt(values.astype(BF16), features(keys, True))
    blank = jnp.zeros((VDIM, LANES - EDGE), F32)
    return state[:, :LANES], jnp.concatenate([state[:, LANES:], blank], axis=1)


def joined(rest, tail_rest, key_rest):
    lane = lanes(VDIM)
    return jnp.where(lane < EDGE, rest, jnp.where(lane < EDGE + 2, tail_rest, key_rest))


def pack_kernel(head_ref, q_ref, k_ref, v_ref, w_ref, gain_ref, out_ref, taps_ref):
    out_ref[:, 0:FEAT, :] = q_ref[...].T.reshape(HEADS, FEAT, BLK)
    out_ref[:, FEAT : 2 * FEAT, :] = k_ref[...].T.reshape(HEADS, FEAT, BLK)
    out_ref[:, 2 * FEAT :, :] = v_ref[...].T.reshape(HEADS, VDIM, BLK)
    rows = jnp.concatenate([w_ref[...], gain_ref[...], jnp.zeros((4, HEADS * VDIM), F32)], axis=0)
    mine = jnp.zeros((8, VDIM), F32)
    for head in range(HEADS):
        mine = jnp.where(head_ref[0] == head, rows[:, head * VDIM : (head + 1) * VDIM], mine)
    columns = mine.T
    for index in range(TAPS + 1):
        taps_ref[index] = jnp.broadcast_to(columns[:, index : index + 1], (VDIM, LANES))


def state_kernel(x_ref, taps_ref, sent_ref, own_ref, conv_ref):
    count = x_ref.shape[0]
    taps = [taps_ref[index] for index in range(TAPS)]
    total = jnp.zeros((VDIM, NPHI), F32)
    before = jnp.zeros((VDIM, BLK), F32)
    for blk in range(count):
        raw = x_ref[blk, 2 * FEAT :, :].astype(F32)
        conv = convolve(taps, raw, before)
        conv_ref[blk] = conv
        phi = features(x_ref[blk, FEAT : 2 * FEAT, :].astype(F32), True)
        total = total + nt(conv, phi)
        before = raw
    lane = lanes(VDIM)
    blank = jnp.zeros((VDIM, LANES - EDGE), F32)
    rest = jnp.concatenate([total[:, LANES:], blank], axis=1)
    tail = pltpu.roll(before, EDGE + 2, 1)
    first = x_ref[0, FEAT : 2 * FEAT, :].astype(F32)
    first = jnp.concatenate([first, jnp.zeros((VDIM - FEAT, BLK), F32)], axis=0)
    first = jnp.where(lane < EDGE + 4, pltpu.roll(first, EDGE + 2, 1), 0.0)
    rest = joined(rest, tail, first)
    main = total[:, :LANES]
    own_ref[0] = main
    own_ref[1] = rest
    sent_ref[0:STATE_ROWS, :] = fold(main, rest)
    sent_ref[STATE_ROWS:, :] = x_ref[count - 1, FEAT:, :]


def inside_window(first):
    row = lax.broadcasted_iota(jnp.int32, (WIN + BLK, BLK), 0)
    lane = lax.broadcasted_iota(jnp.int32, (WIN + BLK, BLK), 1)
    inside = (row >= lane) & (row <= lane + WIN)
    return inside if first is None else inside & ((row >= WIN) | (first == 0))


def block_parts(query, key, value, before_key, before_value, inside):
    scores = tn(jnp.concatenate([before_key, key], axis=1), query) * 0.25
    own = scores[BLK:]
    key_row = lax.broadcasted_iota(jnp.int32, (BLK, BLK), 0)
    query_lane = lax.broadcasted_iota(jnp.int32, (BLK, BLK), 1)
    weights = 1.0 + own + 0.5 * own * own
    weights = jnp.where(key_row <= query_lane, weights, 0.0).astype(BF16)
    masked = jnp.where(inside, scores[BLK - WIN :], -1e30)
    row_max = jnp.max(masked, axis=0, keepdims=True)
    exp_scores = jnp.exp(masked - row_max)
    row_sum = jnp.sum(exp_scores, axis=0, keepdims=True)
    blank = jnp.zeros((BLK - WIN, BLK), BF16)
    probs = jnp.concatenate([blank, exp_scores.astype(BF16)], axis=0)
    window = nn(jnp.concatenate([before_value, value], axis=1), probs)
    return nn(value, weights), window / row_sum


def local_kernel(x_ref, conv_ref, num_ref, win_ref, phi_ref):
    count = x_ref.shape[0]
    inside = inside_window(None)
    state = jnp.zeros((VDIM, NPHI), F32)
    for blk in range(count):
        query = x_ref[blk, 0:FEAT, :]
        key = x_ref[blk, FEAT : 2 * FEAT, :]
        value = conv_ref[blk]
        phi_query = features(query.astype(F32), False)
        phi_ref[:, blk * BLK : (blk + 1) * BLK] = phi_query
        if blk > 0:
            own, win = block_parts(query, key, value, before_key, before_value, inside)
            num_ref[blk] = own + nn(state.astype(BF16), phi_query)
            win_ref[blk] = win
        if blk + 1 < count:
            state = state + nt(value, features(key.astype(F32), True))
        before_key, before_value = key, value


def merge_kernel(
    first_ref,
    own_ref,
    near_ref,
    taps_ref,
    x_ref,
    num_in_ref,
    win_in_ref,
    sent_ref,
    pair_ref,
    edge_ref,
    num_ref,
    win_ref,
):
    main, rest = own_ref[0], own_ref[1]
    near_main, near_rest = unfold(near_ref[0:STATE_ROWS, :])
    edge_main, edge_rest = edge_state(taps_ref, [(rest, near_rest)])
    edge_ref[0] = edge_main
    edge_ref[1] = edge_rest
    main = main + near_main + edge_main
    rest = joined(rest + near_rest + edge_rest, rest, near_rest)
    pair_ref[0] = main
    pair_ref[1] = rest
    sent_ref[...] = fold(main, rest)
    taps = [taps_ref[index] for index in range(TAPS)]
    raw = near_ref[STATE_ROWS + FEAT :, :].astype(F32)
    before_value = convolve(taps, raw, jnp.zeros((VDIM, BLK), F32))
    value = convolve(taps, x_ref[0, 2 * FEAT :, :].astype(F32), raw)
    num_ref[0], win_ref[0] = block_parts(
        x_ref[0, 0:FEAT, :],
        x_ref[0, FEAT : 2 * FEAT, :],
        value,
        near_ref[STATE_ROWS : STATE_ROWS + FEAT, :],
        before_value,
        inside_window(first_ref[0]),
    )


def join_kernel(quad_ref, pair_ref, recv_ref, taps_ref, sent_ref, copy_ref):
    copy_ref[...] = recv_ref[...]
    lowest = quad_ref[0] == 0
    main, rest = pair_ref[0], pair_ref[1]
    recv_main, recv_rest = unfold(recv_ref[...])
    lower = jnp.where(lowest, rest, recv_rest)
    upper = jnp.where(lowest, recv_rest, rest)
    edge_main, edge_rest = edge_state(taps_ref, [(upper, lower)])
    sent_ref[...] = fold(
        main + recv_main + edge_main, joined(rest + recv_rest + edge_rest, upper, lower)
    )


def final_kernel(
    quad_ref,
    pair_recv_ref,
    below_ref,
    low_ref,
    near_ref,
    taps_ref,
    edge_ref,
    num_ref,
    win_ref,
    phi_ref,
    out_ref,
):
    second = quad_ref[0] == 1
    near_main, near_rest = unfold(near_ref[0:STATE_ROWS, :])
    one_main, one_rest = unfold(pair_recv_ref[...])
    two_main, two_rest = unfold(below_ref[...])
    below_main = jnp.where(second, one_main, two_main)
    below_rest = jnp.where(second, one_rest, two_rest)
    low_main, low_rest = unfold(low_ref[...])
    above_low = jnp.where(quad_ref[0] == 2, near_rest, below_rest)
    edge_main, edge_rest = edge_state(taps_ref, [(near_rest, below_rest), (above_low, low_rest)])
    main = near_main + below_main + low_main + edge_main
    rest = near_rest + below_rest + low_rest + edge_rest
    state = jnp.concatenate([main, rest[:, :EDGE]], axis=1)
    group_edge = jnp.concatenate([edge_ref[0], edge_ref[1][:, :EDGE]], axis=1)
    later = (state + group_edge).astype(BF16)
    state = state.astype(BF16)
    gain = taps_ref[TAPS]
    for blk in range(num_ref.shape[0]):
        phi = phi_ref[:, blk * BLK : (blk + 1) * BLK]
        num = num_ref[blk] + nn(state if blk == 0 else later, phi)
        mean_square = jnp.sum(num * num, axis=0, keepdims=True) * (1.0 / VDIM)
        linear = num * lax.rsqrt(mean_square + 1e-06) * gain
        out_ref[blk] = (linear + win_ref[blk]).astype(BF16)


def unpack_kernel(x_ref, out_ref):
    out_ref[...] = x_ref[...].reshape(HEADS * VDIM, BLK).T


SMEM = pl.BlockSpec(memory_space=pltpu.SMEM)
VMEM = pl.BlockSpec(memory_space=pltpu.VMEM)


def call(kernel, outs, scalars, outer_arrays, arrays, aliases=None):
    limit = None if outer_arrays else 8 * 1024 * 1024
    arrays = [pltpu.with_memory_space_constraint(array, pltpu.VMEM) for array in arrays]
    count = len(outer_arrays) + len(arrays)
    single = len(outs) == 1
    return pl.pallas_call(
        kernel,
        out_shape=outs[0] if single else tuple(outs),
        in_specs=[SMEM] * len(scalars) + [VMEM] * count,
        out_specs=VMEM if single else tuple(VMEM for _ in outs),
        input_output_aliases=aliases or {},
        compiler_params=pltpu.CompilerParams(vmem_limit_bytes=limit),
    )(*scalars, *outer_arrays, *arrays)


def scalar(value):
    return jnp.asarray(value).astype(jnp.int32).reshape(1)


def on_device(query_rows, key_rows, value_rows, conv_weight, norm_gain):
    group = ("pair", "core", "inner")
    stack = ("quad", "half")
    members = lax.axis_size(group)
    groups = lax.axis_size(stack)

    def upward(value):
        return lax.ppermute(value, stack, [(i, i + 1) for i in range(groups - 1)])

    packed, taps = call(
        pack_kernel,
        [pltpu.VMEM((HEADS, PART, BLK), BF16), pltpu.VMEM((TAPS + 1, VDIM, LANES), F32)],
        [scalar(lax.axis_index(group))],
        [query_rows, key_rows, value_rows, conv_weight, norm_gain.reshape(1, HEADS * VDIM)],
        [],
    )
    mine = lax.all_to_all(packed, group, 0, 0)
    sent, own, conv = call(
        state_kernel,
        [
            pltpu.VMEM((STATE_ROWS + FEAT + VDIM, BLK), BF16),
            pltpu.VMEM((2, VDIM, LANES), F32),
            pltpu.VMEM((members, VDIM, BLK), BF16),
        ],
        [],
        [],
        [mine, taps],
    )
    near = upward(sent)
    block = (VDIM, BLK)
    num, win, phi = call(
        local_kernel,
        [
            pltpu.VMEM((members, *block), F32),
            pltpu.VMEM((members, *block), F32),
            pltpu.VMEM((NPHI, members * BLK), BF16),
        ],
        [],
        [],
        [mine, conv],
    )
    sent, pair, edge, num, win = call(
        merge_kernel,
        [
            pltpu.VMEM((STATE_ROWS, LANES), BF16),
            pltpu.VMEM((2, VDIM, LANES), F32),
            pltpu.VMEM((2, VDIM, LANES), F32),
            pltpu.VMEM((members, *block), F32),
            pltpu.VMEM((members, *block), F32),
        ],
        [scalar(lax.axis_index(stack) == 0)],
        [],
        [own, near, taps, mine, num, win],
        {5: 3, 6: 4},
    )
    quad = lax.axis_index("quad")

    below = lax.ppermute(sent, "quad", [(2, 3)])

    def lower_pair(sent):
        recv = lax.ppermute(sent, "quad", [(0, 1), (1, 0)])
        return call(
            join_kernel,
            [pltpu.VMEM((STATE_ROWS, LANES), BF16), pltpu.VMEM((STATE_ROWS, LANES), BF16)],
            [scalar(quad)],
            [],
            [pair, recv, taps],
        )

    both, pair_recv = lax.cond(quad < 2, lower_pair, lambda sent: (sent, sent), sent)
    low = lax.ppermute(both, "quad", [(0, 2), (1, 3)])
    done = call(
        final_kernel,
        [pltpu.VMEM((members, *block), BF16)],
        [scalar(quad)],
        [],
        [pair_recv, below, low, near, taps, edge, num, win, phi],
    )
    heads = lax.all_to_all(done, group, 0, 0)
    out = jax.ShapeDtypeStruct((BLK, HEADS * VDIM), BF16)
    return call(unpack_kernel, [out], [], [], [heads])


def solution(mesh):
    outer, inner = mesh.shape["outer"], mesh.shape["inner"]
    pair = HEADS // inner // 2
    shape = (mesh.shape["dp"], outer // (2 * 2 * pair), 2, pair, 2, inner)
    split = Mesh(
        np.asarray(mesh.devices).reshape(shape), ("dp", "quad", "half", "pair", "core", "inner")
    )
    rows = P(("dp", "quad", "half", "pair", "core", "inner"), None)
    return jax.shard_map(
        on_device,
        mesh=split,
        in_specs=(rows, rows, rows, P(), P()),
        out_specs=rows,
        check_vma=False,
    )
```

```python
import jax
import jax.numpy as jnp
import numpy as np
from jax import lax
from jax.experimental import pallas as pl
from jax.experimental.pallas import tpu as pltpu
from jax.sharding import Mesh, PartitionSpec as P

HEADS = 16
FEAT = 16
VDIM = 64
TAPS = 3
WIN = 64
BLK = 128
NPHI = 160
LANES = 128
EDGE = NPHI - LANES
HALF = VDIM // 2
STATE_ROWS = VDIM + HALF
PART = FEAT + FEAT + VDIM
F32 = jnp.float32
BF16 = jnp.bfloat16


def nt(lhs, rhs):
    return lax.dot_general(lhs, rhs, (((1,), (1,)), ((), ())), preferred_element_type=F32)


def tn(lhs, rhs):
    return lax.dot_general(lhs, rhs, (((0,), (0,)), ((), ())), preferred_element_type=F32)


def nn(lhs, rhs):
    return lax.dot_general(lhs, rhs, (((1,), (0,)), ((), ())), preferred_element_type=F32)


def lanes(rows):
    return lax.broadcasted_iota(jnp.int32, (rows, LANES), 1)


def features(entries, weighted):
    lin, diag, off = (0.25, 1.0 / 32.0, 1.0 / 16.0) if weighted else (1.0, 1.0, 1.0)
    rows = [entries * lin if weighted else entries]
    base = entries * off if weighted else entries
    rows.append(entries * entries * diag if weighted else entries * entries)
    for step in range(1, FEAT // 2):
        rolled = jnp.concatenate([entries[step:], entries[:step]], axis=0)
        rows.append(base * rolled)
    rows.append(base[: FEAT // 2] * entries[FEAT // 2 :])
    tail = lax.broadcasted_iota(jnp.int32, (8, entries.shape[1]), 0)
    rows.append(jnp.where(tail == 0, 1.0, 0.0).astype(F32))
    return jnp.concatenate(rows, axis=0).astype(BF16)


def convolve(taps, raw, before):
    lane = lanes(VDIM)
    one = jnp.where(lane < 1, pltpu.roll(before, 1, 1), pltpu.roll(raw, 1, 1))
    two = jnp.where(lane < 2, pltpu.roll(before, 2, 1), pltpu.roll(raw, 2, 1))
    return (taps[0] * raw + taps[1] * one + taps[2] * two).astype(BF16)


def fold(main, rest):
    both = rest[:HALF] + pltpu.roll(rest[HALF:], LANES // 2, 1)
    return jnp.concatenate([main, both], axis=0).astype(BF16)


def unfold(packed):
    wide = packed.astype(F32)
    both = wide[VDIM:STATE_ROWS]
    low = lanes(HALF) < LANES // 2
    upper = jnp.where(low, both, 0.0)
    lower = jnp.where(low, pltpu.roll(both, LANES // 2, 1), 0.0)
    return wide[:VDIM], jnp.concatenate([upper, lower], axis=0)


def edge_state(taps_ref, edges):
    lane = lanes(VDIM)
    values = jnp.zeros((VDIM, LANES), F32)
    keys = jnp.zeros((FEAT, LANES), F32)
    for index, (key_rest, tail_rest) in enumerate(edges):
        at = 2 * index
        same = pltpu.roll(tail_rest, (LANES - EDGE + at) % LANES, 1)
        last = pltpu.roll(tail_rest, (LANES - EDGE - 1 + at) % LANES, 1)
        missing = jnp.where(lane == at, taps_ref[1] * last + taps_ref[2] * same, 0.0)
        missing = jnp.where(lane == at + 1, taps_ref[2] * same, missing)
        values = values + missing
        moved = pltpu.roll(key_rest[:FEAT], (LANES - EDGE - 2 + at) % LANES, 1)
        place = lanes(FEAT)
        keys = keys + jnp.where((place >= at) & (place < at + 2), moved, 0.0)
    state = nt(values.astype(BF16), features(keys, True))
    blank = jnp.zeros((VDIM, LANES - EDGE), F32)
    return state[:, :LANES], jnp.concatenate([state[:, LANES:], blank], axis=1)


def joined(rest, tail_rest, key_rest):
    lane = lanes(VDIM)
    return jnp.where(lane < EDGE, rest, jnp.where(lane < EDGE + 2, tail_rest, key_rest))


def pack_kernel(head_ref, q_ref, k_ref, v_ref, w_ref, gain_ref, out_ref, taps_ref):
    out_ref[:, 0:FEAT, :] = q_ref[...].T.reshape(HEADS, FEAT, BLK)
    out_ref[:, FEAT : 2 * FEAT, :] = k_ref[...].T.reshape(HEADS, FEAT, BLK)
    out_ref[:, 2 * FEAT :, :] = v_ref[...].T.reshape(HEADS, VDIM, BLK)
    rows = jnp.concatenate([w_ref[...], gain_ref[...], jnp.zeros((4, HEADS * VDIM), F32)], axis=0)
    mine = jnp.zeros((8, VDIM), F32)
    for head in range(HEADS):
        mine = jnp.where(head_ref[0] == head, rows[:, head * VDIM : (head + 1) * VDIM], mine)
    columns = mine.T
    for index in range(TAPS + 1):
        taps_ref[index] = jnp.broadcast_to(columns[:, index : index + 1], (VDIM, LANES))


def state_kernel(x_ref, taps_ref, sent_ref, own_ref, conv_ref):
    count = x_ref.shape[0]
    taps = [taps_ref[index] for index in range(TAPS)]
    total = jnp.zeros((VDIM, NPHI), F32)
    before = jnp.zeros((VDIM, BLK), F32)
    for blk in range(count):
        raw = x_ref[blk, 2 * FEAT :, :].astype(F32)
        conv = convolve(taps, raw, before)
        conv_ref[blk] = conv
        phi = features(x_ref[blk, FEAT : 2 * FEAT, :].astype(F32), True)
        total = total + nt(conv, phi)
        before = raw
    lane = lanes(VDIM)
    blank = jnp.zeros((VDIM, LANES - EDGE), F32)
    rest = jnp.concatenate([total[:, LANES:], blank], axis=1)
    tail = pltpu.roll(before, EDGE + 2, 1)
    first = x_ref[0, FEAT : 2 * FEAT, :].astype(F32)
    first = jnp.concatenate([first, jnp.zeros((VDIM - FEAT, BLK), F32)], axis=0)
    first = jnp.where(lane < EDGE + 4, pltpu.roll(first, EDGE + 2, 1), 0.0)
    rest = joined(rest, tail, first)
    main = total[:, :LANES]
    own_ref[0] = main
    own_ref[1] = rest
    sent_ref[0:STATE_ROWS, :] = fold(main, rest)
    sent_ref[STATE_ROWS:, :] = x_ref[count - 1, FEAT:, :]


def inside_window(first):
    row = lax.broadcasted_iota(jnp.int32, (WIN + BLK, BLK), 0)
    lane = lax.broadcasted_iota(jnp.int32, (WIN + BLK, BLK), 1)
    inside = (row >= lane) & (row <= lane + WIN)
    return inside if first is None else inside & ((row >= WIN) | (first == 0))


def block_parts(query, key, value, before_key, before_value, inside):
    scores = tn(jnp.concatenate([before_key, key], axis=1), query) * 0.25
    own = scores[BLK:]
    key_row = lax.broadcasted_iota(jnp.int32, (BLK, BLK), 0)
    query_lane = lax.broadcasted_iota(jnp.int32, (BLK, BLK), 1)
    weights = 1.0 + own + 0.5 * own * own
    weights = jnp.where(key_row <= query_lane, weights, 0.0).astype(BF16)
    masked = jnp.where(inside, scores[BLK - WIN :], -1e30)
    row_max = jnp.max(masked, axis=0, keepdims=True)
    exp_scores = jnp.exp(masked - row_max)
    row_sum = jnp.sum(exp_scores, axis=0, keepdims=True)
    blank = jnp.zeros((BLK - WIN, BLK), BF16)
    probs = jnp.concatenate([blank, exp_scores.astype(BF16)], axis=0)
    window = nn(jnp.concatenate([before_value, value], axis=1), probs)
    return nn(value, weights), window / row_sum


def local_blocks(first_ref, x_ref, conv_ref, near_ref, taps_ref, num_ref, win_ref, phi_ref):
    count = x_ref.shape[0]
    inside = inside_window(None)
    state = jnp.zeros((VDIM, NPHI), F32)
    taps = [taps_ref[index] for index in range(TAPS)]
    before_raw = near_ref[STATE_ROWS + FEAT :, :].astype(F32)
    before_value = convolve(taps, before_raw, jnp.zeros((VDIM, BLK), F32))
    before_key = near_ref[STATE_ROWS : STATE_ROWS + FEAT, :]
    for blk in range(count):
        query = x_ref[blk, 0:FEAT, :]
        key = x_ref[blk, FEAT : 2 * FEAT, :]
        if blk == 0:
            value = convolve(taps, x_ref[0, 2 * FEAT :, :].astype(F32), before_raw)
        else:
            value = conv_ref[blk]
        phi_query = features(query.astype(F32), False)
        phi_ref[:, blk * BLK : (blk + 1) * BLK] = phi_query
        mask = inside if blk > 0 or first_ref is None else inside_window(first_ref[0])
        own, win = block_parts(query, key, value, before_key, before_value, mask)
        num_ref[blk] = own + nn(state.astype(BF16), phi_query) if blk > 0 else own
        win_ref[blk] = win
        if blk + 1 < count:
            state = state + nt(value, features(key.astype(F32), True))
        before_key, before_value = key, value


def lower_local_kernel(first_ref, *refs):
    local_blocks(first_ref, *refs)


def unwritten_kernel(num_ref, win_ref, phi_ref):
    pass


def upper_local_kernel(quad_ref, x_ref, conv_ref, near_ref, taps_ref, *refs):
    @pl.when(quad_ref[0] > 1)
    def _():
        local_blocks(None, x_ref, conv_ref, near_ref, taps_ref, *refs[3:])


def merge_kernel(own_ref, near_ref, taps_ref, sent_ref, pair_ref):
    main, rest = own_ref[0], own_ref[1]
    near_main, near_rest = unfold(near_ref[0:STATE_ROWS, :])
    edge_main, edge_rest = edge_state(taps_ref, [(rest, near_rest)])
    main = main + near_main + edge_main
    rest = joined(rest + near_rest + edge_rest, rest, near_rest)
    pair_ref[0] = main
    pair_ref[1] = rest
    sent_ref[...] = fold(main, rest)


def join_kernel(quad_ref, pair_ref, recv_ref, taps_ref, sent_ref, copy_ref):
    copy_ref[...] = recv_ref[...]
    lowest = quad_ref[0] == 0
    main, rest = pair_ref[0], pair_ref[1]
    recv_main, recv_rest = unfold(recv_ref[...])
    lower = jnp.where(lowest, rest, recv_rest)
    upper = jnp.where(lowest, recv_rest, rest)
    edge_main, edge_rest = edge_state(taps_ref, [(upper, lower)])
    sent_ref[...] = fold(
        main + recv_main + edge_main, joined(rest + recv_rest + edge_rest, upper, lower)
    )


def final_kernel(
    quad_ref,
    pair_recv_ref,
    below_ref,
    low_ref,
    near_ref,
    taps_ref,
    num_ref,
    win_ref,
    phi_ref,
    out_ref,
):
    second = quad_ref[0] == 1
    near_main, near_rest = unfold(near_ref[0:STATE_ROWS, :])
    one_main, one_rest = unfold(pair_recv_ref[...])
    two_main, two_rest = unfold(below_ref[...])
    below_main = jnp.where(second, one_main, two_main)
    below_rest = jnp.where(second, one_rest, two_rest)
    low_main, low_rest = unfold(low_ref[...])
    above_low = jnp.where(quad_ref[0] == 2, near_rest, below_rest)
    edge_main, edge_rest = edge_state(taps_ref, [(near_rest, below_rest), (above_low, low_rest)])
    main = near_main + below_main + low_main + edge_main
    rest = near_rest + below_rest + low_rest + edge_rest
    state = jnp.concatenate([main, rest[:, :EDGE]], axis=1).astype(BF16)
    gain = taps_ref[TAPS]
    for blk in range(num_ref.shape[0]):
        phi = phi_ref[:, blk * BLK : (blk + 1) * BLK]
        num = num_ref[blk] + nn(state, phi)
        mean_square = jnp.sum(num * num, axis=0, keepdims=True) * (1.0 / VDIM)
        linear = num * lax.rsqrt(mean_square + 1e-06) * gain
        out_ref[blk] = (linear + win_ref[blk]).astype(BF16)


def unpack_kernel(x_ref, out_ref):
    out_ref[...] = x_ref[...].reshape(HEADS * VDIM, BLK).T


SMEM = pl.BlockSpec(memory_space=pltpu.SMEM)
VMEM = pl.BlockSpec(memory_space=pltpu.VMEM)


def call(kernel, outs, scalars, outer_arrays, arrays, aliases=None):
    limit = None if outer_arrays else 8 * 1024 * 1024
    arrays = [pltpu.with_memory_space_constraint(array, pltpu.VMEM) for array in arrays]
    count = len(outer_arrays) + len(arrays)
    single = len(outs) == 1
    return pl.pallas_call(
        kernel,
        out_shape=outs[0] if single else tuple(outs),
        in_specs=[SMEM] * len(scalars) + [VMEM] * count,
        out_specs=VMEM if single else tuple(VMEM for _ in outs),
        input_output_aliases=aliases or {},
        compiler_params=pltpu.CompilerParams(vmem_limit_bytes=limit),
    )(*scalars, *outer_arrays, *arrays)


def scalar(value):
    return jnp.asarray(value).astype(jnp.int32).reshape(1)


def on_device(query_rows, key_rows, value_rows, conv_weight, norm_gain):
    group = ("pair", "core", "inner")
    stack = ("quad", "half")
    members = lax.axis_size(group)
    groups = lax.axis_size(stack)

    def upward(value):
        return lax.ppermute(value, stack, [(i, i + 1) for i in range(groups - 1)])

    packed, taps = call(
        pack_kernel,
        [pltpu.VMEM((HEADS, PART, BLK), BF16), pltpu.VMEM((TAPS + 1, VDIM, LANES), F32)],
        [scalar(lax.axis_index(group))],
        [query_rows, key_rows, value_rows, conv_weight, norm_gain.reshape(1, HEADS * VDIM)],
        [],
    )
    mine = lax.all_to_all(packed, group, 0, 0)
    sent, own, conv = call(
        state_kernel,
        [
            pltpu.VMEM((STATE_ROWS + FEAT + VDIM, BLK), BF16),
            pltpu.VMEM((2, VDIM, LANES), F32),
            pltpu.VMEM((members, VDIM, BLK), BF16),
        ],
        [],
        [],
        [mine, taps],
    )
    near = upward(sent)
    block = (VDIM, BLK)
    sent, pair = call(
        merge_kernel,
        [pltpu.VMEM((STATE_ROWS, LANES), BF16), pltpu.VMEM((2, VDIM, LANES), F32)],
        [],
        [],
        [own, near, taps],
    )
    quad = lax.axis_index("quad")
    first = scalar(lax.axis_index(stack) == 0)
    local_shapes = [
        pltpu.VMEM((members, *block), F32),
        pltpu.VMEM((members, *block), F32),
        pltpu.VMEM((NPHI, members * BLK), BF16),
    ]
    local_arrays = [mine, conv, near, taps]

    def lower(sent):
        recv = lax.ppermute(sent, "quad", [(0, 1), (1, 0)])
        local = call(lower_local_kernel, local_shapes, [first], [], local_arrays)
        both, recv = call(
            join_kernel,
            [pltpu.VMEM((STATE_ROWS, LANES), BF16), pltpu.VMEM((STATE_ROWS, LANES), BF16)],
            [scalar(quad)],
            [],
            [pair, recv, taps],
        )
        return both, recv, *local

    def upper(sent):
        return sent, sent, *call(unwritten_kernel, local_shapes, [], [], [])

    both, pair_recv, *local = lax.cond(quad < 2, lower, upper, sent)
    low = lax.ppermute(both, "quad", [(1, 2), (0, 3)])
    below = lax.ppermute(sent, "quad", [(2, 3)])
    num, win, phi = call(
        upper_local_kernel,
        local_shapes,
        [scalar(quad)],
        [],
        [*local_arrays, *local],
        {5: 0, 6: 1, 7: 2},
    )
    done = call(
        final_kernel,
        [pltpu.VMEM((members, *block), BF16)],
        [scalar(quad)],
        [],
        [pair_recv, below, low, near, taps, num, win, phi],
    )
    heads = lax.all_to_all(done, group, 0, 0)
    out = jax.ShapeDtypeStruct((BLK, HEADS * VDIM), BF16)
    return call(unpack_kernel, [out], [], [], [heads])


def solution(mesh):
    outer, inner = mesh.shape["outer"], mesh.shape["inner"]
    pair = HEADS // inner // 2
    shape = (mesh.shape["dp"], outer // (2 * 2 * pair), 2, pair, 2, inner)
    split = Mesh(
        np.asarray(mesh.devices).reshape(shape), ("dp", "quad", "half", "pair", "core", "inner")
    )
    rows = P(("dp", "quad", "half", "pair", "core", "inner"), None)
    return jax.shard_map(
        on_device,
        mesh=split,
        in_specs=(rows, rows, rows, P(), P()),
        out_specs=rows,
        check_vma=False,
    )
```

```python
import jax
import jax.numpy as jnp
import numpy as np
from jax import lax
from jax.experimental import pallas as pl
from jax.experimental.pallas import tpu as pltpu
from jax.sharding import Mesh, PartitionSpec as P

HEADS = 16
FEAT = 16
VDIM = 64
TAPS = 3
WIN = 64
BLK = 128
NPHI = 160
LANES = 128
EDGE = NPHI - LANES
HALF = VDIM // 2
STATE_ROWS = VDIM + HALF
HALO_ROWS = STATE_ROWS + HALF
PIECES = 4
PART = FEAT + FEAT + VDIM
F32 = jnp.float32
BF16 = jnp.bfloat16


def nt(lhs, rhs):
    return lax.dot_general(lhs, rhs, (((1,), (1,)), ((), ())), preferred_element_type=F32)


def tn(lhs, rhs):
    return lax.dot_general(lhs, rhs, (((0,), (0,)), ((), ())), preferred_element_type=F32)


def nn(lhs, rhs):
    return lax.dot_general(lhs, rhs, (((1,), (0,)), ((), ())), preferred_element_type=F32)


def lanes(rows):
    return lax.broadcasted_iota(jnp.int32, (rows, LANES), 1)


def features(entries, weighted):
    lin, diag, off = (0.25, 1.0 / 32.0, 1.0 / 16.0) if weighted else (1.0, 1.0, 1.0)
    rows = [entries * lin if weighted else entries]
    base = entries * off if weighted else entries
    rows.append(entries * entries * diag if weighted else entries * entries)
    for step in range(1, FEAT // 2):
        rolled = jnp.concatenate([entries[step:], entries[:step]], axis=0)
        rows.append(base * rolled)
    rows.append(base[: FEAT // 2] * entries[FEAT // 2 :])
    tail = lax.broadcasted_iota(jnp.int32, (8, entries.shape[1]), 0)
    rows.append(jnp.where(tail == 0, 1.0, 0.0).astype(F32))
    return jnp.concatenate(rows, axis=0).astype(BF16)


def convolve(taps, raw, before):
    lane = lanes(VDIM)
    one = jnp.where(lane < 1, pltpu.roll(before, 1, 1), pltpu.roll(raw, 1, 1))
    two = jnp.where(lane < 2, pltpu.roll(before, 2, 1), pltpu.roll(raw, 2, 1))
    return (taps[0] * raw + taps[1] * one + taps[2] * two).astype(BF16)


def fold(main, rest):
    both = rest[:HALF] + pltpu.roll(rest[HALF:], LANES // 2, 1)
    return jnp.concatenate([main, both], axis=0).astype(BF16)


def unfold(packed):
    wide = packed.astype(F32)
    both = wide[VDIM:STATE_ROWS]
    low = lanes(HALF) < LANES // 2
    upper = jnp.where(low, both, 0.0)
    lower = jnp.where(low, pltpu.roll(both, LANES // 2, 1), 0.0)
    return wide[:VDIM], jnp.concatenate([upper, lower], axis=0)


def edge_state(taps_ref, edges):
    lane = lanes(VDIM)
    values = jnp.zeros((VDIM, LANES), F32)
    keys = jnp.zeros((FEAT, LANES), F32)
    for index, (key_rest, tail_rest) in enumerate(edges):
        at = 2 * index
        same = pltpu.roll(tail_rest, (LANES - EDGE + at) % LANES, 1)
        last = pltpu.roll(tail_rest, (LANES - EDGE - 1 + at) % LANES, 1)
        missing = jnp.where(lane == at, taps_ref[1] * last + taps_ref[2] * same, 0.0)
        missing = jnp.where(lane == at + 1, taps_ref[2] * same, missing)
        values = values + missing
        moved = pltpu.roll(key_rest[:FEAT], (LANES - EDGE - 2 + at) % LANES, 1)
        place = lanes(FEAT)
        keys = keys + jnp.where((place >= at) & (place < at + 2), moved, 0.0)
    state = nt(values.astype(BF16), features(keys, True))
    blank = jnp.zeros((VDIM, LANES - EDGE), F32)
    return state[:, :LANES], jnp.concatenate([state[:, LANES:], blank], axis=1)


def joined(rest, tail_rest, key_rest):
    lane = lanes(VDIM)
    return jnp.where(lane < EDGE, rest, jnp.where(lane < EDGE + 2, tail_rest, key_rest))


def pack_kernel(
    head_ref,
    q_hbm,
    k_hbm,
    v_hbm,
    w_hbm,
    gain_hbm,
    out_ref,
    taps_ref,
    q_ref,
    k_ref,
    v_ref,
    w_ref,
    gain_ref,
    sems,
):
    def copy(source, target, index):
        return pltpu.make_async_copy(source, target, sems.at[index])

    width = HEADS * VDIM // PIECES
    heads = HEADS // PIECES
    pieces = [
        copy(
            v_hbm.at[:, pl.ds(piece * width, width)],
            v_ref.at[:, pl.ds(piece * width, width)],
            4 + piece,
        )
        for piece in range(PIECES)
    ]
    query, key = copy(q_hbm, q_ref, 0), copy(k_hbm, k_ref, 1)
    conv, gain = copy(w_hbm, w_ref, 2), copy(gain_hbm, gain_ref, 3)
    for started in (query, key, *pieces, conv, gain):
        started.start()
    query.wait()
    out_ref[:, 0:FEAT, :] = q_ref[...].T.reshape(HEADS, FEAT, BLK)
    key.wait()
    out_ref[:, FEAT : 2 * FEAT, :] = k_ref[...].T.reshape(HEADS, FEAT, BLK)
    for piece in range(PIECES):
        pieces[piece].wait()
        turned = v_ref[:, piece * width : (piece + 1) * width].T.reshape(heads, VDIM, BLK)
        out_ref[piece * heads : (piece + 1) * heads, 2 * FEAT :, :] = turned
    conv.wait()
    gain.wait()
    rows = jnp.concatenate([w_ref[...], gain_ref[...], jnp.zeros((4, HEADS * VDIM), F32)], axis=0)
    mine = jnp.zeros((8, VDIM), F32)
    for head in range(HEADS):
        mine = jnp.where(head_ref[0] == head, rows[:, head * VDIM : (head + 1) * VDIM], mine)
    columns = mine.T
    for index in range(TAPS + 1):
        taps_ref[index] = jnp.broadcast_to(columns[:, index : index + 1], (VDIM, LANES))


def state_kernel(x_ref, taps_ref, sent_ref, own_ref, conv_ref):
    count = x_ref.shape[0]
    taps = [taps_ref[index] for index in range(TAPS)]
    total = jnp.zeros((VDIM, NPHI), F32)
    before = jnp.zeros((VDIM, BLK), F32)
    for blk in range(count):
        raw = x_ref[blk, 2 * FEAT :, :].astype(F32)
        conv = convolve(taps, raw, before)
        conv_ref[blk] = conv
        phi = features(x_ref[blk, FEAT : 2 * FEAT, :].astype(F32), True)
        total = total + nt(conv, phi)
        before = raw
    lane = lanes(VDIM)
    blank = jnp.zeros((VDIM, LANES - EDGE), F32)
    rest = jnp.concatenate([total[:, LANES:], blank], axis=1)
    tail = pltpu.roll(before, EDGE + 2, 1)
    first = x_ref[0, FEAT : 2 * FEAT, :].astype(F32)
    first = jnp.concatenate([first, jnp.zeros((VDIM - FEAT, BLK), F32)], axis=0)
    first = jnp.where(lane < EDGE + 4, pltpu.roll(first, EDGE + 2, 1), 0.0)
    rest = joined(rest, tail, first)
    main = total[:, :LANES]
    own_ref[0] = main
    own_ref[1] = rest
    sent_ref[0:STATE_ROWS, :] = fold(main, rest)
    wide = conv.astype(F32)
    upper = pltpu.roll(wide[:HALF], WIN, 1)
    sent_ref[STATE_ROWS:HALO_ROWS, :] = jnp.where(lanes(HALF) < WIN, upper, wide[HALF:]).astype(BF16)
    sent_ref[HALO_ROWS:, :] = x_ref[count - 1, FEAT : 2 * FEAT, :]


def inside_window(first):
    row = lax.broadcasted_iota(jnp.int32, (WIN + BLK, BLK), 0)
    lane = lax.broadcasted_iota(jnp.int32, (WIN + BLK, BLK), 1)
    inside = (row >= lane) & (row <= lane + WIN)
    return inside if first is None else inside & ((row >= WIN) | (first == 0))


def block_parts(query, key, value, before_key, before_value, inside):
    scores = tn(jnp.concatenate([before_key, key], axis=1), query) * 0.25
    own = scores[BLK:]
    key_row = lax.broadcasted_iota(jnp.int32, (BLK, BLK), 0)
    query_lane = lax.broadcasted_iota(jnp.int32, (BLK, BLK), 1)
    weights = 1.0 + own + 0.5 * own * own
    weights = jnp.where(key_row <= query_lane, weights, 0.0).astype(BF16)
    masked = jnp.where(inside, scores[BLK - WIN :], -1e30)
    row_max = jnp.max(masked, axis=0, keepdims=True)
    exp_scores = jnp.exp(masked - row_max)
    row_sum = jnp.sum(exp_scores, axis=0, keepdims=True)
    blank = jnp.zeros((BLK - WIN, BLK), BF16)
    probs = jnp.concatenate([blank, exp_scores.astype(BF16)], axis=0)
    window = nn(jnp.concatenate([before_value, value], axis=1), probs)
    return nn(value, weights), window / row_sum


def local_blocks(first_ref, x_ref, conv_ref, near_ref, taps_ref, num_ref, win_ref, phi_ref):
    count = x_ref.shape[0]
    inside = inside_window(None)
    state = jnp.zeros((VDIM, NPHI), F32)
    taps = [taps_ref[index] for index in range(TAPS)]
    before_raw = pltpu.roll(unfold(near_ref[0:STATE_ROWS, :])[1], LANES - EDGE - 2, 1)
    halves = near_ref[STATE_ROWS:HALO_ROWS, :].astype(F32)
    before_value = jnp.concatenate([pltpu.roll(halves, WIN, 1), halves], axis=0).astype(BF16)
    before_key = near_ref[HALO_ROWS:, :]
    for blk in range(count):
        query = x_ref[blk, 0:FEAT, :]
        key = x_ref[blk, FEAT : 2 * FEAT, :]
        if blk == 0:
            value = convolve(taps, x_ref[0, 2 * FEAT :, :].astype(F32), before_raw)
        else:
            value = conv_ref[blk]
        phi_query = features(query.astype(F32), False)
        phi_ref[:, blk * BLK : (blk + 1) * BLK] = phi_query
        mask = inside if blk > 0 or first_ref is None else inside_window(first_ref[0])
        own, win = block_parts(query, key, value, before_key, before_value, mask)
        num_ref[blk] = own + nn(state.astype(BF16), phi_query) if blk > 0 else own
        win_ref[blk] = win
        if blk + 1 < count:
            state = state + nt(value, features(key.astype(F32), True))
        before_key, before_value = key, value


def lower_local_kernel(first_ref, *refs):
    local_blocks(first_ref, *refs)


def unwritten_kernel(num_ref, win_ref, phi_ref):
    pass


def upper_local_kernel(quad_ref, x_ref, conv_ref, near_ref, taps_ref, *refs):
    @pl.when(quad_ref[0] > 1)
    def _():
        local_blocks(None, x_ref, conv_ref, near_ref, taps_ref, *refs[3:])


def merge_kernel(own_ref, near_ref, taps_ref, sent_ref, pair_ref):
    main, rest = own_ref[0], own_ref[1]
    near_main, near_rest = unfold(near_ref[0:STATE_ROWS, :])
    edge_main, edge_rest = edge_state(taps_ref, [(rest, near_rest)])
    main = main + near_main + edge_main
    rest = joined(rest + near_rest + edge_rest, rest, near_rest)
    pair_ref[0] = main
    pair_ref[1] = rest
    sent_ref[...] = fold(main, rest)


def join_kernel(quad_ref, pair_ref, recv_ref, taps_ref, sent_ref, copy_ref):
    copy_ref[...] = recv_ref[...]
    lowest = quad_ref[0] == 0
    main, rest = pair_ref[0], pair_ref[1]
    recv_main, recv_rest = unfold(recv_ref[...])
    lower = jnp.where(lowest, rest, recv_rest)
    upper = jnp.where(lowest, recv_rest, rest)
    edge_main, edge_rest = edge_state(taps_ref, [(upper, lower)])
    sent_ref[...] = fold(
        main + recv_main + edge_main, joined(rest + recv_rest + edge_rest, upper, lower)
    )


def final_kernel(
    quad_ref,
    pair_recv_ref,
    below_ref,
    low_ref,
    near_ref,
    taps_ref,
    num_ref,
    win_ref,
    phi_ref,
    out_ref,
):
    second = quad_ref[0] == 1
    near_main, near_rest = unfold(near_ref[0:STATE_ROWS, :])
    one_main, one_rest = unfold(pair_recv_ref[...])
    two_main, two_rest = unfold(below_ref[...])
    below_main = jnp.where(second, one_main, two_main)
    below_rest = jnp.where(second, one_rest, two_rest)
    low_main, low_rest = unfold(low_ref[...])
    above_low = jnp.where(quad_ref[0] == 2, near_rest, below_rest)
    edge_main, edge_rest = edge_state(taps_ref, [(near_rest, below_rest), (above_low, low_rest)])
    main = near_main + below_main + low_main + edge_main
    rest = near_rest + below_rest + low_rest + edge_rest
    state = jnp.concatenate([main, rest[:, :EDGE]], axis=1).astype(BF16)
    gain = taps_ref[TAPS]
    for blk in range(num_ref.shape[0]):
        phi = phi_ref[:, blk * BLK : (blk + 1) * BLK]
        num = num_ref[blk] + nn(state, phi)
        mean_square = jnp.sum(num * num, axis=0, keepdims=True) * (1.0 / VDIM)
        linear = num * lax.rsqrt(mean_square + 1e-06) * gain
        out_ref[blk] = (linear + win_ref[blk]).astype(BF16)


def unpack_kernel(x_ref, out_ref):
    out_ref[...] = x_ref[...].reshape(HEADS * VDIM, BLK).T


SMEM = pl.BlockSpec(memory_space=pltpu.SMEM)
VMEM = pl.BlockSpec(memory_space=pltpu.VMEM)


def call(kernel, outs, scalars, arrays, aliases=None):
    arrays = [pltpu.with_memory_space_constraint(array, pltpu.VMEM) for array in arrays]
    single = len(outs) == 1
    return pl.pallas_call(
        kernel,
        out_shape=outs[0] if single else tuple(outs),
        in_specs=[SMEM] * len(scalars) + [VMEM] * len(arrays),
        out_specs=VMEM if single else tuple(VMEM for _ in outs),
        input_output_aliases=aliases or {},
        compiler_params=pltpu.CompilerParams(vmem_limit_bytes=8 * 1024 * 1024),
    )(*scalars, *arrays)


def scalar(value):
    return jnp.asarray(value).astype(jnp.int32).reshape(1)


def on_device(query_rows, key_rows, value_rows, conv_weight, norm_gain):
    group = ("pair", "core", "inner")
    stack = ("quad", "half")
    members = lax.axis_size(group)
    groups = lax.axis_size(stack)

    def upward(value):
        return lax.ppermute(value, stack, [(i, i + 1) for i in range(groups - 1)])

    rows = [query_rows, key_rows, value_rows, conv_weight, norm_gain.reshape(1, HEADS * VDIM)]
    packed, taps = pl.pallas_call(
        pack_kernel,
        out_shape=(
            pltpu.VMEM((HEADS, PART, BLK), BF16),
            pltpu.VMEM((TAPS + 1, VDIM, LANES), F32),
        ),
        in_specs=[SMEM] + [pl.BlockSpec(memory_space=pl.ANY)] * len(rows),
        out_specs=(VMEM, VMEM),
        scratch_shapes=[pltpu.VMEM(array.shape, array.dtype) for array in rows]
        + [pltpu.SemaphoreType.DMA((4 + PIECES,))],
    )(scalar(lax.axis_index(group)), *rows)
    mine = lax.all_to_all(packed, group, 0, 0)
    sent, own, conv = call(
        state_kernel,
        [
            pltpu.VMEM((HALO_ROWS + FEAT, BLK), BF16),
            pltpu.VMEM((2, VDIM, LANES), F32),
            pltpu.VMEM((members, VDIM, BLK), BF16),
        ],
        [],
        [mine, taps],
    )
    near = upward(sent)
    block = (VDIM, BLK)
    sent, pair = call(
        merge_kernel,
        [pltpu.VMEM((STATE_ROWS, LANES), BF16), pltpu.VMEM((2, VDIM, LANES), F32)],
        [],
        [own, near, taps],
    )
    quad = lax.axis_index("quad")
    first = scalar(lax.axis_index(stack) == 0)
    local_shapes = [
        pltpu.VMEM((members, *block), F32),
        pltpu.VMEM((members, *block), F32),
        pltpu.VMEM((NPHI, members * BLK), BF16),
    ]
    local_arrays = [mine, conv, near, taps]

    def lower(sent):
        recv = lax.ppermute(sent, "quad", [(0, 1), (1, 0)])
        local = call(lower_local_kernel, local_shapes, [first], local_arrays)
        both, recv = call(
            join_kernel,
            [pltpu.VMEM((STATE_ROWS, LANES), BF16), pltpu.VMEM((STATE_ROWS, LANES), BF16)],
            [scalar(quad)],
            [pair, recv, taps],
        )
        return both, recv, *local

    def upper(sent):
        return sent, sent, *call(unwritten_kernel, local_shapes, [], [])

    both, pair_recv, *local = lax.cond(quad < 2, lower, upper, sent)
    low = lax.ppermute(both, "quad", [(1, 2), (0, 3)])
    below = lax.ppermute(sent, "quad", [(2, 3)])
    num, win, phi = call(
        upper_local_kernel,
        local_shapes,
        [scalar(quad)],
        [*local_arrays, *local],
        {5: 0, 6: 1, 7: 2},
    )
    done = call(
        final_kernel,
        [pltpu.VMEM((members, *block), BF16)],
        [scalar(quad)],
        [pair_recv, below, low, near, taps, num, win, phi],
    )
    heads = lax.all_to_all(done, group, 0, 0)
    out = jax.ShapeDtypeStruct((BLK, HEADS * VDIM), BF16)
    return call(unpack_kernel, [out], [], [heads])


def solution(mesh):
    outer, inner = mesh.shape["outer"], mesh.shape["inner"]
    pair = HEADS // inner // 2
    shape = (mesh.shape["dp"], outer // (2 * 2 * pair), 2, pair, 2, inner)
    split = Mesh(
        np.asarray(mesh.devices).reshape(shape), ("dp", "quad", "half", "pair", "core", "inner")
    )
    rows = P(("dp", "quad", "half", "pair", "core", "inner"), None)
    return jax.shard_map(
        on_device,
        mesh=split,
        in_specs=(rows, rows, rows, P(), P()),
        out_specs=rows,
        check_vma=False,
    )
```

```python
import jax
import jax.numpy as jnp
import numpy as np
from jax import lax
from jax.experimental import pallas as pl
from jax.experimental.pallas import tpu as pltpu
from jax.sharding import Mesh, PartitionSpec as P

HEADS = 16
FEAT = 16
VDIM = 64
TAPS = 3
WIN = 64
BLK = 128
NPHI = 160
LANES = 128
EDGE = NPHI - LANES
HALF = VDIM // 2
STATE_ROWS = VDIM + HALF
HALO_ROWS = STATE_ROWS + HALF
PART = FEAT + FEAT + VDIM
F32 = jnp.float32
BF16 = jnp.bfloat16


def nt(lhs, rhs):
    return lax.dot_general(lhs, rhs, (((1,), (1,)), ((), ())), preferred_element_type=F32)


def tn(lhs, rhs):
    return lax.dot_general(lhs, rhs, (((0,), (0,)), ((), ())), preferred_element_type=F32)


def nn(lhs, rhs):
    return lax.dot_general(lhs, rhs, (((1,), (0,)), ((), ())), preferred_element_type=F32)


def lanes(rows):
    return lax.broadcasted_iota(jnp.int32, (rows, LANES), 1)


def features(entries, weighted):
    lin, diag, off = (0.25, 1.0 / 32.0, 1.0 / 16.0) if weighted else (1.0, 1.0, 1.0)
    rows = [entries * lin if weighted else entries]
    base = entries * off if weighted else entries
    rows.append(entries * entries * diag if weighted else entries * entries)
    for step in range(1, FEAT // 2):
        rolled = jnp.concatenate([entries[step:], entries[:step]], axis=0)
        rows.append(base * rolled)
    rows.append(base[: FEAT // 2] * entries[FEAT // 2 :])
    tail = lax.broadcasted_iota(jnp.int32, (8, entries.shape[1]), 0)
    rows.append(jnp.where(tail == 0, 1.0, 0.0).astype(F32))
    return jnp.concatenate(rows, axis=0).astype(BF16)


def convolve(taps, raw, before):
    lane = lanes(VDIM)
    one = jnp.where(lane < 1, pltpu.roll(before, 1, 1), pltpu.roll(raw, 1, 1))
    two = jnp.where(lane < 2, pltpu.roll(before, 2, 1), pltpu.roll(raw, 2, 1))
    return (taps[0] * raw + taps[1] * one + taps[2] * two).astype(BF16)


def fold(main, rest):
    both = rest[:HALF] + pltpu.roll(rest[HALF:], LANES // 2, 1)
    return jnp.concatenate([main, both], axis=0).astype(BF16)


def unfold(packed):
    wide = packed.astype(F32)
    both = wide[VDIM:STATE_ROWS]
    low = lanes(HALF) < LANES // 2
    upper = jnp.where(low, both, 0.0)
    lower = jnp.where(low, pltpu.roll(both, LANES // 2, 1), 0.0)
    return wide[:VDIM], jnp.concatenate([upper, lower], axis=0)


def edge_state(taps_ref, edges):
    lane = lanes(VDIM)
    values = jnp.zeros((VDIM, LANES), F32)
    keys = jnp.zeros((FEAT, LANES), F32)
    for index, (key_rest, tail_rest) in enumerate(edges):
        at = 2 * index
        same = pltpu.roll(tail_rest, (LANES - EDGE + at) % LANES, 1)
        last = pltpu.roll(tail_rest, (LANES - EDGE - 1 + at) % LANES, 1)
        missing = jnp.where(lane == at, taps_ref[1] * last + taps_ref[2] * same, 0.0)
        missing = jnp.where(lane == at + 1, taps_ref[2] * same, missing)
        values = values + missing
        moved = pltpu.roll(key_rest[:FEAT], (LANES - EDGE - 2 + at) % LANES, 1)
        place = lanes(FEAT)
        keys = keys + jnp.where((place >= at) & (place < at + 2), moved, 0.0)
    state = nt(values.astype(BF16), features(keys, True))
    blank = jnp.zeros((VDIM, LANES - EDGE), F32)
    return state[:, :LANES], jnp.concatenate([state[:, LANES:], blank], axis=1)


def joined(rest, tail_rest, key_rest):
    lane = lanes(VDIM)
    return jnp.where(lane < EDGE, rest, jnp.where(lane < EDGE + 2, tail_rest, key_rest))


def pack_kernel(head_ref, q_ref, k_ref, v_ref, w_ref, gain_ref, out_ref, taps_ref):
    out_ref[:, 0:FEAT, :] = q_ref[...].T.reshape(HEADS, FEAT, BLK)
    out_ref[:, FEAT : 2 * FEAT, :] = k_ref[...].T.reshape(HEADS, FEAT, BLK)
    out_ref[:, 2 * FEAT :, :] = v_ref[...].T.reshape(HEADS, VDIM, BLK)
    head = head_ref[0]
    start = pl.multiple_of(head // 2 * LANES, LANES)
    odd = head % 2 == 1
    for index in range(TAPS + 1):
        source, at = (w_ref, index) if index < TAPS else (gain_ref, 0)
        row = source[at : at + 1, pl.ds(start, LANES)]
        both = jnp.broadcast_to(row, (LANES, LANES)).T
        taps_ref[index] = jnp.where(odd, both[VDIM:], both[:VDIM])


def state_kernel(x_ref, taps_ref, sent_ref, own_ref, conv_ref):
    count = x_ref.shape[0]
    taps = [taps_ref[index] for index in range(TAPS)]
    total = jnp.zeros((VDIM, NPHI), F32)
    before = jnp.zeros((VDIM, BLK), F32)
    for blk in range(count):
        raw = x_ref[blk, 2 * FEAT :, :].astype(F32)
        conv = convolve(taps, raw, before)
        conv_ref[blk] = conv
        phi = features(x_ref[blk, FEAT : 2 * FEAT, :].astype(F32), True)
        total = total + nt(conv, phi)
        before = raw
    lane = lanes(VDIM)
    blank = jnp.zeros((VDIM, LANES - EDGE), F32)
    rest = jnp.concatenate([total[:, LANES:], blank], axis=1)
    tail = pltpu.roll(before, EDGE + 2, 1)
    first = x_ref[0, FEAT : 2 * FEAT, :].astype(F32)
    first = jnp.concatenate([first, jnp.zeros((VDIM - FEAT, BLK), F32)], axis=0)
    first = jnp.where(lane < EDGE + 4, pltpu.roll(first, EDGE + 2, 1), 0.0)
    rest = joined(rest, tail, first)
    main = total[:, :LANES]
    own_ref[0] = main
    own_ref[1] = rest
    sent_ref[0:STATE_ROWS, :] = fold(main, rest)
    wide = conv.astype(F32)
    upper = pltpu.roll(wide[:HALF], WIN, 1)
    sent_ref[STATE_ROWS:HALO_ROWS, :] = jnp.where(lanes(HALF) < WIN, upper, wide[HALF:]).astype(BF16)
    sent_ref[HALO_ROWS:, :] = x_ref[count - 1, FEAT : 2 * FEAT, :]


def inside_window(first):
    row = lax.broadcasted_iota(jnp.int32, (WIN + BLK, BLK), 0)
    lane = lax.broadcasted_iota(jnp.int32, (WIN + BLK, BLK), 1)
    inside = (row >= lane) & (row <= lane + WIN)
    return inside if first is None else inside & ((row >= WIN) | (first == 0))


def block_parts(query, key, value, before_key, before_value, inside):
    scores = tn(jnp.concatenate([before_key, key], axis=1), query) * 0.25
    own = scores[BLK:]
    key_row = lax.broadcasted_iota(jnp.int32, (BLK, BLK), 0)
    query_lane = lax.broadcasted_iota(jnp.int32, (BLK, BLK), 1)
    weights = 1.0 + own + 0.5 * own * own
    weights = jnp.where(key_row <= query_lane, weights, 0.0).astype(BF16)
    masked = jnp.where(inside, scores[BLK - WIN :], -1e30)
    row_max = jnp.max(masked, axis=0, keepdims=True)
    exp_scores = jnp.exp(masked - row_max)
    row_sum = jnp.sum(exp_scores, axis=0, keepdims=True)
    blank = jnp.zeros((BLK - WIN, BLK), BF16)
    probs = jnp.concatenate([blank, exp_scores.astype(BF16)], axis=0)
    window = nn(jnp.concatenate([before_value, value], axis=1), probs)
    return nn(value, weights), window / row_sum


def local_blocks(first_ref, x_ref, conv_ref, near_ref, taps_ref, num_ref, win_ref, phi_ref):
    count = x_ref.shape[0]
    inside = inside_window(None)
    state = jnp.zeros((VDIM, NPHI), F32)
    taps = [taps_ref[index] for index in range(TAPS)]
    before_raw = pltpu.roll(unfold(near_ref[0:STATE_ROWS, :])[1], LANES - EDGE - 2, 1)
    halves = near_ref[STATE_ROWS:HALO_ROWS, :].astype(F32)
    before_value = jnp.concatenate([pltpu.roll(halves, WIN, 1), halves], axis=0).astype(BF16)
    before_key = near_ref[HALO_ROWS:, :]
    for blk in range(count):
        query = x_ref[blk, 0:FEAT, :]
        key = x_ref[blk, FEAT : 2 * FEAT, :]
        if blk == 0:
            value = convolve(taps, x_ref[0, 2 * FEAT :, :].astype(F32), before_raw)
        else:
            value = conv_ref[blk]
        phi_query = features(query.astype(F32), False)
        phi_ref[:, blk * BLK : (blk + 1) * BLK] = phi_query
        mask = inside if blk > 0 or first_ref is None else inside_window(first_ref[0])
        own, win = block_parts(query, key, value, before_key, before_value, mask)
        num_ref[blk] = own + nn(state.astype(BF16), phi_query) if blk > 0 else own
        win_ref[blk] = win
        if blk + 1 < count:
            state = state + nt(value, features(key.astype(F32), True))
        before_key, before_value = key, value


def second_local_kernel(quad_ref, x_ref, conv_ref, near_ref, taps_ref, *refs):
    @pl.when(quad_ref[0] == 1)
    def _():
        local_blocks(None, x_ref, conv_ref, near_ref, taps_ref, *refs[3:])


def upper_local_kernel(quad_ref, x_ref, conv_ref, near_ref, taps_ref, *refs):
    @pl.when(quad_ref[0] > 1)
    def _():
        local_blocks(None, x_ref, conv_ref, near_ref, taps_ref, *refs[3:])


def merge_kernel(
    quad_ref,
    first_ref,
    own_ref,
    x_ref,
    conv_ref,
    near_ref,
    taps_ref,
    sent_ref,
    pair_ref,
    num_ref,
    win_ref,
    phi_ref,
):
    main, rest = own_ref[0], own_ref[1]
    near_main, near_rest = unfold(near_ref[0:STATE_ROWS, :])
    edge_main, edge_rest = edge_state(taps_ref, [(rest, near_rest)])
    main = main + near_main + edge_main
    rest = joined(rest + near_rest + edge_rest, rest, near_rest)
    pair_ref[0] = main
    pair_ref[1] = rest
    sent_ref[...] = fold(main, rest)

    @pl.when(quad_ref[0] == 0)
    def _():
        local_blocks(first_ref, x_ref, conv_ref, near_ref, taps_ref, num_ref, win_ref, phi_ref)


def join_kernel(quad_ref, pair_ref, recv_ref, taps_ref, sent_ref, copy_ref):
    @pl.when(quad_ref[0] == 1)
    def _():
        main, rest = pair_ref[0], pair_ref[1]
        recv_main, recv_rest = unfold(recv_ref[...])
        edge_main, edge_rest = edge_state(taps_ref, [(rest, recv_rest)])
        copy_ref[...] = recv_ref[...]
        sent_ref[...] = fold(
            main + recv_main + edge_main, joined(rest + recv_rest + edge_rest, rest, recv_rest)
        )

    @pl.when(quad_ref[0] != 1)
    def _():
        copy_ref[...] = recv_ref[...]
        sent_ref[...] = recv_ref[...]


def final_kernel(
    quad_ref,
    pair_recv_ref,
    below_ref,
    low_ref,
    near_ref,
    taps_ref,
    num_ref,
    win_ref,
    phi_ref,
    out_ref,
):
    second = quad_ref[0] == 1
    near_main, near_rest = unfold(near_ref[0:STATE_ROWS, :])
    one_main, one_rest = unfold(pair_recv_ref[...])
    two_main, two_rest = unfold(below_ref[...])
    below_main = jnp.where(second, one_main, two_main)
    below_rest = jnp.where(second, one_rest, two_rest)
    low_main, low_rest = unfold(low_ref[...])
    edge_main, edge_rest = edge_state(taps_ref, [(near_rest, below_rest), (below_rest, low_rest)])
    main = near_main + below_main + low_main + edge_main
    rest = near_rest + below_rest + low_rest + edge_rest
    state = jnp.concatenate([main, rest[:, :EDGE]], axis=1).astype(BF16)
    gain = taps_ref[TAPS]
    for blk in range(num_ref.shape[0]):
        phi = phi_ref[:, blk * BLK : (blk + 1) * BLK]
        num = num_ref[blk] + nn(state, phi)
        mean_square = jnp.sum(num * num, axis=0, keepdims=True) * (1.0 / VDIM)
        linear = num * lax.rsqrt(mean_square + 1e-06) * gain
        out_ref[blk] = (linear + win_ref[blk]).astype(BF16)


def unpack_kernel(x_ref, out_ref):
    out_ref[...] = x_ref[...].reshape(HEADS * VDIM, BLK).T


SMEM = pl.BlockSpec(memory_space=pltpu.SMEM)
VMEM = pl.BlockSpec(memory_space=pltpu.VMEM)


def call(kernel, outs, scalars, arrays, aliases=None):
    arrays = [pltpu.with_memory_space_constraint(array, pltpu.VMEM) for array in arrays]
    single = len(outs) == 1
    return pl.pallas_call(
        kernel,
        out_shape=outs[0] if single else tuple(outs),
        in_specs=[SMEM] * len(scalars) + [VMEM] * len(arrays),
        out_specs=VMEM if single else tuple(VMEM for _ in outs),
        input_output_aliases=aliases or {},
        compiler_params=pltpu.CompilerParams(vmem_limit_bytes=8 * 1024 * 1024),
    )(*scalars, *arrays)


def scalar(value):
    return jnp.asarray(value).astype(jnp.int32).reshape(1)


def on_device(query_rows, key_rows, value_rows, conv_weight, norm_gain):
    group = ("pair", "core", "inner")
    stack = ("quad", "half")
    members = lax.axis_size(group)
    groups = lax.axis_size(stack)

    def upward(value):
        return lax.ppermute(value, stack, [(i, i + 1) for i in range(groups - 1)])

    packed, taps = pl.pallas_call(
        pack_kernel,
        out_shape=(
            pltpu.VMEM((HEADS, PART, BLK), BF16),
            pltpu.VMEM((TAPS + 1, VDIM, LANES), F32),
        ),
        in_specs=[SMEM] + [VMEM] * 5,
        out_specs=(VMEM, VMEM),
    )(
        scalar(lax.axis_index(group)),
        query_rows,
        key_rows,
        value_rows,
        conv_weight,
        norm_gain.reshape(1, HEADS * VDIM),
    )
    mine = lax.all_to_all(packed, group, 0, 0)
    sent, own, conv = call(
        state_kernel,
        [
            pltpu.VMEM((HALO_ROWS + FEAT, BLK), BF16),
            pltpu.VMEM((2, VDIM, LANES), F32),
            pltpu.VMEM((members, VDIM, BLK), BF16),
        ],
        [],
        [mine, taps],
    )
    near = upward(sent)
    block = (VDIM, BLK)
    quad = lax.axis_index("quad")
    first = scalar(lax.axis_index(stack) == 0)
    local_shapes = [
        pltpu.VMEM((members, *block), F32),
        pltpu.VMEM((members, *block), F32),
        pltpu.VMEM((NPHI, members * BLK), BF16),
    ]
    local_arrays = [mine, conv, near, taps]
    sent, pair, *local = call(
        merge_kernel,
        [
            pltpu.VMEM((STATE_ROWS, LANES), BF16),
            pltpu.VMEM((2, VDIM, LANES), F32),
            *local_shapes,
        ],
        [scalar(quad), first],
        [own, *local_arrays],
    )
    in_place = {5: 0, 6: 1, 7: 2}

    def lower(sent, *local):
        recv = lax.ppermute(sent, "quad", [(0, 1)])
        local = call(
            second_local_kernel, local_shapes, [scalar(quad)], [*local_arrays, *local], in_place
        )
        both, recv = call(
            join_kernel,
            [pltpu.VMEM((STATE_ROWS, LANES), BF16), pltpu.VMEM((STATE_ROWS, LANES), BF16)],
            [scalar(quad)],
            [pair, recv, taps],
        )
        return both, recv, *local

    def upper(sent, *local):
        return sent, sent, *local

    both, pair_recv, *local = lax.cond(quad < 2, lower, upper, sent, *local)
    low = lax.ppermute(both, "quad", [(1, 3)])
    below = lax.ppermute(both, "quad", [(1, 2), (2, 3)])
    num, win, phi = call(
        upper_local_kernel,
        local_shapes,
        [scalar(quad)],
        [*local_arrays, *local],
        in_place,
    )
    done = call(
        final_kernel,
        [pltpu.VMEM((members, *block), BF16)],
        [scalar(quad)],
        [pair_recv, below, low, near, taps, num, win, phi],
    )
    heads = lax.all_to_all(done, group, 0, 0)
    out = jax.ShapeDtypeStruct((BLK, HEADS * VDIM), BF16)
    return call(unpack_kernel, [out], [], [heads])


def solution(mesh):
    outer, inner = mesh.shape["outer"], mesh.shape["inner"]
    pair = HEADS // inner // 2
    shape = (mesh.shape["dp"], outer // (2 * 2 * pair), 2, pair, 2, inner)
    split = Mesh(
        np.asarray(mesh.devices).reshape(shape), ("dp", "quad", "half", "pair", "core", "inner")
    )
    rows = P(("dp", "quad", "half", "pair", "core", "inner"), None)
    return jax.shard_map(
        on_device,
        mesh=split,
        in_specs=(rows, rows, rows, P(), P()),
        out_specs=rows,
        check_vma=False,
    )
```

```python
import jax
import jax.numpy as jnp
import numpy as np
from jax import lax
from jax.experimental import pallas as pl
from jax.experimental.pallas import tpu as pltpu
from jax.sharding import Mesh, PartitionSpec as P

HEADS = 16
FEAT = 16
VDIM = 64
TAPS = 3
WIN = 64
BLK = 128
NPHI = 160
LANES = 128
EDGE = NPHI - LANES
HALF = VDIM // 2
STATE_ROWS = VDIM + HALF
HALO_ROWS = STATE_ROWS + HALF
PART = FEAT + FEAT + VDIM
F32 = jnp.float32
BF16 = jnp.bfloat16


def nt(lhs, rhs):
    return lax.dot_general(lhs, rhs, (((1,), (1,)), ((), ())), preferred_element_type=F32)


def tn(lhs, rhs):
    return lax.dot_general(lhs, rhs, (((0,), (0,)), ((), ())), preferred_element_type=F32)


def nn(lhs, rhs):
    return lax.dot_general(lhs, rhs, (((1,), (0,)), ((), ())), preferred_element_type=F32)


def lanes(rows):
    return lax.broadcasted_iota(jnp.int32, (rows, LANES), 1)


def features(entries, weighted):
    lin, diag, off = (0.25, 1.0 / 32.0, 1.0 / 16.0) if weighted else (1.0, 1.0, 1.0)
    rows = [entries * lin if weighted else entries]
    base = entries * off if weighted else entries
    rows.append(entries * entries * diag if weighted else entries * entries)
    for step in range(1, FEAT // 2):
        rolled = jnp.concatenate([entries[step:], entries[:step]], axis=0)
        rows.append(base * rolled)
    rows.append(base[: FEAT // 2] * entries[FEAT // 2 :])
    tail = lax.broadcasted_iota(jnp.int32, (8, entries.shape[1]), 0)
    rows.append(jnp.where(tail == 0, 1.0, 0.0).astype(F32))
    return jnp.concatenate(rows, axis=0).astype(BF16)


def convolve(taps, raw, before):
    lane = lanes(VDIM)
    one = jnp.where(lane < 1, pltpu.roll(before, 1, 1), pltpu.roll(raw, 1, 1))
    two = jnp.where(lane < 2, pltpu.roll(before, 2, 1), pltpu.roll(raw, 2, 1))
    return (taps[0] * raw + taps[1] * one + taps[2] * two).astype(BF16)


def fold(main, rest):
    both = rest[:HALF] + pltpu.roll(rest[HALF:], LANES // 2, 1)
    return jnp.concatenate([main, both], axis=0).astype(BF16)


def unfold(packed):
    wide = packed.astype(F32)
    both = wide[VDIM:STATE_ROWS]
    low = lanes(HALF) < LANES // 2
    upper = jnp.where(low, both, 0.0)
    lower = jnp.where(low, pltpu.roll(both, LANES // 2, 1), 0.0)
    return wide[:VDIM], jnp.concatenate([upper, lower], axis=0)


def edge_state(taps_ref, edges):
    lane = lanes(VDIM)
    values = jnp.zeros((VDIM, LANES), F32)
    keys = jnp.zeros((FEAT, LANES), F32)
    for index, (key_rest, tail_rest) in enumerate(edges):
        at = 2 * index
        same = pltpu.roll(tail_rest, (LANES - EDGE + at) % LANES, 1)
        last = pltpu.roll(tail_rest, (LANES - EDGE - 1 + at) % LANES, 1)
        missing = jnp.where(lane == at, taps_ref[1] * last + taps_ref[2] * same, 0.0)
        missing = jnp.where(lane == at + 1, taps_ref[2] * same, missing)
        values = values + missing
        moved = pltpu.roll(key_rest[:FEAT], (LANES - EDGE - 2 + at) % LANES, 1)
        place = lanes(FEAT)
        keys = keys + jnp.where((place >= at) & (place < at + 2), moved, 0.0)
    state = nt(values.astype(BF16), features(keys, True))
    blank = jnp.zeros((VDIM, LANES - EDGE), F32)
    return state[:, :LANES], jnp.concatenate([state[:, LANES:], blank], axis=1)


def joined(rest, tail_rest, key_rest):
    lane = lanes(VDIM)
    return jnp.where(lane < EDGE, rest, jnp.where(lane < EDGE + 2, tail_rest, key_rest))


def pack_kernel(head_ref, q_ref, k_ref, v_ref, w_ref, gain_ref, out_ref, taps_ref):
    out_ref[:, 0:FEAT, :] = q_ref[...].T.reshape(HEADS, FEAT, BLK)
    out_ref[:, FEAT : 2 * FEAT, :] = k_ref[...].T.reshape(HEADS, FEAT, BLK)
    out_ref[:, 2 * FEAT :, :] = v_ref[...].T.reshape(HEADS, VDIM, BLK)
    head = head_ref[0]
    start = pl.multiple_of(head // 2 * LANES, LANES)
    odd = head % 2 == 1
    for index in range(TAPS + 1):
        source, at = (w_ref, index) if index < TAPS else (gain_ref, 0)
        row = source[at : at + 1, pl.ds(start, LANES)]
        both = jnp.broadcast_to(row, (LANES, LANES)).T
        taps_ref[index] = jnp.where(odd, both[VDIM:], both[:VDIM])


def state_kernel(x_ref, taps_ref, sent_ref, own_ref, conv_ref):
    count = x_ref.shape[0]
    taps = [taps_ref[index] for index in range(TAPS)]
    total = jnp.zeros((VDIM, NPHI), F32)
    before = jnp.zeros((VDIM, BLK), F32)
    for blk in range(count):
        raw = x_ref[blk, 2 * FEAT :, :].astype(F32)
        conv = convolve(taps, raw, before)
        conv_ref[blk] = conv
        phi = features(x_ref[blk, FEAT : 2 * FEAT, :].astype(F32), True)
        total = total + nt(conv, phi)
        before = raw
    lane = lanes(VDIM)
    blank = jnp.zeros((VDIM, LANES - EDGE), F32)
    rest = jnp.concatenate([total[:, LANES:], blank], axis=1)
    tail = pltpu.roll(before, EDGE + 2, 1)
    first = x_ref[0, FEAT : 2 * FEAT, :].astype(F32)
    first = jnp.concatenate([first, jnp.zeros((VDIM - FEAT, BLK), F32)], axis=0)
    first = jnp.where(lane < EDGE + 4, pltpu.roll(first, EDGE + 2, 1), 0.0)
    rest = joined(rest, tail, first)
    main = total[:, :LANES]
    own_ref[0] = main
    own_ref[1] = rest
    sent_ref[0:STATE_ROWS, :] = fold(main, rest)
    wide = conv.astype(F32)
    upper = pltpu.roll(wide[:HALF], WIN, 1)
    sent_ref[STATE_ROWS:HALO_ROWS, :] = jnp.where(lanes(HALF) < WIN, upper, wide[HALF:]).astype(BF16)
    sent_ref[HALO_ROWS:, :] = x_ref[count - 1, FEAT : 2 * FEAT, :]


def inside_window(first):
    row = lax.broadcasted_iota(jnp.int32, (WIN + BLK, BLK), 0)
    lane = lax.broadcasted_iota(jnp.int32, (WIN + BLK, BLK), 1)
    inside = (row >= lane) & (row <= lane + WIN)
    return inside if first is None else inside & ((row >= WIN) | (first == 0))


def block_parts(query, key, value, before_key, before_value, inside):
    scores = tn(jnp.concatenate([before_key, key], axis=1), query) * 0.25
    own = scores[BLK:]
    key_row = lax.broadcasted_iota(jnp.int32, (BLK, BLK), 0)
    query_lane = lax.broadcasted_iota(jnp.int32, (BLK, BLK), 1)
    weights = 1.0 + own + 0.5 * own * own
    weights = jnp.where(key_row <= query_lane, weights, 0.0).astype(BF16)
    masked = jnp.where(inside, scores[BLK - WIN :], -1e30)
    row_max = jnp.max(masked, axis=0, keepdims=True)
    exp_scores = jnp.exp(masked - row_max)
    row_sum = jnp.sum(exp_scores, axis=0, keepdims=True)
    blank = jnp.zeros((BLK - WIN, BLK), BF16)
    probs = jnp.concatenate([blank, exp_scores.astype(BF16)], axis=0)
    window = nn(jnp.concatenate([before_value, value], axis=1), probs)
    return nn(value, weights), window / row_sum


def local_blocks(first_ref, x_ref, conv_ref, near_ref, taps_ref, num_ref, win_ref, phi_ref):
    count = x_ref.shape[0]
    inside = inside_window(None)
    state = jnp.zeros((VDIM, NPHI), F32)
    taps = [taps_ref[index] for index in range(TAPS)]
    before_raw = pltpu.roll(unfold(near_ref[0:STATE_ROWS, :])[1], LANES - EDGE - 2, 1)
    halves = near_ref[STATE_ROWS:HALO_ROWS, :].astype(F32)
    before_value = jnp.concatenate([pltpu.roll(halves, WIN, 1), halves], axis=0).astype(BF16)
    before_key = near_ref[HALO_ROWS:, :]
    for blk in range(count):
        query = x_ref[blk, 0:FEAT, :]
        key = x_ref[blk, FEAT : 2 * FEAT, :]
        if blk == 0:
            value = convolve(taps, x_ref[0, 2 * FEAT :, :].astype(F32), before_raw)
        else:
            value = conv_ref[blk]
        phi_query = features(query.astype(F32), False)
        phi_ref[:, blk * BLK : (blk + 1) * BLK] = phi_query
        mask = inside if blk > 0 or first_ref is None else inside_window(first_ref[0])
        own, win = block_parts(query, key, value, before_key, before_value, mask)
        num_ref[blk] = own + nn(state.astype(BF16), phi_query) if blk > 0 else own
        win_ref[blk] = win
        if blk + 1 < count:
            state = state + nt(value, features(key.astype(F32), True))
        before_key, before_value = key, value


def upper_local_kernel(quad_ref, x_ref, conv_ref, near_ref, taps_ref, *refs):
    @pl.when(quad_ref[0] > 1)
    def _():
        local_blocks(None, x_ref, conv_ref, near_ref, taps_ref, *refs[3:])


def paired(own_ref, near_ref, taps_ref):
    main, rest = own_ref[0], own_ref[1]
    near_main, near_rest = unfold(near_ref[0:STATE_ROWS, :])
    edge_main, edge_rest = edge_state(taps_ref, [(rest, near_rest)])
    main = main + near_main + edge_main
    return main, joined(rest + near_rest + edge_rest, rest, near_rest)


def lowest_kernel(
    quad_ref,
    first_ref,
    own_ref,
    x_ref,
    conv_ref,
    near_ref,
    taps_ref,
    sent_ref,
    num_ref,
    win_ref,
    phi_ref,
):
    @pl.when(quad_ref[0] == 0)
    def _():
        sent_ref[...] = fold(*paired(own_ref, near_ref, taps_ref))
        local_blocks(first_ref, x_ref, conv_ref, near_ref, taps_ref, num_ref, win_ref, phi_ref)


def second_kernel(
    quad_ref,
    own_ref,
    x_ref,
    conv_ref,
    near_ref,
    taps_ref,
    num_in_ref,
    win_in_ref,
    phi_in_ref,
    sent_ref,
    pair_ref,
    num_ref,
    win_ref,
    phi_ref,
):
    @pl.when(quad_ref[0] == 1)
    def _():
        main, rest = paired(own_ref, near_ref, taps_ref)
        pair_ref[0] = main
        pair_ref[1] = rest
        sent_ref[...] = fold(main, rest)
        local_blocks(None, x_ref, conv_ref, near_ref, taps_ref, num_ref, win_ref, phi_ref)


def join_kernel(quad_ref, pair_ref, recv_ref, taps_ref, sent_ref):
    @pl.when(quad_ref[0] == 1)
    def _():
        main, rest = pair_ref[0], pair_ref[1]
        recv_main, recv_rest = unfold(recv_ref[...])
        edge_main, edge_rest = edge_state(taps_ref, [(rest, recv_rest)])
        sent_ref[...] = fold(
            main + recv_main + edge_main, joined(rest + recv_rest + edge_rest, rest, recv_rest)
        )


def upper_kernel(
    quad_ref, own_ref, low_ref, second_ref, upper_ref, taps_ref, both_ref, sent_ref, near_ref
):
    @pl.when(quad_ref[0] == 0)
    def _():
        near_ref[...] = low_ref[...]

    @pl.when(quad_ref[0] == 1)
    def _():
        near_ref[...] = second_ref[...]
        sent_ref[...] = both_ref[...]

    @pl.when(quad_ref[0] > 1)
    def _():
        near_ref[...] = upper_ref[...]
        sent_ref[...] = fold(*paired(own_ref, upper_ref, taps_ref))


def final_kernel(
    zero_to_one_ref,
    below_ref,
    one_to_three_ref,
    zero_to_three_ref,
    near_ref,
    taps_ref,
    num_ref,
    win_ref,
    phi_ref,
    out_ref,
):
    near_main, near_rest = unfold(near_ref[0:STATE_ROWS, :])
    below = [unfold(ref[...]) for ref in (zero_to_one_ref, below_ref)]
    below_main = below[0][0] + below[1][0]
    below_rest = below[0][1] + below[1][1]
    one_main, one_rest = unfold(one_to_three_ref[...])
    zero_main, zero_rest = unfold(zero_to_three_ref[...])
    edge_main, edge_rest = edge_state(
        taps_ref, [(near_rest, below_rest), (below_rest, one_rest), (one_rest, zero_rest)]
    )
    main = near_main + below_main + one_main + zero_main + edge_main
    rest = near_rest + below_rest + one_rest + zero_rest + edge_rest
    state = jnp.concatenate([main, rest[:, :EDGE]], axis=1).astype(BF16)
    gain = taps_ref[TAPS]
    for blk in range(num_ref.shape[0]):
        phi = phi_ref[:, blk * BLK : (blk + 1) * BLK]
        num = num_ref[blk] + nn(state, phi)
        mean_square = jnp.sum(num * num, axis=0, keepdims=True) * (1.0 / VDIM)
        linear = num * lax.rsqrt(mean_square + 1e-06) * gain
        out_ref[blk] = (linear + win_ref[blk]).astype(BF16)


def unpack_kernel(x_ref, out_ref):
    out_ref[...] = x_ref[...].reshape(HEADS * VDIM, BLK).T


SMEM = pl.BlockSpec(memory_space=pltpu.SMEM)
VMEM = pl.BlockSpec(memory_space=pltpu.VMEM)


def call(kernel, outs, scalars, arrays, aliases=None):
    arrays = [pltpu.with_memory_space_constraint(array, pltpu.VMEM) for array in arrays]
    single = len(outs) == 1
    return pl.pallas_call(
        kernel,
        out_shape=outs[0] if single else tuple(outs),
        in_specs=[SMEM] * len(scalars) + [VMEM] * len(arrays),
        out_specs=VMEM if single else tuple(VMEM for _ in outs),
        input_output_aliases=aliases or {},
        compiler_params=pltpu.CompilerParams(vmem_limit_bytes=8 * 1024 * 1024),
    )(*scalars, *arrays)


def scalar(value):
    return jnp.asarray(value).astype(jnp.int32).reshape(1)


def on_device(query_rows, key_rows, value_rows, conv_weight, norm_gain):
    group = ("pair", "core", "inner")
    stack = ("quad", "half")
    members = lax.axis_size(group)
    groups = lax.axis_size(stack)

    packed, taps = pl.pallas_call(
        pack_kernel,
        out_shape=(
            pltpu.VMEM((HEADS, PART, BLK), BF16),
            pltpu.VMEM((TAPS + 1, VDIM, LANES), F32),
        ),
        in_specs=[SMEM] + [VMEM] * 5,
        out_specs=(VMEM, VMEM),
    )(
        scalar(lax.axis_index(group)),
        query_rows,
        key_rows,
        value_rows,
        conv_weight,
        norm_gain.reshape(1, HEADS * VDIM),
    )
    mine = lax.all_to_all(packed, group, 0, 0)
    sent, own, conv = call(
        state_kernel,
        [
            pltpu.VMEM((HALO_ROWS + FEAT, BLK), BF16),
            pltpu.VMEM((2, VDIM, LANES), F32),
            pltpu.VMEM((members, VDIM, BLK), BF16),
        ],
        [],
        [mine, taps],
    )
    block = (VDIM, BLK)
    quad = scalar(lax.axis_index("quad"))
    first = scalar(lax.axis_index(stack) == 0)
    packed_state = pltpu.VMEM((STATE_ROWS, LANES), BF16)
    local_shapes = [
        pltpu.VMEM((members, *block), F32),
        pltpu.VMEM((members, *block), F32),
        pltpu.VMEM((NPHI, members * BLK), BF16),
    ]
    low_near = lax.ppermute(sent, stack, [(0, 1)])
    second_near = lax.ppermute(sent, stack, [(1, 2), (2, 3)])
    upper_near = lax.ppermute(sent, stack, [(i, i + 1) for i in range(3, groups - 1)])
    lowest, *local = call(
        lowest_kernel,
        [packed_state, *local_shapes],
        [quad, first],
        [own, mine, conv, low_near, taps],
    )
    zero_to_one = lax.ppermute(lowest, "quad", [(0, 1)])
    second, pair, *local = call(
        second_kernel,
        [packed_state, pltpu.VMEM((2, VDIM, LANES), F32), *local_shapes],
        [quad],
        [own, mine, conv, second_near, taps, *local],
        {6: 2, 7: 3, 8: 4},
    )
    one_to_three = lax.ppermute(second, "quad", [(1, 3)])
    zero_to_three = lax.ppermute(lowest, "quad", [(0, 3)])
    both = call(join_kernel, [packed_state], [quad], [pair, zero_to_one, taps])
    upper, near = call(
        upper_kernel,
        [packed_state, pltpu.VMEM((HALO_ROWS + FEAT, BLK), BF16)],
        [quad],
        [own, low_near, second_near, upper_near, taps, both],
    )
    below = lax.ppermute(upper, "quad", [(1, 2), (2, 3)])
    num, win, phi = call(
        upper_local_kernel,
        local_shapes,
        [quad],
        [mine, conv, near, taps, *local],
        {5: 0, 6: 1, 7: 2},
    )
    done = call(
        final_kernel,
        [pltpu.VMEM((members, *block), BF16)],
        [],
        [
            zero_to_one,
            below,
            one_to_three,
            zero_to_three,
            near,
            taps,
            num,
            win,
            phi,
        ],
    )
    heads = lax.all_to_all(done, group, 0, 0)
    out = jax.ShapeDtypeStruct((BLK, HEADS * VDIM), BF16)
    return call(unpack_kernel, [out], [], [heads])


def solution(mesh):
    outer, inner = mesh.shape["outer"], mesh.shape["inner"]
    pair = HEADS // inner // 2
    shape = (mesh.shape["dp"], outer // (2 * 2 * pair), 2, pair, 2, inner)
    split = Mesh(
        np.asarray(mesh.devices).reshape(shape), ("dp", "quad", "half", "pair", "core", "inner")
    )
    rows = P(("dp", "quad", "half", "pair", "core", "inner"), None)
    return jax.shard_map(
        on_device,
        mesh=split,
        in_specs=(rows, rows, rows, P(), P()),
        out_specs=rows,
        check_vma=False,
    )
```

```python
import jax
import jax.numpy as jnp
import numpy as np
from jax import lax
from jax.experimental import pallas as pl
from jax.experimental.pallas import tpu as pltpu
from jax.sharding import Mesh, PartitionSpec as P

HEADS = 16
FEAT = 16
VDIM = 64
TAPS = 3
WIN = 64
BLK = 128
NPHI = 160
LANES = 128
EDGE = NPHI - LANES
HALF = VDIM // 2
STATE_ROWS = VDIM + HALF
HALO_ROWS = STATE_ROWS + HALF
PART = FEAT + FEAT + VDIM
F32 = jnp.float32
BF16 = jnp.bfloat16


def nt(lhs, rhs):
    return lax.dot_general(lhs, rhs, (((1,), (1,)), ((), ())), preferred_element_type=F32)


def tn(lhs, rhs):
    return lax.dot_general(lhs, rhs, (((0,), (0,)), ((), ())), preferred_element_type=F32)


def nn(lhs, rhs):
    return lax.dot_general(lhs, rhs, (((1,), (0,)), ((), ())), preferred_element_type=F32)


def lanes(rows):
    return lax.broadcasted_iota(jnp.int32, (rows, LANES), 1)


def features(entries, weighted):
    lin, diag, off = (0.25, 1.0 / 32.0, 1.0 / 16.0) if weighted else (1.0, 1.0, 1.0)
    rows = [entries * lin if weighted else entries]
    base = entries * off if weighted else entries
    rows.append(entries * entries * diag if weighted else entries * entries)
    for step in range(1, FEAT // 2):
        rolled = jnp.concatenate([entries[step:], entries[:step]], axis=0)
        rows.append(base * rolled)
    rows.append(base[: FEAT // 2] * entries[FEAT // 2 :])
    tail = lax.broadcasted_iota(jnp.int32, (8, entries.shape[1]), 0)
    rows.append(jnp.where(tail == 0, 1.0, 0.0).astype(F32))
    return jnp.concatenate(rows, axis=0).astype(BF16)


def convolve(taps, raw, before):
    lane = lanes(VDIM)
    one = jnp.where(lane < 1, pltpu.roll(before, 1, 1), pltpu.roll(raw, 1, 1))
    two = jnp.where(lane < 2, pltpu.roll(before, 2, 1), pltpu.roll(raw, 2, 1))
    return (taps[0] * raw + taps[1] * one + taps[2] * two).astype(BF16)


def fold(main, rest):
    both = rest[:HALF] + pltpu.roll(rest[HALF:], LANES // 2, 1)
    return jnp.concatenate([main, both], axis=0).astype(BF16)


def unfold(packed):
    wide = packed.astype(F32)
    both = wide[VDIM:STATE_ROWS]
    low = lanes(HALF) < LANES // 2
    upper = jnp.where(low, both, 0.0)
    lower = jnp.where(low, pltpu.roll(both, LANES // 2, 1), 0.0)
    return wide[:VDIM], jnp.concatenate([upper, lower], axis=0)


def edge_state(taps_ref, edges):
    lane = lanes(VDIM)
    values = jnp.zeros((VDIM, LANES), F32)
    keys = jnp.zeros((FEAT, LANES), F32)
    for index, (key_rest, tail_rest) in enumerate(edges):
        at = 2 * index
        same = pltpu.roll(tail_rest, (LANES - EDGE + at) % LANES, 1)
        last = pltpu.roll(tail_rest, (LANES - EDGE - 1 + at) % LANES, 1)
        missing = jnp.where(lane == at, taps_ref[1] * last + taps_ref[2] * same, 0.0)
        missing = jnp.where(lane == at + 1, taps_ref[2] * same, missing)
        values = values + missing
        moved = pltpu.roll(key_rest[:FEAT], (LANES - EDGE - 2 + at) % LANES, 1)
        place = lanes(FEAT)
        keys = keys + jnp.where((place >= at) & (place < at + 2), moved, 0.0)
    state = nt(values.astype(BF16), features(keys, True))
    blank = jnp.zeros((VDIM, LANES - EDGE), F32)
    return state[:, :LANES], jnp.concatenate([state[:, LANES:], blank], axis=1)


def joined(rest, tail_rest, key_rest):
    lane = lanes(VDIM)
    return jnp.where(lane < EDGE, rest, jnp.where(lane < EDGE + 2, tail_rest, key_rest))


def pack_kernel(head_ref, q_ref, k_ref, v_ref, w_ref, gain_ref, out_ref, taps_ref):
    out_ref[:, 0:FEAT, :] = q_ref[...].T.reshape(HEADS, FEAT, BLK)
    out_ref[:, FEAT : 2 * FEAT, :] = k_ref[...].T.reshape(HEADS, FEAT, BLK)
    out_ref[:, 2 * FEAT :, :] = v_ref[...].T.reshape(HEADS, VDIM, BLK)
    head = head_ref[0]
    start = pl.multiple_of(head // 2 * LANES, LANES)
    odd = head % 2 == 1
    for index in range(TAPS + 1):
        source, at = (w_ref, index) if index < TAPS else (gain_ref, 0)
        row = source[at : at + 1, pl.ds(start, LANES)]
        both = jnp.broadcast_to(row, (LANES, LANES)).T
        taps_ref[index] = jnp.where(odd, both[VDIM:], both[:VDIM])


def state_kernel(x_ref, taps_ref, sent_ref, own_ref, conv_ref):
    count = x_ref.shape[0]
    taps = [taps_ref[index] for index in range(TAPS)]
    before = jnp.zeros((VDIM, BLK), F32)
    convs, phis = [], []
    for blk in range(count):
        raw = x_ref[blk, 2 * FEAT :, :].astype(F32)
        conv = convolve(taps, raw, before)
        conv_ref[blk] = conv
        convs.append(conv)
        phis.append(features(x_ref[blk, FEAT : 2 * FEAT, :].astype(F32), True))
        before = raw
    total = nt(jnp.concatenate(convs, axis=1), jnp.concatenate(phis, axis=1))
    lane = lanes(VDIM)
    blank = jnp.zeros((VDIM, LANES - EDGE), F32)
    rest = jnp.concatenate([total[:, LANES:], blank], axis=1)
    tail = pltpu.roll(before, EDGE + 2, 1)
    first = x_ref[0, FEAT : 2 * FEAT, :].astype(F32)
    first = jnp.concatenate([first, jnp.zeros((VDIM - FEAT, BLK), F32)], axis=0)
    first = jnp.where(lane < EDGE + 4, pltpu.roll(first, EDGE + 2, 1), 0.0)
    rest = joined(rest, tail, first)
    main = total[:, :LANES]
    own_ref[0] = main
    own_ref[1] = rest
    sent_ref[0:STATE_ROWS, :] = fold(main, rest)
    wide = conv.astype(F32)
    upper = pltpu.roll(wide[:HALF], WIN, 1)
    sent_ref[STATE_ROWS:HALO_ROWS, :] = jnp.where(lanes(HALF) < WIN, upper, wide[HALF:]).astype(BF16)
    sent_ref[HALO_ROWS:, :] = x_ref[count - 1, FEAT : 2 * FEAT, :]


def inside_window(first):
    row = lax.broadcasted_iota(jnp.int32, (WIN + BLK, BLK), 0)
    lane = lax.broadcasted_iota(jnp.int32, (WIN + BLK, BLK), 1)
    inside = (row >= lane) & (row <= lane + WIN)
    return inside if first is None else inside & ((row >= WIN) | (first == 0))


def block_parts(query, key, value, before_key, before_value, inside):
    scores = tn(jnp.concatenate([before_key, key], axis=1), query) * 0.25
    own = scores[BLK:]
    key_row = lax.broadcasted_iota(jnp.int32, (BLK, BLK), 0)
    query_lane = lax.broadcasted_iota(jnp.int32, (BLK, BLK), 1)
    weights = 1.0 + own + 0.5 * own * own
    weights = jnp.where(key_row <= query_lane, weights, 0.0).astype(BF16)
    masked = jnp.where(inside, scores[BLK - WIN :], -1e30)
    row_max = jnp.max(masked, axis=0, keepdims=True)
    exp_scores = jnp.exp(masked - row_max)
    row_sum = jnp.sum(exp_scores, axis=0, keepdims=True)
    blank = jnp.zeros((BLK - WIN, BLK), BF16)
    probs = jnp.concatenate([blank, exp_scores.astype(BF16)], axis=0)
    window = nn(jnp.concatenate([before_value, value], axis=1), probs)
    return nn(value, weights), window / row_sum


def local_blocks(first_ref, x_ref, conv_ref, near_ref, taps_ref, num_ref, win_ref, phi_ref):
    count = x_ref.shape[0]
    inside = inside_window(None)
    state = jnp.zeros((VDIM, NPHI), F32)
    taps = [taps_ref[index] for index in range(TAPS)]
    before_raw = pltpu.roll(unfold(near_ref[0:STATE_ROWS, :])[1], LANES - EDGE - 2, 1)
    halves = near_ref[STATE_ROWS:HALO_ROWS, :].astype(F32)
    before_value = jnp.concatenate([pltpu.roll(halves, WIN, 1), halves], axis=0).astype(BF16)
    before_key = near_ref[HALO_ROWS:, :]
    for blk in range(count):
        query = x_ref[blk, 0:FEAT, :]
        key = x_ref[blk, FEAT : 2 * FEAT, :]
        if blk == 0:
            value = convolve(taps, x_ref[0, 2 * FEAT :, :].astype(F32), before_raw)
        else:
            value = conv_ref[blk]
        phi_query = features(query.astype(F32), False)
        phi_ref[:, blk * BLK : (blk + 1) * BLK] = phi_query
        mask = inside if blk > 0 or first_ref is None else inside_window(first_ref[0])
        own, win = block_parts(query, key, value, before_key, before_value, mask)
        num_ref[blk] = own + nn(state.astype(BF16), phi_query) if blk > 0 else own
        win_ref[blk] = win
        if blk + 1 < count:
            state = state + nt(value, features(key.astype(F32), True))
        before_key, before_value = key, value


def upper_local_kernel(quad_ref, x_ref, conv_ref, near_ref, taps_ref, *refs):
    @pl.when(quad_ref[0] > 1)
    def _():
        local_blocks(None, x_ref, conv_ref, near_ref, taps_ref, *refs[3:])


def paired(own_ref, near_ref, taps_ref):
    main, rest = own_ref[0], own_ref[1]
    near_main, near_rest = unfold(near_ref[0:STATE_ROWS, :])
    edge_main, edge_rest = edge_state(taps_ref, [(rest, near_rest)])
    main = main + near_main + edge_main
    return main, joined(rest + near_rest + edge_rest, rest, near_rest)


def lowest_kernel(
    quad_ref,
    first_ref,
    own_ref,
    x_ref,
    conv_ref,
    near_ref,
    taps_ref,
    sent_ref,
    num_ref,
    win_ref,
    phi_ref,
):
    @pl.when(quad_ref[0] == 0)
    def _():
        sent_ref[...] = fold(*paired(own_ref, near_ref, taps_ref))
        local_blocks(first_ref, x_ref, conv_ref, near_ref, taps_ref, num_ref, win_ref, phi_ref)


def second_kernel(
    quad_ref,
    own_ref,
    x_ref,
    conv_ref,
    near_ref,
    taps_ref,
    num_in_ref,
    win_in_ref,
    phi_in_ref,
    sent_ref,
    pair_ref,
    num_ref,
    win_ref,
    phi_ref,
):
    @pl.when(quad_ref[0] == 1)
    def _():
        main, rest = paired(own_ref, near_ref, taps_ref)
        pair_ref[0] = main
        pair_ref[1] = rest
        sent_ref[...] = fold(main, rest)
        local_blocks(None, x_ref, conv_ref, near_ref, taps_ref, num_ref, win_ref, phi_ref)


def join_kernel(quad_ref, pair_ref, recv_ref, taps_ref, sent_ref):
    @pl.when(quad_ref[0] == 1)
    def _():
        main, rest = pair_ref[0], pair_ref[1]
        recv_main, recv_rest = unfold(recv_ref[...])
        edge_main, edge_rest = edge_state(taps_ref, [(rest, recv_rest)])
        sent_ref[...] = fold(
            main + recv_main + edge_main, joined(rest + recv_rest + edge_rest, rest, recv_rest)
        )


def upper_kernel(
    quad_ref, own_ref, low_ref, second_ref, upper_ref, taps_ref, both_ref, sent_ref, near_ref
):
    @pl.when(quad_ref[0] == 0)
    def _():
        near_ref[...] = low_ref[...]

    @pl.when(quad_ref[0] == 1)
    def _():
        near_ref[...] = second_ref[...]
        sent_ref[...] = both_ref[...]

    @pl.when(quad_ref[0] > 1)
    def _():
        near_ref[...] = upper_ref[...]
        sent_ref[...] = fold(*paired(own_ref, upper_ref, taps_ref))


def final_kernel(
    zero_to_one_ref,
    below_ref,
    one_to_three_ref,
    zero_to_three_ref,
    near_ref,
    taps_ref,
    num_ref,
    win_ref,
    phi_ref,
    out_ref,
):
    near_main, near_rest = unfold(near_ref[0:STATE_ROWS, :])
    below = [unfold(ref[...]) for ref in (zero_to_one_ref, below_ref)]
    below_main = below[0][0] + below[1][0]
    below_rest = below[0][1] + below[1][1]
    one_main, one_rest = unfold(one_to_three_ref[...])
    zero_main, zero_rest = unfold(zero_to_three_ref[...])
    edge_main, edge_rest = edge_state(
        taps_ref, [(near_rest, below_rest), (below_rest, one_rest), (one_rest, zero_rest)]
    )
    main = near_main + below_main + one_main + zero_main + edge_main
    rest = near_rest + below_rest + one_rest + zero_rest + edge_rest
    state = jnp.concatenate([main, rest[:, :EDGE]], axis=1).astype(BF16)
    gain = taps_ref[TAPS]
    earlier = nn(state, phi_ref[...])
    for blk in range(num_ref.shape[0]):
        num = num_ref[blk] + earlier[:, blk * BLK : (blk + 1) * BLK]
        mean_square = jnp.sum(num * num, axis=0, keepdims=True) * (1.0 / VDIM)
        linear = num * lax.rsqrt(mean_square + 1e-06) * gain
        out_ref[blk] = (linear + win_ref[blk]).astype(BF16)


def unpack_kernel(x_ref, out_ref):
    out_ref[...] = x_ref[...].reshape(HEADS * VDIM, BLK).T


SMEM = pl.BlockSpec(memory_space=pltpu.SMEM)
VMEM = pl.BlockSpec(memory_space=pltpu.VMEM)


def call(kernel, outs, scalars, arrays, aliases=None):
    arrays = [pltpu.with_memory_space_constraint(array, pltpu.VMEM) for array in arrays]
    single = len(outs) == 1
    return pl.pallas_call(
        kernel,
        out_shape=outs[0] if single else tuple(outs),
        in_specs=[SMEM] * len(scalars) + [VMEM] * len(arrays),
        out_specs=VMEM if single else tuple(VMEM for _ in outs),
        input_output_aliases=aliases or {},
        compiler_params=pltpu.CompilerParams(vmem_limit_bytes=8 * 1024 * 1024),
    )(*scalars, *arrays)


def scalar(value):
    return jnp.asarray(value).astype(jnp.int32).reshape(1)


def on_device(query_rows, key_rows, value_rows, conv_weight, norm_gain):
    group = ("pair", "core", "inner")
    stack = ("quad", "half")
    members = lax.axis_size(group)
    groups = lax.axis_size(stack)

    packed, taps = pl.pallas_call(
        pack_kernel,
        out_shape=(
            pltpu.VMEM((HEADS, PART, BLK), BF16),
            pltpu.VMEM((TAPS + 1, VDIM, LANES), F32),
        ),
        in_specs=[SMEM] + [VMEM] * 5,
        out_specs=(VMEM, VMEM),
    )(
        scalar(lax.axis_index(group)),
        query_rows,
        key_rows,
        value_rows,
        conv_weight,
        norm_gain.reshape(1, HEADS * VDIM),
    )
    mine = lax.all_to_all(packed, group, 0, 0)
    sent, own, conv = call(
        state_kernel,
        [
            pltpu.VMEM((HALO_ROWS + FEAT, BLK), BF16),
            pltpu.VMEM((2, VDIM, LANES), F32),
            pltpu.VMEM((members, VDIM, BLK), BF16),
        ],
        [],
        [mine, taps],
    )
    block = (VDIM, BLK)
    quad = scalar(lax.axis_index("quad"))
    first = scalar(lax.axis_index(stack) == 0)
    packed_state = pltpu.VMEM((STATE_ROWS, LANES), BF16)
    local_shapes = [
        pltpu.VMEM((members, *block), F32),
        pltpu.VMEM((members, *block), F32),
        pltpu.VMEM((NPHI, members * BLK), BF16),
    ]
    low_near = lax.ppermute(sent, stack, [(0, 1)])
    second_near = lax.ppermute(sent, stack, [(1, 2), (2, 3)])
    upper_near = lax.ppermute(sent, stack, [(i, i + 1) for i in range(3, groups - 1)])
    lowest, *local = call(
        lowest_kernel,
        [packed_state, *local_shapes],
        [quad, first],
        [own, mine, conv, low_near, taps],
    )
    zero_to_one = lax.ppermute(lowest, "quad", [(0, 1)])
    second, pair, *local = call(
        second_kernel,
        [packed_state, pltpu.VMEM((2, VDIM, LANES), F32), *local_shapes],
        [quad],
        [own, mine, conv, second_near, taps, *local],
        {6: 2, 7: 3, 8: 4},
    )
    one_to_three = lax.ppermute(second, "quad", [(1, 3)])
    zero_to_three = lax.ppermute(lowest, "quad", [(0, 3)])
    both = call(join_kernel, [packed_state], [quad], [pair, zero_to_one, taps])
    upper, near = call(
        upper_kernel,
        [packed_state, pltpu.VMEM((HALO_ROWS + FEAT, BLK), BF16)],
        [quad],
        [own, low_near, second_near, upper_near, taps, both],
    )
    below = lax.ppermute(upper, "quad", [(1, 2), (2, 3)])
    num, win, phi = call(
        upper_local_kernel,
        local_shapes,
        [quad],
        [mine, conv, near, taps, *local],
        {5: 0, 6: 1, 7: 2},
    )
    done = call(
        final_kernel,
        [pltpu.VMEM((members, *block), BF16)],
        [],
        [
            zero_to_one,
            below,
            one_to_three,
            zero_to_three,
            near,
            taps,
            num,
            win,
            phi,
        ],
    )
    heads = lax.all_to_all(done, group, 0, 0)
    out = jax.ShapeDtypeStruct((BLK, HEADS * VDIM), BF16)
    return call(unpack_kernel, [out], [], [heads])


def solution(mesh):
    outer, inner = mesh.shape["outer"], mesh.shape["inner"]
    pair = HEADS // inner // 2
    shape = (mesh.shape["dp"], outer // (2 * 2 * pair), 2, pair, 2, inner)
    split = Mesh(
        np.asarray(mesh.devices).reshape(shape), ("dp", "quad", "half", "pair", "core", "inner")
    )
    rows = P(("dp", "quad", "half", "pair", "core", "inner"), None)
    return jax.shard_map(
        on_device,
        mesh=split,
        in_specs=(rows, rows, rows, P(), P()),
        out_specs=rows,
        check_vma=False,
    )
```

```python
import jax
import jax.numpy as jnp
import numpy as np
from jax import lax
from jax.experimental import pallas as pl
from jax.experimental.pallas import tpu as pltpu
from jax.sharding import Mesh, PartitionSpec as P

HEADS = 16
FEAT = 16
VDIM = 64
TAPS = 3
WIN = 64
BLK = 128
NPHI = 160
LANES = 128
EDGE = NPHI - LANES
HALF = VDIM // 2
STATE_ROWS = VDIM + HALF
HALO_ROWS = STATE_ROWS + HALF
PART = FEAT + FEAT + VDIM
F32 = jnp.float32
BF16 = jnp.bfloat16


def nt(lhs, rhs):
    return lax.dot_general(lhs, rhs, (((1,), (1,)), ((), ())), preferred_element_type=F32)


def tn(lhs, rhs):
    return lax.dot_general(lhs, rhs, (((0,), (0,)), ((), ())), preferred_element_type=F32)


def nn(lhs, rhs):
    return lax.dot_general(lhs, rhs, (((1,), (0,)), ((), ())), preferred_element_type=F32)


def lanes(rows):
    return lax.broadcasted_iota(jnp.int32, (rows, LANES), 1)


def features(entries, weighted):
    lin, diag, off = (0.25, 1.0 / 32.0, 1.0 / 16.0) if weighted else (1.0, 1.0, 1.0)
    rows = [entries * lin if weighted else entries]
    base = entries * off if weighted else entries
    rows.append(entries * entries * diag if weighted else entries * entries)
    for step in range(1, FEAT // 2):
        rolled = jnp.concatenate([entries[step:], entries[:step]], axis=0)
        rows.append(base * rolled)
    rows.append(base[: FEAT // 2] * entries[FEAT // 2 :])
    tail = lax.broadcasted_iota(jnp.int32, (8, entries.shape[1]), 0)
    rows.append(jnp.where(tail == 0, 1.0, 0.0).astype(F32))
    return jnp.concatenate(rows, axis=0).astype(BF16)


def convolve(taps, raw, before):
    lane = lanes(VDIM)
    one = jnp.where(lane < 1, pltpu.roll(before, 1, 1), pltpu.roll(raw, 1, 1))
    two = jnp.where(lane < 2, pltpu.roll(before, 2, 1), pltpu.roll(raw, 2, 1))
    return (taps[0] * raw + taps[1] * one + taps[2] * two).astype(BF16)


def fold(main, rest):
    both = rest[:HALF] + pltpu.roll(rest[HALF:], LANES // 2, 1)
    return jnp.concatenate([main, both], axis=0).astype(BF16)


def unfold(packed):
    wide = packed.astype(F32)
    both = wide[VDIM:STATE_ROWS]
    low = lanes(HALF) < LANES // 2
    upper = jnp.where(low, both, 0.0)
    lower = jnp.where(low, pltpu.roll(both, LANES // 2, 1), 0.0)
    return wide[:VDIM], jnp.concatenate([upper, lower], axis=0)


def edge_state(taps_ref, edges):
    lane = lanes(VDIM)
    values = jnp.zeros((VDIM, LANES), F32)
    keys = jnp.zeros((FEAT, LANES), F32)
    for index, (key_rest, tail_rest) in enumerate(edges):
        at = 2 * index
        same = pltpu.roll(tail_rest, (LANES - EDGE + at) % LANES, 1)
        last = pltpu.roll(tail_rest, (LANES - EDGE - 1 + at) % LANES, 1)
        missing = jnp.where(lane == at, taps_ref[1] * last + taps_ref[2] * same, 0.0)
        missing = jnp.where(lane == at + 1, taps_ref[2] * same, missing)
        values = values + missing
        moved = pltpu.roll(key_rest[:FEAT], (LANES - EDGE - 2 + at) % LANES, 1)
        place = lanes(FEAT)
        keys = keys + jnp.where((place >= at) & (place < at + 2), moved, 0.0)
    state = nt(values.astype(BF16), features(keys, True))
    blank = jnp.zeros((VDIM, LANES - EDGE), F32)
    return state[:, :LANES], jnp.concatenate([state[:, LANES:], blank], axis=1)


def joined(rest, tail_rest, key_rest):
    lane = lanes(VDIM)
    return jnp.where(lane < EDGE, rest, jnp.where(lane < EDGE + 2, tail_rest, key_rest))


def pack_kernel(head_ref, q_ref, k_ref, v_ref, w_ref, gain_ref, out_ref, taps_ref):
    out_ref[:, 0:FEAT, :] = q_ref[...].T.reshape(HEADS, FEAT, BLK)
    out_ref[:, FEAT : 2 * FEAT, :] = k_ref[...].T.reshape(HEADS, FEAT, BLK)
    out_ref[:, 2 * FEAT :, :] = v_ref[...].T.reshape(HEADS, VDIM, BLK)
    head = head_ref[0]
    start = pl.multiple_of(head // 2 * LANES, LANES)
    odd = head % 2 == 1
    for index in range(TAPS + 1):
        source, at = (w_ref, index) if index < TAPS else (gain_ref, 0)
        row = source[at : at + 1, pl.ds(start, LANES)]
        both = jnp.broadcast_to(row, (LANES, LANES)).T
        taps_ref[index] = jnp.where(odd, both[VDIM:], both[:VDIM])


def state_kernel(x_ref, taps_ref, sent_ref, again_ref, own_ref, conv_ref):
    count = x_ref.shape[0]
    taps = [taps_ref[index] for index in range(TAPS)]
    before = jnp.zeros((VDIM, BLK), F32)
    convs, phis = [], []
    for blk in range(count):
        raw = x_ref[blk, 2 * FEAT :, :].astype(F32)
        conv = convolve(taps, raw, before)
        conv_ref[blk] = conv
        convs.append(conv)
        phis.append(features(x_ref[blk, FEAT : 2 * FEAT, :].astype(F32), True))
        before = raw
    total = nt(jnp.concatenate(convs, axis=1), jnp.concatenate(phis, axis=1))
    lane = lanes(VDIM)
    blank = jnp.zeros((VDIM, LANES - EDGE), F32)
    rest = jnp.concatenate([total[:, LANES:], blank], axis=1)
    tail = pltpu.roll(before, EDGE + 2, 1)
    first = x_ref[0, FEAT : 2 * FEAT, :].astype(F32)
    first = jnp.concatenate([first, jnp.zeros((VDIM - FEAT, BLK), F32)], axis=0)
    first = jnp.where(lane < EDGE + 4, pltpu.roll(first, EDGE + 2, 1), 0.0)
    rest = joined(rest, tail, first)
    main = total[:, :LANES]
    own_ref[0] = main
    own_ref[1] = rest
    sent_ref[0:STATE_ROWS, :] = fold(main, rest)
    wide = conv.astype(F32)
    upper = pltpu.roll(wide[:HALF], WIN, 1)
    sent_ref[STATE_ROWS:HALO_ROWS, :] = jnp.where(lanes(HALF) < WIN, upper, wide[HALF:]).astype(BF16)
    sent_ref[HALO_ROWS:, :] = x_ref[count - 1, FEAT : 2 * FEAT, :]
    again_ref[...] = sent_ref[...]


def inside_window(first):
    row = lax.broadcasted_iota(jnp.int32, (WIN + BLK, BLK), 0)
    lane = lax.broadcasted_iota(jnp.int32, (WIN + BLK, BLK), 1)
    inside = (row >= lane) & (row <= lane + WIN)
    return inside if first is None else inside & ((row >= WIN) | (first == 0))


def block_parts(query, key, value, before_key, before_value, inside):
    scores = tn(jnp.concatenate([before_key, key], axis=1), query) * 0.25
    own = scores[BLK:]
    key_row = lax.broadcasted_iota(jnp.int32, (BLK, BLK), 0)
    query_lane = lax.broadcasted_iota(jnp.int32, (BLK, BLK), 1)
    weights = 1.0 + own + 0.5 * own * own
    weights = jnp.where(key_row <= query_lane, weights, 0.0).astype(BF16)
    masked = jnp.where(inside, scores[BLK - WIN :], -1e30)
    row_max = jnp.max(masked, axis=0, keepdims=True)
    exp_scores = jnp.exp(masked - row_max)
    row_sum = jnp.sum(exp_scores, axis=0, keepdims=True)
    blank = jnp.zeros((BLK - WIN, BLK), BF16)
    probs = jnp.concatenate([blank, exp_scores.astype(BF16)], axis=0)
    window = nn(jnp.concatenate([before_value, value], axis=1), probs)
    return nn(value, weights), window / row_sum


def local_blocks(first_ref, x_ref, conv_ref, near_ref, taps_ref, num_ref, win_ref, phi_ref):
    count = x_ref.shape[0]
    inside = inside_window(None)
    state = jnp.zeros((VDIM, NPHI), F32)
    taps = [taps_ref[index] for index in range(TAPS)]
    before_raw = pltpu.roll(unfold(near_ref[0:STATE_ROWS, :])[1], LANES - EDGE - 2, 1)
    halves = near_ref[STATE_ROWS:HALO_ROWS, :].astype(F32)
    before_value = jnp.concatenate([pltpu.roll(halves, WIN, 1), halves], axis=0).astype(BF16)
    before_key = near_ref[HALO_ROWS:, :]
    for blk in range(count):
        query = x_ref[blk, 0:FEAT, :]
        key = x_ref[blk, FEAT : 2 * FEAT, :]
        if blk == 0:
            value = convolve(taps, x_ref[0, 2 * FEAT :, :].astype(F32), before_raw)
        else:
            value = conv_ref[blk]
        phi_query = features(query.astype(F32), False)
        phi_ref[:, blk * BLK : (blk + 1) * BLK] = phi_query
        mask = inside if blk > 0 or first_ref is None else inside_window(first_ref[0])
        own, win = block_parts(query, key, value, before_key, before_value, mask)
        num_ref[blk] = own + nn(state.astype(BF16), phi_query) if blk > 0 else own
        win_ref[blk] = win
        if blk + 1 < count:
            state = state + nt(value, features(key.astype(F32), True))
        before_key, before_value = key, value


def upper_local_kernel(quad_ref, x_ref, conv_ref, near_ref, taps_ref, *refs):
    @pl.when(quad_ref[0] > 1)
    def _():
        local_blocks(None, x_ref, conv_ref, near_ref, taps_ref, *refs[3:])


def paired(own_ref, near_ref, taps_ref):
    main, rest = own_ref[0], own_ref[1]
    near_main, near_rest = unfold(near_ref[0:STATE_ROWS, :])
    edge_main, edge_rest = edge_state(taps_ref, [(rest, near_rest)])
    main = main + near_main + edge_main
    return main, joined(rest + near_rest + edge_rest, rest, near_rest)


def lowest_kernel(
    quad_ref,
    first_ref,
    own_ref,
    x_ref,
    conv_ref,
    near_ref,
    taps_ref,
    sent_ref,
    num_ref,
    win_ref,
    phi_ref,
):
    @pl.when(quad_ref[0] == 0)
    def _():
        sent_ref[0:STATE_ROWS] = fold(*paired(own_ref, near_ref, taps_ref))
        local_blocks(first_ref, x_ref, conv_ref, near_ref, taps_ref, num_ref, win_ref, phi_ref)


def hand_on_kernel(value_ref, after_ref, out_ref):
    pass


def second_kernel(
    quad_ref,
    own_ref,
    x_ref,
    conv_ref,
    near_ref,
    taps_ref,
    num_in_ref,
    win_in_ref,
    phi_in_ref,
    sent_ref,
    pair_ref,
    num_ref,
    win_ref,
    phi_ref,
):
    @pl.when(quad_ref[0] == 1)
    def _():
        main, rest = paired(own_ref, near_ref, taps_ref)
        pair_ref[0] = main
        pair_ref[1] = rest
        sent_ref[...] = fold(main, rest)
        local_blocks(None, x_ref, conv_ref, near_ref, taps_ref, num_ref, win_ref, phi_ref)


def join_kernel(quad_ref, pair_ref, recv_ref, taps_ref, sent_ref):
    @pl.when(quad_ref[0] == 1)
    def _():
        main, rest = pair_ref[0], pair_ref[1]
        recv_main, recv_rest = unfold(recv_ref[0:STATE_ROWS])
        edge_main, edge_rest = edge_state(taps_ref, [(rest, recv_rest)])
        sent_ref[...] = fold(
            main + recv_main + edge_main, joined(rest + recv_rest + edge_rest, rest, recv_rest)
        )


def upper_kernel(
    quad_ref, own_ref, low_ref, second_ref, upper_ref, taps_ref, both_ref, sent_ref, near_ref
):
    @pl.when(quad_ref[0] == 0)
    def _():
        near_ref[...] = low_ref[...]

    @pl.when(quad_ref[0] == 1)
    def _():
        near_ref[...] = second_ref[...]
        sent_ref[...] = both_ref[...]

    @pl.when(quad_ref[0] > 1)
    def _():
        near_ref[...] = upper_ref[...]
        sent_ref[...] = fold(*paired(own_ref, upper_ref, taps_ref))


def final_kernel(
    zero_to_one_ref,
    below_ref,
    one_to_three_ref,
    zero_to_three_ref,
    near_ref,
    taps_ref,
    num_ref,
    win_ref,
    phi_ref,
    out_ref,
):
    near_main, near_rest = unfold(near_ref[0:STATE_ROWS, :])
    below = [unfold(ref[0:STATE_ROWS]) for ref in (zero_to_one_ref, below_ref)]
    below_main = below[0][0] + below[1][0]
    below_rest = below[0][1] + below[1][1]
    one_main, one_rest = unfold(one_to_three_ref[...])
    zero_main, zero_rest = unfold(zero_to_three_ref[0:STATE_ROWS])
    edge_main, edge_rest = edge_state(
        taps_ref, [(near_rest, below_rest), (below_rest, one_rest), (one_rest, zero_rest)]
    )
    main = near_main + below_main + one_main + zero_main + edge_main
    rest = near_rest + below_rest + one_rest + zero_rest + edge_rest
    state = jnp.concatenate([main, rest[:, :EDGE]], axis=1).astype(BF16)
    gain = taps_ref[TAPS]
    earlier = nn(state, phi_ref[...])
    for blk in range(num_ref.shape[0]):
        num = num_ref[blk] + earlier[:, blk * BLK : (blk + 1) * BLK]
        mean_square = jnp.sum(num * num, axis=0, keepdims=True) * (1.0 / VDIM)
        linear = num * lax.rsqrt(mean_square + 1e-06) * gain
        out_ref[blk] = (linear + win_ref[blk]).astype(BF16)


def unpack_kernel(x_ref, out_ref):
    out_ref[...] = x_ref[...].reshape(HEADS * VDIM, BLK).T


SMEM = pl.BlockSpec(memory_space=pltpu.SMEM)
VMEM = pl.BlockSpec(memory_space=pltpu.VMEM)


def call(kernel, outs, scalars, arrays, aliases=None):
    arrays = [pltpu.with_memory_space_constraint(array, pltpu.VMEM) for array in arrays]
    single = len(outs) == 1
    return pl.pallas_call(
        kernel,
        out_shape=outs[0] if single else tuple(outs),
        in_specs=[SMEM] * len(scalars) + [VMEM] * len(arrays),
        out_specs=VMEM if single else tuple(VMEM for _ in outs),
        input_output_aliases=aliases or {},
        compiler_params=pltpu.CompilerParams(vmem_limit_bytes=8 * 1024 * 1024),
    )(*scalars, *arrays)


def scalar(value):
    return jnp.asarray(value).astype(jnp.int32).reshape(1)


def on_device(query_rows, key_rows, value_rows, conv_weight, norm_gain):
    group = ("pair", "core", "inner")
    stack = ("quad", "half")
    members = lax.axis_size(group)
    groups = lax.axis_size(stack)

    packed, taps = pl.pallas_call(
        pack_kernel,
        out_shape=(
            pltpu.VMEM((HEADS, PART, BLK), BF16),
            pltpu.VMEM((TAPS + 1, VDIM, LANES), F32),
        ),
        in_specs=[SMEM] + [VMEM] * 5,
        out_specs=(VMEM, VMEM),
    )(
        scalar(lax.axis_index(group)),
        query_rows,
        key_rows,
        value_rows,
        conv_weight,
        norm_gain.reshape(1, HEADS * VDIM),
    )
    mine = lax.all_to_all(packed, group, 0, 0)
    sent, again, own, conv = call(
        state_kernel,
        [
            pltpu.VMEM((HALO_ROWS + FEAT, BLK), BF16),
            pltpu.VMEM((HALO_ROWS + FEAT, BLK), BF16),
            pltpu.VMEM((2, VDIM, LANES), F32),
            pltpu.VMEM((members, VDIM, BLK), BF16),
        ],
        [],
        [mine, taps],
    )
    block = (VDIM, BLK)
    quad = scalar(lax.axis_index("quad"))
    first = scalar(lax.axis_index(stack) == 0)
    packed_state = pltpu.VMEM((STATE_ROWS, LANES), BF16)
    local_shapes = [
        pltpu.VMEM((members, *block), F32),
        pltpu.VMEM((members, *block), F32),
        pltpu.VMEM((NPHI, members * BLK), BF16),
    ]
    low_near = lax.ppermute(sent, stack, [(0, 1)])
    second_near = lax.ppermute(sent, stack, [(1, 2), (2, 3)])
    lowest, *local = call(
        lowest_kernel,
        [pltpu.VMEM((144, BLK), BF16), *local_shapes],
        [quad, first],
        [own, mine, conv, low_near, taps],
    )
    zero_to_one = lax.ppermute(lowest, "quad", [(0, 1)])
    again = call(
        hand_on_kernel, [pltpu.VMEM((HALO_ROWS + FEAT, BLK), BF16)], [], [again, lowest], {0: 0}
    )
    upper_near = lax.ppermute(again, stack, [(i, i + 1) for i in range(3, groups - 1)])
    second, pair, *local = call(
        second_kernel,
        [packed_state, pltpu.VMEM((2, VDIM, LANES), F32), *local_shapes],
        [quad],
        [own, mine, conv, second_near, taps, *local],
        {6: 2, 7: 3, 8: 4},
    )
    one_to_three = lax.ppermute(second, "quad", [(1, 3)])
    zero_to_three = lax.ppermute(lowest, "quad", [(0, 3)])
    both = call(join_kernel, [packed_state], [quad], [pair, zero_to_one, taps])
    upper, near = call(
        upper_kernel,
        [packed_state, pltpu.VMEM((HALO_ROWS + FEAT, BLK), BF16)],
        [quad],
        [own, low_near, second_near, upper_near, taps, both],
    )
    below = lax.ppermute(upper, "quad", [(1, 2), (2, 3)])
    num, win, phi = call(
        upper_local_kernel,
        local_shapes,
        [quad],
        [mine, conv, near, taps, *local],
        {5: 0, 6: 1, 7: 2},
    )
    done = call(
        final_kernel,
        [pltpu.VMEM((members, *block), BF16)],
        [],
        [
            zero_to_one,
            below,
            one_to_three,
            zero_to_three,
            near,
            taps,
            num,
            win,
            phi,
        ],
    )
    heads = lax.all_to_all(done, group, 0, 0)
    out = jax.ShapeDtypeStruct((BLK, HEADS * VDIM), BF16)
    return call(unpack_kernel, [out], [], [heads])


def solution(mesh):
    outer, inner = mesh.shape["outer"], mesh.shape["inner"]
    pair = HEADS // inner // 2
    shape = (mesh.shape["dp"], outer // (2 * 2 * pair), 2, pair, 2, inner)
    split = Mesh(
        np.asarray(mesh.devices).reshape(shape), ("dp", "quad", "half", "pair", "core", "inner")
    )
    rows = P(("dp", "quad", "half", "pair", "core", "inner"), None)
    return jax.shard_map(
        on_device,
        mesh=split,
        in_specs=(rows, rows, rows, P(), P()),
        out_specs=rows,
        check_vma=False,
    )
```

```python
import jax
import jax.numpy as jnp
import numpy as np
from jax import lax
from jax.experimental import pallas as pl
from jax.experimental.pallas import tpu as pltpu
from jax.sharding import Mesh, PartitionSpec as P

HEADS = 16
FEAT = 16
VDIM = 64
TAPS = 3
WIN = 64
BLK = 128
NPHI = 160
LANES = 128
EDGE = NPHI - LANES
HALF = VDIM // 2
STATE_ROWS = VDIM + HALF
HALO_ROWS = STATE_ROWS + HALF
PART = FEAT + FEAT + VDIM
F32 = jnp.float32
BF16 = jnp.bfloat16


def nt(lhs, rhs):
    return lax.dot_general(lhs, rhs, (((1,), (1,)), ((), ())), preferred_element_type=F32)


def tn(lhs, rhs):
    return lax.dot_general(lhs, rhs, (((0,), (0,)), ((), ())), preferred_element_type=F32)


def nn(lhs, rhs):
    return lax.dot_general(lhs, rhs, (((1,), (0,)), ((), ())), preferred_element_type=F32)


def lanes(rows):
    return lax.broadcasted_iota(jnp.int32, (rows, LANES), 1)


def features(entries, weighted):
    lin, diag, off = (0.25, 1.0 / 32.0, 1.0 / 16.0) if weighted else (1.0, 1.0, 1.0)
    rows = [entries * lin if weighted else entries]
    base = entries * off if weighted else entries
    rows.append(entries * entries * diag if weighted else entries * entries)
    for step in range(1, FEAT // 2):
        rolled = jnp.concatenate([entries[step:], entries[:step]], axis=0)
        rows.append(base * rolled)
    rows.append(base[: FEAT // 2] * entries[FEAT // 2 :])
    tail = lax.broadcasted_iota(jnp.int32, (8, entries.shape[1]), 0)
    rows.append(jnp.where(tail == 0, 1.0, 0.0).astype(F32))
    return jnp.concatenate(rows, axis=0).astype(BF16)


def convolve(taps, raw, before):
    lane = lanes(VDIM)
    one = jnp.where(lane < 1, pltpu.roll(before, 1, 1), pltpu.roll(raw, 1, 1))
    two = jnp.where(lane < 2, pltpu.roll(before, 2, 1), pltpu.roll(raw, 2, 1))
    return (taps[0] * raw + taps[1] * one + taps[2] * two).astype(BF16)


def fold(main, rest):
    both = rest[:HALF] + pltpu.roll(rest[HALF:], LANES // 2, 1)
    return jnp.concatenate([main, both], axis=0).astype(BF16)


def unfold(packed):
    wide = packed.astype(F32)
    both = wide[VDIM:STATE_ROWS]
    low = lanes(HALF) < LANES // 2
    upper = jnp.where(low, both, 0.0)
    lower = jnp.where(low, pltpu.roll(both, LANES // 2, 1), 0.0)
    return wide[:VDIM], jnp.concatenate([upper, lower], axis=0)


def edge_state(taps_ref, edges):
    lane = lanes(VDIM)
    values = jnp.zeros((VDIM, LANES), F32)
    keys = jnp.zeros((FEAT, LANES), F32)
    for index, (key_rest, tail_rest) in enumerate(edges):
        at = 2 * index
        same = pltpu.roll(tail_rest, (LANES - EDGE + at) % LANES, 1)
        last = pltpu.roll(tail_rest, (LANES - EDGE - 1 + at) % LANES, 1)
        missing = jnp.where(lane == at, taps_ref[1] * last + taps_ref[2] * same, 0.0)
        missing = jnp.where(lane == at + 1, taps_ref[2] * same, missing)
        values = values + missing
        moved = pltpu.roll(key_rest[:FEAT], (LANES - EDGE - 2 + at) % LANES, 1)
        place = lanes(FEAT)
        keys = keys + jnp.where((place >= at) & (place < at + 2), moved, 0.0)
    state = nt(values.astype(BF16), features(keys, True))
    blank = jnp.zeros((VDIM, LANES - EDGE), F32)
    return state[:, :LANES], jnp.concatenate([state[:, LANES:], blank], axis=1)


def joined(rest, tail_rest, key_rest):
    lane = lanes(VDIM)
    return jnp.where(lane < EDGE, rest, jnp.where(lane < EDGE + 2, tail_rest, key_rest))


def pack_kernel(head_ref, q_ref, k_ref, v_ref, w_ref, gain_ref, out_ref, taps_ref):
    out_ref[:, 0:FEAT, :] = q_ref[...].T.reshape(HEADS, FEAT, BLK)
    out_ref[:, FEAT : 2 * FEAT, :] = k_ref[...].T.reshape(HEADS, FEAT, BLK)
    out_ref[:, 2 * FEAT :, :] = v_ref[...].T.reshape(HEADS, VDIM, BLK)
    head = head_ref[0]
    start = pl.multiple_of(head // 2 * LANES, LANES)
    odd = head % 2 == 1
    for index in range(TAPS + 1):
        source, at = (w_ref, index) if index < TAPS else (gain_ref, 0)
        row = source[at : at + 1, pl.ds(start, LANES)]
        both = jnp.broadcast_to(row, (LANES, LANES)).T
        taps_ref[index] = jnp.where(odd, both[VDIM:], both[:VDIM])


def state_kernel(x_ref, taps_ref, sent_ref, own_ref, conv_ref):
    count = x_ref.shape[0]
    taps = [taps_ref[index] for index in range(TAPS)]
    before = jnp.zeros((VDIM, BLK), F32)
    convs, phis = [], []
    for blk in range(count):
        raw = x_ref[blk, 2 * FEAT :, :].astype(F32)
        conv = convolve(taps, raw, before)
        conv_ref[blk] = conv
        convs.append(conv)
        phis.append(features(x_ref[blk, FEAT : 2 * FEAT, :].astype(F32), True))
        before = raw
    total = nt(jnp.concatenate(convs, axis=1), jnp.concatenate(phis, axis=1))
    lane = lanes(VDIM)
    blank = jnp.zeros((VDIM, LANES - EDGE), F32)
    rest = jnp.concatenate([total[:, LANES:], blank], axis=1)
    tail = pltpu.roll(before, EDGE + 2, 1)
    first = x_ref[0, FEAT : 2 * FEAT, :].astype(F32)
    first = jnp.concatenate([first, jnp.zeros((VDIM - FEAT, BLK), F32)], axis=0)
    first = jnp.where(lane < EDGE + 4, pltpu.roll(first, EDGE + 2, 1), 0.0)
    rest = joined(rest, tail, first)
    main = total[:, :LANES]
    own_ref[0] = main
    own_ref[1] = rest
    sent_ref[0:STATE_ROWS, :] = fold(main, rest)
    wide = conv.astype(F32)
    upper = pltpu.roll(wide[:HALF], WIN, 1)
    sent_ref[STATE_ROWS:HALO_ROWS, :] = jnp.where(lanes(HALF) < WIN, upper, wide[HALF:]).astype(BF16)
    sent_ref[HALO_ROWS:, :] = x_ref[count - 1, FEAT : 2 * FEAT, :]


def inside_window(first):
    row = lax.broadcasted_iota(jnp.int32, (WIN + BLK, BLK), 0)
    lane = lax.broadcasted_iota(jnp.int32, (WIN + BLK, BLK), 1)
    inside = (row >= lane) & (row <= lane + WIN)
    return inside if first is None else inside & ((row >= WIN) | (first == 0))


def block_parts(query, key, value, before_key, before_value, inside):
    scores = tn(jnp.concatenate([before_key, key], axis=1), query) * 0.25
    own = scores[BLK:]
    key_row = lax.broadcasted_iota(jnp.int32, (BLK, BLK), 0)
    query_lane = lax.broadcasted_iota(jnp.int32, (BLK, BLK), 1)
    weights = 1.0 + own + 0.5 * own * own
    weights = jnp.where(key_row <= query_lane, weights, 0.0).astype(BF16)
    masked = jnp.where(inside, scores[BLK - WIN :], -1e30)
    row_max = jnp.max(masked, axis=0, keepdims=True)
    exp_scores = jnp.exp(masked - row_max)
    row_sum = jnp.sum(exp_scores, axis=0, keepdims=True)
    blank = jnp.zeros((BLK - WIN, BLK), BF16)
    probs = jnp.concatenate([blank, exp_scores.astype(BF16)], axis=0)
    window = nn(jnp.concatenate([before_value, value], axis=1), probs)
    return nn(value, weights), window / row_sum


def local_blocks(first_ref, x_ref, conv_ref, near_ref, taps_ref, num_ref, win_ref, phi_ref):
    count = x_ref.shape[0]
    inside = inside_window(None)
    state = jnp.zeros((VDIM, NPHI), F32)
    taps = [taps_ref[index] for index in range(TAPS)]
    before_raw = pltpu.roll(unfold(near_ref[0:STATE_ROWS, :])[1], LANES - EDGE - 2, 1)
    halves = near_ref[STATE_ROWS:HALO_ROWS, :].astype(F32)
    before_value = jnp.concatenate([pltpu.roll(halves, WIN, 1), halves], axis=0).astype(BF16)
    before_key = near_ref[HALO_ROWS:, :]
    for blk in range(count):
        query = x_ref[blk, 0:FEAT, :]
        key = x_ref[blk, FEAT : 2 * FEAT, :]
        if blk == 0:
            value = convolve(taps, x_ref[0, 2 * FEAT :, :].astype(F32), before_raw)
        else:
            value = conv_ref[blk]
        phi_query = features(query.astype(F32), False)
        phi_ref[:, blk * BLK : (blk + 1) * BLK] = phi_query
        mask = inside if blk > 0 or first_ref is None else inside_window(first_ref[0])
        own, win = block_parts(query, key, value, before_key, before_value, mask)
        num_ref[blk] = own + nn(state.astype(BF16), phi_query) if blk > 0 else own
        win_ref[blk] = win
        if blk + 1 < count:
            state = state + nt(value, features(key.astype(F32), True))
        before_key, before_value = key, value


def upper_local_kernel(quad_ref, x_ref, conv_ref, near_ref, taps_ref, *refs):
    @pl.when(quad_ref[0] > 1)
    def _():
        local_blocks(None, x_ref, conv_ref, near_ref, taps_ref, *refs[3:])


def paired(own_ref, near_ref, taps_ref):
    main, rest = own_ref[0], own_ref[1]
    near_main, near_rest = unfold(near_ref[0:STATE_ROWS, :])
    edge_main, edge_rest = edge_state(taps_ref, [(rest, near_rest)])
    main = main + near_main + edge_main
    return main, joined(rest + near_rest + edge_rest, rest, near_rest)


def lowest_kernel(
    quad_ref,
    first_ref,
    own_ref,
    x_ref,
    conv_ref,
    near_ref,
    taps_ref,
    sent_ref,
    three_ref,
    num_ref,
    win_ref,
    phi_ref,
):
    @pl.when(quad_ref[0] == 0)
    def _():
        sent_ref[...] = fold(*paired(own_ref, near_ref, taps_ref))
        three_ref[...] = sent_ref[...]
        local_blocks(first_ref, x_ref, conv_ref, near_ref, taps_ref, num_ref, win_ref, phi_ref)


def second_kernel(
    quad_ref,
    own_ref,
    x_ref,
    conv_ref,
    near_ref,
    taps_ref,
    num_in_ref,
    win_in_ref,
    phi_in_ref,
    three_in_ref,
    sent_ref,
    pair_ref,
    num_ref,
    win_ref,
    phi_ref,
    three_ref,
):
    @pl.when(quad_ref[0] == 1)
    def _():
        main, rest = paired(own_ref, near_ref, taps_ref)
        pair_ref[0] = main
        pair_ref[1] = rest
        sent_ref[...] = fold(main, rest)
        local_blocks(None, x_ref, conv_ref, near_ref, taps_ref, num_ref, win_ref, phi_ref)


def join_kernel(quad_ref, pair_ref, recv_ref, taps_ref, sent_ref):
    @pl.when(quad_ref[0] == 1)
    def _():
        main, rest = pair_ref[0], pair_ref[1]
        recv_main, recv_rest = unfold(recv_ref[...])
        edge_main, edge_rest = edge_state(taps_ref, [(rest, recv_rest)])
        sent_ref[...] = fold(
            main + recv_main + edge_main, joined(rest + recv_rest + edge_rest, rest, recv_rest)
        )


def upper_kernel(
    quad_ref, own_ref, low_ref, second_ref, upper_ref, taps_ref, both_ref, sent_ref, near_ref
):
    @pl.when(quad_ref[0] == 0)
    def _():
        near_ref[...] = low_ref[...]

    @pl.when(quad_ref[0] == 1)
    def _():
        near_ref[...] = second_ref[...]
        sent_ref[...] = both_ref[...]

    @pl.when(quad_ref[0] > 1)
    def _():
        near_ref[...] = upper_ref[...]
        sent_ref[...] = fold(*paired(own_ref, upper_ref, taps_ref))


def final_kernel(
    zero_to_one_ref,
    below_ref,
    one_to_three_ref,
    zero_to_three_ref,
    near_ref,
    taps_ref,
    num_ref,
    win_ref,
    phi_ref,
    out_ref,
):
    near_main, near_rest = unfold(near_ref[0:STATE_ROWS, :])
    below = [unfold(ref[...]) for ref in (zero_to_one_ref, below_ref)]
    below_main = below[0][0] + below[1][0]
    below_rest = below[0][1] + below[1][1]
    one_main, one_rest = unfold(one_to_three_ref[...])
    zero_main, zero_rest = unfold(zero_to_three_ref[...])
    edge_main, edge_rest = edge_state(
        taps_ref, [(near_rest, below_rest), (below_rest, one_rest), (one_rest, zero_rest)]
    )
    main = near_main + below_main + one_main + zero_main + edge_main
    rest = near_rest + below_rest + one_rest + zero_rest + edge_rest
    state = jnp.concatenate([main, rest[:, :EDGE]], axis=1).astype(BF16)
    gain = taps_ref[TAPS]
    earlier = nn(state, phi_ref[...])
    for blk in range(num_ref.shape[0]):
        num = num_ref[blk] + earlier[:, blk * BLK : (blk + 1) * BLK]
        mean_square = jnp.sum(num * num, axis=0, keepdims=True) * (1.0 / VDIM)
        linear = num * lax.rsqrt(mean_square + 1e-06) * gain
        out_ref[blk] = (linear + win_ref[blk]).astype(BF16)


def unpack_kernel(x_ref, out_ref):
    out_ref[...] = x_ref[...].reshape(HEADS * VDIM, BLK).T


SMEM = pl.BlockSpec(memory_space=pltpu.SMEM)
VMEM = pl.BlockSpec(memory_space=pltpu.VMEM)


def call(kernel, outs, scalars, arrays, aliases=None):
    arrays = [pltpu.with_memory_space_constraint(array, pltpu.VMEM) for array in arrays]
    single = len(outs) == 1
    return pl.pallas_call(
        kernel,
        out_shape=outs[0] if single else tuple(outs),
        in_specs=[SMEM] * len(scalars) + [VMEM] * len(arrays),
        out_specs=VMEM if single else tuple(VMEM for _ in outs),
        input_output_aliases=aliases or {},
        compiler_params=pltpu.CompilerParams(vmem_limit_bytes=8 * 1024 * 1024),
    )(*scalars, *arrays)


def scalar(value):
    return jnp.asarray(value).astype(jnp.int32).reshape(1)


def on_device(query_rows, key_rows, value_rows, conv_weight, norm_gain):
    group = ("pair", "core", "inner")
    stack = ("quad", "half")
    members = lax.axis_size(group)
    groups = lax.axis_size(stack)

    packed, taps = pl.pallas_call(
        pack_kernel,
        out_shape=(
            pltpu.VMEM((HEADS, PART, BLK), BF16),
            pltpu.VMEM((TAPS + 1, VDIM, LANES), F32),
        ),
        in_specs=[SMEM] + [VMEM] * 5,
        out_specs=(VMEM, VMEM),
    )(
        scalar(lax.axis_index(group)),
        query_rows,
        key_rows,
        value_rows,
        conv_weight,
        norm_gain.reshape(1, HEADS * VDIM),
    )
    mine = lax.all_to_all(packed, group, 0, 0)
    sent, own, conv = call(
        state_kernel,
        [
            pltpu.VMEM((HALO_ROWS + FEAT, BLK), BF16),
            pltpu.VMEM((2, VDIM, LANES), F32),
            pltpu.VMEM((members, VDIM, BLK), BF16),
        ],
        [],
        [mine, taps],
    )
    block = (VDIM, BLK)
    quad = scalar(lax.axis_index("quad"))
    first = scalar(lax.axis_index(stack) == 0)
    packed_state = pltpu.VMEM((STATE_ROWS, LANES), BF16)
    local_shapes = [
        pltpu.VMEM((members, *block), F32),
        pltpu.VMEM((members, *block), F32),
        pltpu.VMEM((NPHI, members * BLK), BF16),
    ]
    low_near = lax.ppermute(sent, stack, [(0, 1)])
    second_near = lax.ppermute(sent, stack, [(1, 2), (2, 3)])
    upper_near = lax.ppermute(sent, stack, [(i, i + 1) for i in range(3, groups - 1)])
    lowest, three, *local = call(
        lowest_kernel,
        [packed_state, packed_state, *local_shapes],
        [quad, first],
        [own, mine, conv, low_near, taps],
    )
    zero_to_one = lax.ppermute(lowest, "quad", [(0, 1)])
    second, pair, *local, three = call(
        second_kernel,
        [packed_state, pltpu.VMEM((2, VDIM, LANES), F32), *local_shapes, packed_state],
        [quad],
        [own, mine, conv, second_near, taps, *local, three],
        {6: 2, 7: 3, 8: 4, 9: 5},
    )
    one_to_three = lax.ppermute(second, "quad", [(1, 3)])
    zero_to_three = lax.ppermute(three, "quad", [(0, 3)])
    both = call(join_kernel, [packed_state], [quad], [pair, zero_to_one, taps])
    upper, near = call(
        upper_kernel,
        [packed_state, pltpu.VMEM((HALO_ROWS + FEAT, BLK), BF16)],
        [quad],
        [own, low_near, second_near, upper_near, taps, both],
    )
    below = lax.ppermute(upper, "quad", [(1, 2), (2, 3)])
    num, win, phi = call(
        upper_local_kernel,
        local_shapes,
        [quad],
        [mine, conv, near, taps, *local],
        {5: 0, 6: 1, 7: 2},
    )
    done = call(
        final_kernel,
        [pltpu.VMEM((members, *block), BF16)],
        [],
        [
            zero_to_one,
            below,
            one_to_three,
            zero_to_three,
            near,
            taps,
            num,
            win,
            phi,
        ],
    )
    heads = lax.all_to_all(done, group, 0, 0)
    out = jax.ShapeDtypeStruct((BLK, HEADS * VDIM), BF16)
    return call(unpack_kernel, [out], [], [heads])


def solution(mesh):
    outer, inner = mesh.shape["outer"], mesh.shape["inner"]
    pair = HEADS // inner // 2
    shape = (mesh.shape["dp"], outer // (2 * 2 * pair), 2, pair, 2, inner)
    split = Mesh(
        np.asarray(mesh.devices).reshape(shape), ("dp", "quad", "half", "pair", "core", "inner")
    )
    rows = P(("dp", "quad", "half", "pair", "core", "inner"), None)
    return jax.shard_map(
        on_device,
        mesh=split,
        in_specs=(rows, rows, rows, P(), P()),
        out_specs=rows,
        check_vma=False,
    )
```
